32 devices in a mesh: rep: 8 (over z, y), shard: 4 (over x, core).
Axes of the slice: x: 2, y: 2, z: 4, core: 2. Of those that a mesh axis runs over, the one named last changes fastest.
Arguments:
- tokens: bfloat16 [8, 1024, 2304], P('rep', 'shard'), may hold values from -6 to 6
- cotangent: bfloat16 [8, 1024, 2304], P('rep', 'shard'), may hold values from -6 to 6
- sequence_adapter_index: int32 [8], P('rep'), may hold values from 0 to 7
- image_span_start: int32 [8, 2], P('rep'), may hold values from 0 to 768, as said below
- attention_norm_gain: bfloat16 [2304], replicated, may hold values from 0.099609375 to 1.8984375
- feedforward_norm_gain: bfloat16 [2304], replicated, may hold values from 0.099609375 to 1.8984375
- query_key_value_weight: bfloat16 [3, 2304, 2304], P(None, 'shard'), may hold values from -0.125 to 0.125
- attention_output_weight: bfloat16 [2304, 2304], P('shard'), may hold values from -2 to 2
- gate_up_projection_weight: bfloat16 [2, 2304, 5760], P(None, 'shard'), may hold values from -0.125 to 0.125
- down_projection_weight: bfloat16 [5760, 2304], P('shard'), may hold values from -0.625 to 0.625
- adapter_model_input_maps: bfloat16 [6, 8, 16, 2304], P(None, 'shard'), may hold values from -0.125 to 0.125
- adapter_model_output_maps: bfloat16 [5, 8, 16, 2304], P(None, 'shard'), may hold values from -1.5 to 1.5
- adapter_hidden_input_map: bfloat16 [8, 16, 5760], P('shard'), may hold values from -0.078125 to 0.078125
- adapter_hidden_output_maps: bfloat16 [2, 8, 16, 5760], P(None, 'shard'), may hold values from -1.5 to 1.5
Outputs:
- output: bfloat16 [8, 1024, 2304], P('rep', 'shard')
- input_grad: float32 [8, 1024, 2304], P('rep', 'shard')
- grad_a_model: float32 [6, 8, 16, 2304], P(None, 'shard')
- grad_b_model: float32 [5, 8, 16, 2304], P(None, 'shard')
- grad_a_hidden: float32 [8, 16, 5760], P('shard')
- grad_b_hidden: float32 [2, 8, 16, 5760], P(None, 'shard')
The draws below stay inside these ranges and needn't reach their ends.
Inputs may be any that keep to these rules, and one draw needn't show every extreme that they name: `image_span_start`: in each sequence the first span starts in 0 to 256 and the second in 512 to 768; some sequence's first span starts at 0 and some sequence's second span ends at the sequence's end.
All inputs are finite; a program needn't handle non-finite values.
Results may differ from the reference program's by a relative error of at most 0.023.
Values may be sent and summed in bfloat16 or wider, within the bound.
No kernel may reach another device: no remote copies, remote signals or barrier semaphores. Data moves between devices by JAX's collectives and lax.ppermute only.
A program may use at most 512 MiB of HBM per device.

```python
import math
import jax
import jax.numpy as jnp
from jax import lax

MODEL_WIDTH = 2304
HDIM = 64
FEEDFORWARD_UNITS = 5760
ADAPTER_RANK = 16
ADAPTER_COUNT = 8
SPAN = 256
SEQ_LEN = 1024
SEQS = 8


def draw_image_span_start(key, part):
    middle_point = SEQ_LEN // 2
    first = jax.random.randint(jax.random.fold_in(key, 11), (SEQS,), 0, middle_point - SPAN + 1)
    second = jax.random.randint(jax.random.fold_in(key, 12), (SEQS,), middle_point, SEQ_LEN - SPAN + 1)
    earliest = jax.random.randint(jax.random.fold_in(key, 13), (), 0, SEQS)
    latest = jax.random.randint(jax.random.fold_in(key, 14), (), 0, SEQS)
    first = first.at[earliest].set(0)
    second = second.at[latest].set(SEQ_LEN - SPAN)
    return jnp.stack([first, second], axis=1).astype(jnp.int32)


def with_ends(drawn, stream_key, low, largest):
    spot = [jax.random.randint(jax.random.fold_in(stream_key, axis), (), 0, length) for axis, length in enumerate(drawn.shape)]
    main_axis = drawn.shape.index(max(drawn.shape))
    next_to = spot[:main_axis] + [(spot[main_axis] + 1) % drawn.shape[main_axis]] + spot[main_axis + 1:]
    return drawn.at[tuple(spot)].set(low).at[tuple(next_to)].set(largest)


def steps_of(stream_key, dims, cuts, low, high):
    loudness = 1.0
    for dim, blocks in cuts:
        heights = jax.random.uniform(jax.random.fold_in(jax.random.fold_in(stream_key, 6), dim), (blocks,), jnp.float32, low / len(cuts), high / len(cuts))
        loudness = loudness * jnp.repeat(jnp.exp(heights), dims[dim] // blocks).reshape((-1,) + (1,) * (len(dims) - 1 - dim))
    return loudness


def noise(key, extent, spread, bound, shards=(), kind=jnp.bfloat16):
    values = jax.random.normal(key, extent, jnp.float32) * spread
    if len(shards) > 0:
        values = steps_of(key, extent, shards, -0.22, 0.18) * values
    return jnp.clip(values, min=-bound, max=bound).astype(kind)


def setup_inputs(seed: int = 0) -> dict:
    key_of = jax.random.split(jax.random.key(seed), 15)
    return {
        "tokens": noise(key_of[0], (SEQS, SEQ_LEN, MODEL_WIDTH), 1.0, 6.0, ((0, 8), (1, 4))),
        "cotangent": noise(key_of[1], (SEQS, SEQ_LEN, MODEL_WIDTH), 1.0, 6.0, ((0, 8), (1, 4))),
        "sequence_adapter_index": with_ends(jax.random.randint(key_of[2], (SEQS,), 0, ADAPTER_COUNT), jax.random.fold_in(key_of[2], 1), 0, ADAPTER_COUNT - 1).astype(jnp.int32),
        "image_span_start": draw_image_span_start(jax.random.fold_in(key_of[14], 71), 0),
        "attention_norm_gain": jnp.clip(1.0 + 0.18 * jax.random.normal(key_of[4], (MODEL_WIDTH,), jnp.float32), 0.099609375, 1.8984375).astype(jnp.bfloat16),
        "feedforward_norm_gain": jnp.clip(1.0 + 0.18 * jax.random.normal(key_of[5], (MODEL_WIDTH,), jnp.float32), 0.099609375, 1.8984375).astype(jnp.bfloat16),
        "query_key_value_weight": noise(key_of[6], (3, MODEL_WIDTH, MODEL_WIDTH), MODEL_WIDTH ** -0.5, 0.125, ((1, 4),)),
        "attention_output_weight": noise(key_of[7], (MODEL_WIDTH, MODEL_WIDTH), (max(MODEL_WIDTH // 256, 1)) ** -0.5, 2.0, ((0, 4),)),
        "gate_up_projection_weight": noise(key_of[8], (2, MODEL_WIDTH, FEEDFORWARD_UNITS), MODEL_WIDTH ** -0.5, 0.125, ((1, 4),)),
        "down_projection_weight": noise(key_of[9], (FEEDFORWARD_UNITS, MODEL_WIDTH), (max(FEEDFORWARD_UNITS // 64, 1)) ** -0.5, 0.625, ((0, 4),)),
        "adapter_model_input_maps": noise(key_of[10], (6, ADAPTER_COUNT, ADAPTER_RANK, MODEL_WIDTH), MODEL_WIDTH ** -0.5, 0.125, ((1, 4),)),
        "adapter_model_output_maps": noise(key_of[11], (5, ADAPTER_COUNT, ADAPTER_RANK, MODEL_WIDTH), ADAPTER_RANK ** -0.5, 1.5, ((1, 4),)),
        "adapter_hidden_input_map": noise(key_of[12], (ADAPTER_COUNT, ADAPTER_RANK, FEEDFORWARD_UNITS), FEEDFORWARD_UNITS ** -0.5, 0.078125, ((0, 4),)),
        "adapter_hidden_output_maps": noise(key_of[13], (2, ADAPTER_COUNT, ADAPTER_RANK, FEEDFORWARD_UNITS), ADAPTER_RANK ** -0.5, 1.5, ((1, 4),)),
    }


EPS = 1e-05
THETA = 10000.0
BRANCH = 1.4 / math.sqrt(40.0)
EXACT = lax.Precision.HIGHEST

@jax.custom_vjp
def low(v):
    return lax.optimization_barrier(v.astype(jnp.bfloat16)).astype(jnp.float32)

@jax.custom_vjp
def low_back(v):
    return v

def low_keep(v):
    return (low(v), None)

def low_pass(kept, grad):
    return (grad,)

def back_keep(v):
    return (v, None)

def back_low(kept, grad):
    return (low(grad),)
low.defvjp(low_keep, low_pass)
low_back.defvjp(back_keep, back_low)

def product(left, right):
    return jnp.dot(left, right, precision=EXACT, preferred_element_type=jnp.float32)

def norm_rows(values, gain):
    return values * lax.rsqrt(lax.optimization_barrier(jnp.mean(values * values, axis=-1, keepdims=True)) + EPS) * gain

def rotate(values, positions):
    rows = values.shape[0]
    heads = values.shape[1] // HDIM
    half = HDIM // 2
    exponent = jnp.arange(half, dtype=jnp.float32) * (-2.0 / HDIM)
    frequency = jnp.exp(exponent * math.log(THETA))
    angle = positions.astype(jnp.float32)[:, None] * frequency[None, :]
    cosine = jnp.concatenate([jnp.cos(angle), jnp.cos(angle)], axis=1)[:, None, :]
    sine = jnp.concatenate([jnp.sin(angle), jnp.sin(angle)], axis=1)[:, None, :]
    split = values.reshape(rows, heads, HDIM)
    turned = jnp.concatenate([-split[..., half:], split[..., :half]], axis=-1)
    return (split * cosine + turned * sine).reshape(rows, heads * HDIM)

def span_label(positions, starts):
    label = jnp.full(positions.shape, -1, jnp.int32)
    for number in range(starts.shape[0]):
        inside = (positions >= starts[number]) & (positions < starts[number] + SPAN)
        label = jnp.where(inside, jnp.int32(number), label)
    return label

def visible_pairs(rows, columns, starts):
    row_label = span_label(rows, starts)[:, None]
    column_label = span_label(columns, starts)[None, :]
    causal = columns[None, :] <= rows[:, None]
    return causal | (row_label == column_label) & (row_label >= 0)

def adapted(inputs, weight_matrix, down_map, up_map):
    narrow = low_back(low(product(inputs, down_map.T)))
    return product(inputs, weight_matrix) + product(narrow, up_map)

def attention(queries, keys, values, visible):
    length = queries.shape[0]
    heads = queries.shape[1] // HDIM
    query_heads = queries.reshape(length, heads, HDIM)
    key_heads = keys.reshape(length, heads, HDIM)
    value_heads = values.reshape(length, heads, HDIM)
    raw = jnp.einsum('qhd,khd->hqk', query_heads, key_heads, precision=EXACT)
    scores = jnp.where(visible[None], low_back(raw * (1.0 / math.sqrt(HDIM))), -1e+30)
    top = lax.optimization_barrier(jnp.max(scores, axis=-1, keepdims=True))
    weights = jnp.exp(scores - top)
    probs = weights / lax.optimization_barrier(jnp.sum(weights, axis=-1, keepdims=True))
    mixed = jnp.einsum('hqk,khd->qhd', low(probs), value_heads, precision=EXACT)
    return mixed.reshape(length, heads * HDIM)

def block(tokens, a_model, b_model, a_hidden, b_hidden, frozen, pick, starts):
    attention_norm_gain, feedforward_norm_gain, query_key_value_weight, attention_output_weight, gate_up_projection_weight, down_projection_weight = frozen
    a_one = lax.dynamic_index_in_dim(a_model, pick, 1, keepdims=False)
    b_one = lax.dynamic_index_in_dim(b_model, pick, 1, keepdims=False)
    single_hidden_input_map = lax.dynamic_index_in_dim(a_hidden, pick, 0, keepdims=False)
    b_hidden_one = lax.dynamic_index_in_dim(b_hidden, pick, 1, keepdims=False)
    positions = jnp.arange(tokens.shape[0], dtype=jnp.int32)
    visible = visible_pairs(positions, positions, starts)
    normed = low(norm_rows(tokens, attention_norm_gain))
    query = low_back(adapted(normed, query_key_value_weight[0], a_one[0], b_one[0]))
    key = low_back(adapted(normed, query_key_value_weight[1], a_one[1], b_one[1]))
    value = low_back(low(adapted(normed, query_key_value_weight[2], a_one[2], b_one[2])))
    query_turned = low(rotate(query, positions))
    key_turned = low(rotate(key, positions))
    mixed = low_back(low(attention(query_turned, key_turned, value, visible)))
    branch = low_back(adapted(mixed, attention_output_weight, a_one[3], b_one[3]))
    middle = tokens + BRANCH * branch
    normed_second = low(norm_rows(middle, feedforward_norm_gain))
    gate = low_back(adapted(normed_second, gate_up_projection_weight[0], a_one[4], b_hidden_one[0]))
    up = low_back(adapted(normed_second, gate_up_projection_weight[1], a_one[5], b_hidden_one[1]))
    hidden = low_back(low(jax.nn.silu(gate) * up))
    feed = low_back(adapted(hidden, down_projection_weight, single_hidden_input_map, b_one[4]))
    return middle + BRANCH * feed

def reference(tokens, cotangent, sequence_adapter_index, image_span_start, attention_norm_gain, feedforward_norm_gain, query_key_value_weight, attention_output_weight, gate_up_projection_weight, down_projection_weight, adapter_model_input_maps, adapter_model_output_maps, adapter_hidden_input_map, adapter_hidden_output_maps):
    frozen = tuple((weight_matrix.astype(jnp.float32) for weight_matrix in (attention_norm_gain, feedforward_norm_gain, query_key_value_weight, attention_output_weight, gate_up_projection_weight, down_projection_weight)))
    adapter_bank = tuple((weight_matrix.astype(jnp.float32) for weight_matrix in (adapter_model_input_maps, adapter_model_output_maps, adapter_hidden_input_map, adapter_hidden_output_maps)))

    def one_sequence(totals, items):
        sequence, incoming, pick, starts = items

        def forward(inputs, a_model, b_model, a_hidden, b_hidden):
            return block(inputs, a_model, b_model, a_hidden, b_hidden, frozen, pick, starts)
        result, backward = jax.vjp(forward, sequence.astype(jnp.float32), *adapter_bank)
        grads = backward(incoming.astype(jnp.float32))
        totals = tuple((total + piece for total, piece in zip(totals, grads[1:])))
        return (totals, (result.astype(jnp.bfloat16), grads[0]))
    start_totals = tuple((jnp.zeros(weight_matrix.shape, jnp.float32) for weight_matrix in adapter_bank))
    totals, (outputs, input_grads) = lax.scan(one_sequence, start_totals, (tokens, cotangent, sequence_adapter_index, image_span_start))
    return (outputs, input_grads, totals[0], totals[1], totals[2], totals[3])
```

```python
import functools
import math

import jax
import jax.numpy as jnp
from jax import lax
from jax.experimental import pallas as pl
from jax.experimental.pallas import tpu as pltpu
from jax.sharding import PartitionSpec as P

HDIM = 64
SPAN = 256
EPS = 1e-05
THETA = 10000.0
BRANCH = 1.4 / math.sqrt(40.0)
EXTRA = 128
F32 = jnp.float32
BF16 = jnp.bfloat16
LOG2E = math.log2(math.e)
VMEM_LIMIT = 56 << 20


def hop(values, axis, bit):
    size = lax.axis_size(axis)
    return lax.ppermute(values, axis, [(i, i ^ bit) for i in range(size)])


def core(values):
    return hop(values, "shard", 1)


def across(values):
    return hop(values, "shard", 2)


def gather_tokens(own):
    far = across(own)
    near = core(own)
    return own, near, far, core(far)


def scatter_tokens(blocks):
    chip_sum = (blocks[2].astype(F32) + core(blocks[3]).astype(F32)).astype(BF16)
    far = across(chip_sum)
    near = core(blocks[1])
    return blocks[0].astype(F32) + near.astype(F32) + far.astype(F32)


def sum_group(values):
    other = rows_of(core(values), 4)
    other = jnp.concatenate([other[1], other[0], other[3], other[2]])
    values = (values.astype(F32) + other.astype(F32)).astype(BF16)
    far = rows_of(across(values), 2)
    return (values.astype(F32) + jnp.concatenate([far[1], far[0]]).astype(F32)).astype(BF16)


def rows_of(values, count):
    size = values.shape[0] // count
    return tuple(values[i * size : (i + 1) * size] for i in range(count))


def norm_rows(values, gain):
    return values * lax.rsqrt(jnp.mean(values * values, axis=-1, keepdims=True) + EPS) * gain


def norm_back(values, gain, grad):
    width = values.shape[-1]
    scale = lax.rsqrt(jnp.mean(values * values, axis=-1, keepdims=True) + EPS)
    moved = grad * gain
    inner = jnp.sum(values * moved, axis=-1, keepdims=True) / width
    return scale * moved - values * (scale * scale * scale) * inner


def dot(left, right):
    return jnp.dot(left, right, preferred_element_type=F32)


def dot_t(left, right):
    return lax.dot_general(left, right, (((1,), (1,)), ((), ())), preferred_element_type=F32)


def t_dot(left, right):
    return lax.dot_general(left, right, (((0,), (0,)), ((), ())), preferred_element_type=F32)


def picked(bank, pick, place):
    per = bank.shape[1]
    rank = bank.shape[2]
    owner = pick // per
    mine = lax.dynamic_index_in_dim(bank, pick % per, 1, keepdims=False)
    mine = jnp.where(owner == place, mine, jnp.zeros_like(mine))
    chip = mine + core(mine)
    inside = place % 2
    part = lax.dynamic_slice_in_dim(chip, inside * (rank // 2), rank // 2, 1)
    far = across(part)
    other = core(far)
    low = jnp.where(inside == 0, far, other)
    high = jnp.where(inside == 0, other, far)
    return chip + jnp.concatenate([low, high], axis=1)


def pad_columns(pieces, width):
    used = sum(piece.shape[1] for piece in pieces)
    rest = jnp.zeros((pieces[0].shape[0], width - used), pieces[0].dtype)
    return jnp.concatenate(list(pieces) + [rest], axis=1)


def gather_reps(values, rep_place):
    size = lax.axis_size("rep")
    buffer = jnp.zeros((size,) + values.shape, values.dtype)
    buffer = lax.dynamic_update_slice_in_dim(buffer, values[None], rep_place, 0)
    bit = 1
    while bit < size:
        base = (rep_place // bit) * bit
        have = lax.dynamic_slice_in_dim(buffer, base, bit, 0)
        got = hop(have, "rep", bit)
        buffer = lax.dynamic_update_slice_in_dim(buffer, got, base ^ bit, 0)
        bit *= 2
    return buffer


def owned_sums(values, chosen, place, rep_place):
    group = lax.axis_size("shard")
    everyone = gather_reps(values.astype(BF16), rep_place)
    adapters = chosen.shape[1]
    per = adapters // group

    def sums_for(owner):
        marks = lax.dynamic_slice_in_dim(chosen, owner * per, per, 1)
        return jnp.sum(
            marks[:, :, None, None] * everyone[:, None].astype(F32), axis=0
        ).astype(BF16)

    got = jnp.zeros((group, per) + values.shape, BF16)
    got = lax.dynamic_update_slice_in_dim(got, sums_for(place)[None], place, 0)
    for j in range(1, group):
        arrived = hop(sums_for(place ^ j), "shard", j)
        got = lax.dynamic_update_slice_in_dim(got, arrived[None], place ^ j, 0)
    return jnp.concatenate([got[i] for i in range(group)], axis=-1).astype(F32)


def exchange(weight, size, place, rep_place):
    rows = weight.shape[1]
    quarter = rows // 4
    part = rep_place % 4

    def columns(owner):
        return lax.dynamic_slice_in_dim(weight, owner * size, size, 2)

    pieces = [(place * rows, columns(place)), ((place ^ 1) * rows, core(columns(place ^ 1)))]
    for j in (2, 3):
        mine = lax.dynamic_slice(
            weight, (0, part * quarter, (place ^ j) * size), (weight.shape[0], quarter, size)
        )
        first = hop(mine, "shard", j)
        near, late = (2, 1) if j == 2 else (1, 2)
        second = hop(first, "rep", near)
        third = hop(first, "rep", late)
        fourth = hop(second, "rep", late)
        for bits, piece in ((0, first), (near, second), (late, third), (near ^ late, fourth)):
            pieces.append(((place ^ j) * rows + (part ^ bits) * quarter, piece))
    offsets = jnp.stack([row.astype(jnp.int32) for row, _ in pieces])
    return offsets, [piece for _, piece in pieces]


def load_pieces(offsets, pieces, whole, sems):
    copies = []
    for number, piece in enumerate(pieces):
        start = pl.multiple_of(offsets[number], 16)
        target = whole.at[:, pl.ds(start, piece.shape[1]), :]
        copy = pltpu.make_async_copy(piece, target, sems.at[number])
        copy.start()
        copies.append(copy)
    return copies


def vmem():
    return pl.BlockSpec(memory_space=pltpu.VMEM)


def smem():
    return pl.BlockSpec(memory_space=pltpu.SMEM)


def anywhere():
    return pl.BlockSpec(memory_space=pl.ANY)


def call(kernel, outs, in_specs, out_specs, scratch, flops, moved, name, **more):
    return pl.pallas_call(
        kernel,
        out_shape=outs,
        in_specs=in_specs,
        out_specs=out_specs,
        scratch_shapes=scratch,
        compiler_params=pltpu.CompilerParams(vmem_limit_bytes=VMEM_LIMIT),
        cost_estimate=pl.CostEstimate(flops=flops, bytes_accessed=moved, transcendentals=0),
        name=name,
        **more,
    )


def turn(values, cosine, sine):
    half = HDIM // 2
    turned = jnp.concatenate([-values[:, half:], values[:, :half]], axis=1)
    return values * cosine + turned * sine


def project(blocks, place, offsets, pieces, a_first, b_first, cosine, sine):
    rows, width = blocks[0].shape
    count = len(blocks)
    size = pieces[0].shape[2]
    heads = size // HDIM
    rank = b_first.shape[1]
    n = len(pieces)

    def kernel(place_ref, offsets_ref, *refs):
        x_refs, refs = refs[:count], refs[count:]
        piece_refs, refs = refs[:n], refs[n:]
        a_ref, b_ref, cos_ref, sin_ref, q_ref, k_ref, v_ref, narrow_ref, whole, sems = refs
        copies = load_pieces(offsets_ref, piece_refs, whole, sems)
        for block in range(count):
            narrow = dot_t(x_refs[block][...], a_ref[...]).astype(BF16)
            narrow_ref[pl.ds(block * rows, rows), :] = narrow
        for copy in copies:
            copy.wait()
        for block in range(count):
            start = pl.multiple_of((place_ref[0] ^ block) * rows, rows)
            x = x_refs[block][...]
            narrow = narrow_ref[pl.ds(block * rows, rows), :]
            cosine_here = cos_ref[pl.ds(start, rows), :]
            sine_here = sin_ref[pl.ds(start, rows), :]
            for number, out in enumerate((q_ref, k_ref, v_ref)):
                pre = dot(x, whole[number]) + dot(
                    narrow[:, number * rank : (number + 1) * rank], b_ref[number]
                )
                for head in range(heads):
                    part = pre[:, head * HDIM : (head + 1) * HDIM]
                    if number < 2:
                        part = turn(part, cosine_here, sine_here)
                    out[head, pl.ds(start, rows), :] = part.astype(BF16)

    by_heads = jax.ShapeDtypeStruct((heads, rows * count, HDIM), BF16)
    return call(
        kernel,
        [by_heads] * 3 + [jax.ShapeDtypeStruct((rows * count, 3 * rank), BF16)],
        [smem(), smem()] + [vmem()] * count + [anywhere()] * n + [vmem()] * 4,
        [vmem()] * 4,
        [pltpu.VMEM((3, width, size), BF16), pltpu.SemaphoreType.DMA((n,))],
        2 * rows * count * width * 3 * size,
        2 * (rows * count * width + 3 * width * size + 6 * rows * count * size),
        "project",
    )(place[None], offsets, *blocks, *pieces, a_first, b_first, cosine, sine)


def label_of(positions, starts_ref):
    label = jnp.full(positions.shape, -1, jnp.int32)
    for number in range(starts_ref.shape[0]):
        inside = (positions >= starts_ref[number]) & (positions < starts_ref[number] + SPAN)
        label = jnp.where(inside, jnp.int32(number), label)
    return label


def hidden_bias(query_at, key_at, starts_ref):
    query_label = label_of(query_at, starts_ref)
    key_label = label_of(key_at, starts_ref)
    visible = (key_at <= query_at) | (query_label == key_label) & (query_label >= 0)
    return jnp.where(visible, 0.0, -1e30)


def crosses(starts_ref, edge, rows):
    hit = None
    for number in range(starts_ref.shape[0]):
        start = starts_ref[number]
        here = (start < edge) & (start + SPAN > edge)
        hit = here if hit is None else hit | here
    return hit


def attend(starts, query, key, value, rows):
    heads, length, _ = query.shape
    count = length // rows
    factor = LOG2E / math.sqrt(HDIM)

    def kernel(starts_ref, q_ref, k_ref, v_ref, o_ref, bias):
        @pl.when(pl.program_id(0) == 0)
        def _():
            for block in range(count):
                shape = (rows, 2 * rows)
                query_at = block * rows + lax.broadcasted_iota(jnp.int32, shape, 0)
                key_at = block * rows + lax.broadcasted_iota(jnp.int32, shape, 1)
                bias[block] = hidden_bias(query_at, key_at, starts_ref)

        def one(block, extra):
            low, high = block * rows, (block + 1 + extra) * rows
            q = q_ref[0, low : low + rows, :]
            edge = dot_t(q, k_ref[0, low:high, :]) + bias[block, :, : high - low]
            top = jnp.max(edge, axis=1, keepdims=True)
            if block:
                before = dot_t(q, k_ref[0, :low, :])
                top = jnp.maximum(top, jnp.max(before, axis=1, keepdims=True))
            shift = top * factor
            weight = jnp.exp2(edge * factor - shift)
            total = jnp.sum(weight, axis=1, keepdims=True)
            out = dot(weight.astype(BF16), v_ref[0, low:high, :])
            if block:
                weight = jnp.exp2(before * factor - shift)
                total = total + jnp.sum(weight, axis=1, keepdims=True)
                out = out + dot(weight.astype(BF16), v_ref[0, :low, :])
            o_ref[0, low : low + rows, :] = (out / total).astype(BF16)

        for block in range(count):
            if block == count - 1:
                one(block, 0)
                continue
            wide = crosses(starts_ref, (block + 1) * rows, rows)
            pl.when(wide)(functools.partial(one, block, 1))
            pl.when(jnp.logical_not(wide))(functools.partial(one, block, 0))

    spec = pl.BlockSpec((1, length, HDIM), lambda h: (h, 0, 0))
    return call(
        kernel,
        jax.ShapeDtypeStruct(query.shape, BF16),
        [smem(), spec, spec, spec],
        spec,
        [pltpu.VMEM((count, rows, 2 * rows), F32)],
        4 * heads * length * length * HDIM * 4,
        16 * heads * length * HDIM,
        "attend",
        grid=(heads,),
    )(starts, query, key, value)


def attend_back(starts, query, key, value, grad, cosine, sine, rows):
    heads, length, _ = query.shape
    count = length // rows
    scale = 1.0 / math.sqrt(HDIM)
    factor = LOG2E * scale

    def kernel(
        starts_ref, q_ref, k_ref, v_ref, g_ref, cos_ref, sin_ref, dq_ref, dk_ref, dv_ref,
        bias, key_sum, value_sum, key_turned,
    ):
        @pl.when(pl.program_id(0) == 0)
        def _():
            for block in range(count):
                shape = (2 * rows, rows)
                query_at = block * rows + lax.broadcasted_iota(jnp.int32, shape, 1)
                key_at = block * rows + lax.broadcasted_iota(jnp.int32, shape, 0)
                bias[block] = hidden_bias(query_at, key_at, starts_ref)

        key_sum[...] = jnp.zeros_like(key_sum)
        value_sum[...] = jnp.zeros_like(value_sum)
        key_turned[...] = k_ref[0].astype(F32).T.astype(BF16)

        def one(block, extra):
            low, high = block * rows, (block + 1 + extra) * rows
            q = q_ref[0, low : low + rows, :]
            g = g_ref[0, low : low + rows, :]
            raw = dot_t(k_ref[0, low:high, :], q) + bias[block, : high - low, :]
            if block:
                raw = jnp.concatenate([dot_t(k_ref[0, :low, :], q), raw], axis=0)
            top = jnp.max(raw, axis=0, keepdims=True)
            weight = jnp.exp2(raw * factor - top * factor)
            probs = weight * (1.0 / jnp.sum(weight, axis=0, keepdims=True))
            grad_probs = dot_t(v_ref[0, :high, :], g)
            inner = jnp.sum(grad_probs * probs, axis=0, keepdims=True)
            grad_scores = (probs * (grad_probs - inner)).astype(BF16)
            value_sum[:high, :] += dot(probs.astype(BF16), g)
            key_sum[:high, :] += dot(grad_scores, q)
            turned = dot(key_turned[:, :high], grad_scores)
            back = turned.T * scale
            dq_ref[0, low : low + rows, :] = turn(
                back, cos_ref[low : low + rows, :], -sin_ref[low : low + rows, :]
            ).astype(BF16)

        for block in range(count):
            if block == count - 1:
                one(block, 0)
                continue
            wide = crosses(starts_ref, (block + 1) * rows, rows)
            pl.when(wide)(functools.partial(one, block, 1))
            pl.when(jnp.logical_not(wide))(functools.partial(one, block, 0))
        dk_ref[0] = turn(key_sum[...] * scale, cos_ref[...], -sin_ref[...]).astype(BF16)
        dv_ref[0] = value_sum[...].astype(BF16)

    spec = pl.BlockSpec((1, length, HDIM), lambda h: (h, 0, 0))
    table = pl.BlockSpec((length, HDIM), lambda h: (0, 0))
    return call(
        kernel,
        [jax.ShapeDtypeStruct(query.shape, BF16)] * 3,
        [smem(), spec, spec, spec, spec, table, table],
        [spec] * 3,
        [
            pltpu.VMEM((count, 2 * rows, rows), F32),
            pltpu.VMEM((length, HDIM), F32),
            pltpu.VMEM((length, HDIM), F32),
            pltpu.VMEM((HDIM, length), BF16),
        ],
        10 * heads * length * length * HDIM * 4,
        32 * heads * length * HDIM,
        "attend_back",
        grid=(heads,),
    )(starts, query, key, value, grad, cosine, sine)


def rows_by_heads(ref, start, rows):
    return jnp.concatenate([ref[head, pl.ds(start, rows), :] for head in range(ref.shape[0])], axis=1)


def close_attention(mixed, place, weight, a_out, wanted, rows):
    size, width = weight.shape
    rank = a_out.shape[0]

    def kernel(place_ref, m_ref, w_ref, a_ref, *outs):
        for block, out in zip(wanted, outs):
            start = pl.multiple_of((place_ref[0] ^ block) * rows, rows)
            here = rows_by_heads(m_ref, start, rows)
            out[:, :width] = dot(here, w_ref[...]).astype(BF16)
            narrow = dot_t(here, a_ref[...]).astype(BF16)
            out[:, width:] = jnp.concatenate(
                [narrow, jnp.zeros((rows, EXTRA - rank), BF16)], axis=1
            )

    return call(
        kernel,
        [jax.ShapeDtypeStruct((rows, width + EXTRA), BF16)] * len(wanted),
        [smem()] + [vmem()] * 3,
        [vmem()] * len(wanted),
        [],
        2 * rows * len(wanted) * size * width,
        2 * size * width + 2 * rows * len(wanted) * (width + size),
        "close_attention",
    )(place[None], mixed, weight, a_out)


def open_attention(blocks, place, mixed, weight, a_out, b_out):
    rows, width_ext = blocks[0].shape
    size, width = weight.shape
    rank = a_out.shape[0]
    count = len(blocks)
    heads = size // HDIM

    def kernel(place_ref, *refs):
        g_refs, refs = refs[:count], refs[count:]
        m_ref, w_ref, a_ref, b_ref, out, sum_ref = refs
        total = jnp.zeros((rank, size), F32)
        for block in range(count):
            start = pl.multiple_of((place_ref[0] ^ block) * rows, rows)
            grad = g_refs[block][:, :width]
            narrow = dot_t(grad, b_ref[...]).astype(BF16)
            back = dot_t(grad, w_ref[...]) + dot(narrow, a_ref[...])
            for head in range(heads):
                out[head, pl.ds(start, rows), :] = back[:, head * HDIM : (head + 1) * HDIM].astype(BF16)
            total = total + t_dot(narrow, rows_by_heads(m_ref, start, rows))
        sum_ref[...] = total

    return call(
        kernel,
        [
            jax.ShapeDtypeStruct(mixed.shape, BF16),
            jax.ShapeDtypeStruct((rank, size), F32),
        ],
        [smem()] + [vmem()] * (count + 4),
        [vmem()] * 2,
        [],
        2 * rows * count * size * width,
        2 * size * width + 2 * rows * count * (width + 2 * size),
        "open_attention",
    )(place[None], *blocks, mixed, weight, a_out, b_out)


def feed_forward(blocks, grads, offsets, pieces, down, a_mlp, b_down, a_hidden, b_hidden):
    rows, width = blocks[0].shape
    count = len(blocks)
    size = down.shape[0]
    rank = b_down.shape[0]
    n = len(pieces)

    def kernel(offsets_ref, *refs):
        x_refs, refs = refs[:count], refs[count:]
        g_refs, refs = refs[:count], refs[count:]
        piece_refs, refs = refs[:n], refs[n:]
        down_hbm, am_ref, bd_ref, ah_ref, bh_ref = refs[:5]
        refs = refs[5:]
        feed_refs, refs = refs[:count], refs[count:]
        back_refs, refs = refs[:count], refs[count:]
        a_sum, b_sum, whole, down_ref, sems, down_sem = refs
        copies = load_pieces(offsets_ref, piece_refs, whole, sems)
        down_copy = pltpu.make_async_copy(down_hbm, down_ref, down_sem)
        down_copy.start()
        for copy in copies:
            copy.wait()
        pad = jnp.zeros((rows, EXTRA - rank), BF16)
        for block in range(count):
            x = x_refs[block][...]
            narrow = dot_t(x, am_ref[...]).astype(BF16)
            gate = dot(x, whole[0]) + dot(narrow[:, :rank], bh_ref[0])
            up = dot(x, whole[1]) + dot(narrow[:, rank:], bh_ref[1])
            sigmoid = 1.0 / (1.0 + jnp.exp(-gate))
            silu = gate * sigmoid
            hidden = (silu * up).astype(BF16)
            if block == 0:
                down_copy.wait()
            feed_refs[block][:, :width] = dot(hidden, down_ref[...]).astype(BF16)
            feed_refs[block][:, width:] = jnp.concatenate(
                [dot_t(hidden, ah_ref[...]).astype(BF16), pad], axis=1
            )
            grad = g_refs[block][...]
            grad_narrow = dot_t(grad, bd_ref[...]).astype(BF16)
            grad_hidden = dot_t(grad, down_ref[...]) + dot(grad_narrow, ah_ref[...])
            grad_hidden = grad_hidden.astype(BF16).astype(F32)
            grad_up = (grad_hidden * silu).astype(BF16)
            grad_gate = (grad_hidden * up * (sigmoid * (1.0 + gate * (1.0 - sigmoid)))).astype(BF16)
            back = dot_t(grad_gate, whole[0]) + dot_t(grad_up, whole[1])
            back_refs[block][:, :width] = back.astype(BF16)
            back_refs[block][:, width:] = jnp.concatenate(
                [
                    dot_t(grad_gate, bh_ref[0]).astype(BF16),
                    dot_t(grad_up, bh_ref[1]).astype(BF16),
                    pad[:, rank:],
                ],
                axis=1,
            )
            terms = (
                t_dot(grad_narrow, hidden),
                t_dot(narrow[:, :rank], grad_gate),
                t_dot(narrow[:, rank:], grad_up),
            )
            if block == 0:
                a_sum[...] = terms[0]
                b_sum[0] = terms[1]
                b_sum[1] = terms[2]
            else:
                a_sum[...] += terms[0]
                b_sum[0] += terms[1]
                b_sum[1] += terms[2]

    out = jax.ShapeDtypeStruct((rows, width + EXTRA), BF16)
    return call(
        kernel,
        [out] * (2 * count)
        + [jax.ShapeDtypeStruct((rank, size), F32), jax.ShapeDtypeStruct((2, rank, size), F32)],
        [smem()] + [vmem()] * (2 * count) + [anywhere()] * (n + 1) + [vmem()] * 4,
        [vmem()] * (2 * count + 2),
        [
            pltpu.VMEM((2, width, size), BF16),
            pltpu.VMEM((size, width), BF16),
            pltpu.SemaphoreType.DMA((n,)),
            pltpu.SemaphoreType.DMA,
        ],
        12 * rows * count * width * size,
        6 * width * size + 8 * rows * count * width,
        "feed_forward",
    )(offsets, *blocks, *grads, *pieces, down, a_mlp, b_down, a_hidden, b_hidden)


def project_back(grads, place, offsets, pieces, narrow_first, b_first, wanted, rows):
    heads = grads[0].shape[0]
    maps, _, size = pieces[0].shape
    width = 4 * pieces[0].shape[1]
    rank = b_first.shape[1]
    n = len(pieces)
    count = len(wanted)

    def kernel(place_ref, offsets_ref, *refs):
        g_refs, refs = refs[:maps], refs[maps:]
        piece_refs, refs = refs[:n], refs[n:]
        narrow_ref, b_ref = refs[:2]
        back_refs, refs = refs[2 : 2 + count], refs[2 + count :]
        thin_ref, sum_ref, whole, sems = refs
        copies = load_pieces(offsets_ref, piece_refs, whole, sems)
        waiting = True
        for index, block in enumerate(wanted):
            start = pl.multiple_of((place_ref[0] ^ block) * rows, rows)
            parts = [rows_by_heads(g_refs[number], start, rows) for number in range(maps)]
            narrow = narrow_ref[block * rows : (block + 1) * rows, :]
            thin = [dot_t(parts[number], b_ref[number]) for number in range(maps)]
            thin_ref[index * rows : (index + 1) * rows, :] = jnp.concatenate(thin, axis=1).astype(BF16)
            for number in range(maps):
                term = t_dot(narrow[:, number * rank : (number + 1) * rank], parts[number])
                if index == 0:
                    sum_ref[number] = term
                else:
                    sum_ref[number] += term
            if waiting:
                for copy in copies:
                    copy.wait()
                waiting = False
            back = dot_t(parts[0], whole[0])
            for number in range(1, maps):
                back = back + dot_t(parts[number], whole[number])
            back_refs[index][...] = back.astype(BF16)

    return call(
        kernel,
        [jax.ShapeDtypeStruct((rows, width), BF16)] * count
        + [
            jax.ShapeDtypeStruct((rows * count, maps * rank), BF16),
            jax.ShapeDtypeStruct((maps, rank, size), F32),
        ],
        [smem(), smem()] + [vmem()] * maps + [anywhere()] * n + [vmem()] * 2,
        [vmem()] * (count + 2),
        [pltpu.VMEM((maps, width, size), BF16), pltpu.SemaphoreType.DMA((n,))],
        2 * rows * count * width * maps * size,
        2 * (rows * count * (width + maps * size) + maps * width * size),
        "project_back",
    )(place[None], offsets, *grads, *pieces, narrow_first, b_first)


def shards(
    tokens,
    cotangent,
    sequence_adapter_index,
    image_span_start,
    attention_norm_gain,
    feedforward_norm_gain,
    query_key_value_weight,
    attention_output_weight,
    gate_up_projection_weight,
    down_projection_weight,
    adapter_model_input_maps,
    adapter_model_output_maps,
    adapter_hidden_input_map,
    adapter_hidden_output_maps,
):
    rows = tokens.shape[1]
    width = tokens.shape[2]
    rank = adapter_model_input_maps.shape[2]
    group = lax.axis_size("shard")
    place = lax.axis_index("shard").astype(jnp.int32)
    rep_place = lax.axis_index("rep").astype(jnp.int32)
    pick = sequence_adapter_index[0]
    starts = image_span_start[0]
    head_cols = width // group
    ff_cols = down_projection_weight.shape[0]

    gain_one = attention_norm_gain.astype(F32)
    gain_two = feedforward_norm_gain.astype(F32)
    residual_in = tokens[0].astype(F32)
    grad_out = cotangent[0].astype(F32)

    normed = norm_rows(residual_in, gain_one).astype(BF16)
    grad_feed = (BRANCH * grad_out).astype(BF16)
    first_offsets, first_pieces = exchange(query_key_value_weight, head_cols, place, rep_place)
    first_blocks = gather_tokens(normed)
    model_one = picked(
        jnp.concatenate([adapter_model_input_maps, adapter_model_output_maps]), pick, place
    )
    hidden_one = picked(
        jnp.concatenate([adapter_hidden_input_map[None], adapter_hidden_output_maps]), pick, place
    )
    a_one, b_one = model_one[:6], model_one[6:]

    def own_columns(values, size):
        return lax.dynamic_slice_in_dim(values, place * size, size, values.ndim - 1)

    a_first = a_one[0:3].reshape(3 * rank, width)
    b_first = own_columns(b_one[0:3], head_cols)
    a_out = own_columns(a_one[3], head_cols)
    b_out = b_one[3]
    a_mlp = a_one[4:6].reshape(2 * rank, width)
    b_down = b_one[4]
    hidden_cols = own_columns(hidden_one, ff_cols)
    a_hidden, b_hidden = hidden_cols[0], hidden_cols[1:]

    picks = lax.all_gather(sequence_adapter_index, "rep", axis=0, tiled=True)
    adapters = adapter_model_input_maps.shape[1] * group
    chosen = (picks[:, None] == jnp.arange(adapters, dtype=jnp.int32)[None, :]).astype(F32)

    half = HDIM // 2
    frequency = jnp.exp(jnp.arange(half, dtype=F32) * (-2.0 / HDIM) * math.log(THETA))
    angle = jnp.arange(rows * group, dtype=jnp.int32).astype(F32)[:, None] * frequency[None, :]
    cosine = jnp.concatenate([jnp.cos(angle), jnp.cos(angle)], axis=1)
    sine = jnp.concatenate([jnp.sin(angle), jnp.sin(angle)], axis=1)

    query, key, value, narrow_first = project(
        first_blocks, place, first_offsets, first_pieces, a_first, b_first, cosine, sine
    )
    mlp_offsets, mlp_pieces = exchange(gate_up_projection_weight, ff_cols, place, rep_place)
    feed_blocks = gather_tokens(grad_feed)
    mixed = attend(starts, query, key, value, rows)

    far_out = close_attention(mixed, place, attention_output_weight, a_out, (2, 3), rows)
    near_out = close_attention(mixed, place, attention_output_weight, a_out, (0, 1), rows)
    branch_own = scatter_tokens((*near_out, *far_out))
    narrow_out = branch_own[:, width : width + rank].astype(BF16)
    branch = branch_own[:, :width] + dot(narrow_out, b_out)
    middle = residual_in + BRANCH * branch
    normed_second = norm_rows(middle, gain_two).astype(BF16)
    second_blocks = gather_tokens(normed_second)

    *parts, a_near, b_near = feed_forward(
        second_blocks[:2], feed_blocks[:2], mlp_offsets, mlp_pieces, down_projection_weight,
        a_mlp, b_down, a_hidden, b_hidden,
    )
    feed_near, back_near = parts[:2], parts[2:]
    *parts, a_far, b_far = feed_forward(
        second_blocks[2:], feed_blocks[2:], mlp_offsets, mlp_pieces, down_projection_weight,
        a_mlp, b_down, a_hidden, b_hidden,
    )
    feed_far, back_far = parts[:2], parts[2:]
    second_own = scatter_tokens((*back_near, *back_far))
    grad_narrow_mlp = second_own[:, width : width + 2 * rank].astype(BF16)
    grad_normed_second = second_own[:, :width] + dot(grad_narrow_mlp, a_mlp)
    grad_middle = grad_out + norm_back(middle, gain_two, grad_normed_second)
    grad_branch = (BRANCH * grad_middle).astype(BF16)
    branch_blocks = gather_tokens(
        pad_columns([grad_branch, narrow_out, grad_narrow_mlp], width + EXTRA)
    )

    feed_own = scatter_tokens((*feed_near, *feed_far))
    narrow_down = feed_own[:, width : width + rank].astype(BF16)
    feed = feed_own[:, :width] + dot(narrow_down, b_down)
    output = (middle + BRANCH * feed).astype(BF16)
    narrow_down_blocks = gather_tokens(narrow_down)

    grad_mixed, grad_a_out = open_attention(
        branch_blocks, place, mixed, attention_output_weight, a_out, b_out
    )
    first_grads = attend_back(starts, query, key, value, grad_mixed, cosine, sine, rows)
    *far_back, thin_far, b_first_far = project_back(
        first_grads, place, first_offsets, first_pieces, narrow_first, b_first, (2, 3), rows
    )
    *near_back, thin_near, b_first_near = project_back(
        first_grads, place, first_offsets, first_pieces, narrow_first, b_first, (0, 1), rows
    )
    grad_narrow_first = sum_group(jnp.concatenate([thin_near, thin_far]))
    grad_normed = scatter_tokens((*near_back, *far_back)) + dot(grad_narrow_first[:rows], a_first)
    input_grad = grad_middle + norm_back(residual_in, gain_one, grad_normed)

    def columns_product(thin, wide):
        total = sum(t_dot(left, right) for left, right in zip(thin, wide))
        return own_columns(total, head_cols)

    wide_branch = [block[:, :width] for block in branch_blocks]
    thin_out = [block[:, width : width + rank] for block in branch_blocks]
    thin_mlp = [block[:, width + rank : width + 3 * rank] for block in branch_blocks]
    early_model = jnp.concatenate(
        [
            grad_a_out,
            columns_product(thin_mlp, second_blocks),
            columns_product(thin_out, wide_branch),
            columns_product(narrow_down_blocks, feed_blocks),
        ]
    )
    early_hidden = jnp.concatenate(
        [a_near + a_far, (b_near + b_far).reshape(2 * rank, ff_cols)]
    )
    late_model = jnp.concatenate(
        [
            columns_product(rows_of(grad_narrow_first, group), first_blocks),
            (b_first_near + b_first_far).reshape(3 * rank, head_cols),
        ]
    )
    early_model = owned_sums(early_model, chosen, place, rep_place)
    early_hidden = owned_sums(early_hidden, chosen, place, rep_place)
    late_model = owned_sums(late_model, chosen, place, rep_place)

    def maps_first(values):
        per, count, n = values.shape
        return values.reshape(per, count // rank, rank, n).transpose(1, 0, 2, 3)

    early_model, early_hidden, late_model = map(maps_first, (early_model, early_hidden, late_model))
    grad_a_model = jnp.concatenate([late_model[0:3], early_model[0:3]])
    grad_b_model = jnp.concatenate([late_model[3:6], early_model[3:5]])
    return (
        output[None], input_grad[None], grad_a_model, grad_b_model, early_hidden[0], early_hidden[1:3],
    )


def solution(mesh):
    in_specs = (
        P("rep", "shard", None),
        P("rep", "shard", None),
        P("rep"),
        P("rep", None),
        P(),
        P(),
        P(None, "shard", None),
        P("shard", None),
        P(None, "shard", None),
        P("shard", None),
        P(None, "shard", None, None),
        P(None, "shard", None, None),
        P("shard", None, None),
        P(None, "shard", None, None),
    )
    out_specs = (
        P("rep", "shard", None),
        P("rep", "shard", None),
        P(None, "shard", None, None),
        P(None, "shard", None, None),
        P("shard", None, None),
        P(None, "shard", None, None),
    )
    return jax.shard_map(shards, mesh=mesh, in_specs=in_specs, out_specs=out_specs, check_vma=False)
```

```python
import functools
import math

import jax
import jax.numpy as jnp
from jax import lax
from jax.experimental import pallas as pl
from jax.experimental.pallas import tpu as pltpu
from jax.sharding import PartitionSpec as P

HDIM = 64
SPAN = 256
EPS = 1e-05
THETA = 10000.0
BRANCH = 1.4 / math.sqrt(40.0)
EXTRA = 128
F32 = jnp.float32
BF16 = jnp.bfloat16
LOG2E = math.log2(math.e)
VMEM_LIMIT = 56 << 20


def hop(values, axis, bit):
    size = lax.axis_size(axis)
    return lax.ppermute(values, axis, [(i, i ^ bit) for i in range(size)])


def core(values):
    return hop(values, "shard", 1)


def across(values):
    return hop(values, "shard", 2)


def rows_of(values, count):
    size = values.shape[0] // count
    return tuple(values[i * size : (i + 1) * size] for i in range(count))


def norm_rows(values, gain):
    return values * lax.rsqrt(jnp.mean(values * values, axis=-1, keepdims=True) + EPS) * gain


def norm_back(values, gain, grad):
    width = values.shape[-1]
    scale = lax.rsqrt(jnp.mean(values * values, axis=-1, keepdims=True) + EPS)
    moved = grad * gain
    inner = jnp.sum(values * moved, axis=-1, keepdims=True) / width
    return scale * moved - values * (scale * scale * scale) * inner


def dot(left, right):
    return jnp.dot(left, right, preferred_element_type=F32)


def dot_t(left, right):
    return lax.dot_general(left, right, (((1,), (1,)), ((), ())), preferred_element_type=F32)


def t_dot(left, right):
    return lax.dot_general(left, right, (((0,), (0,)), ((), ())), preferred_element_type=F32)


def pad_columns(pieces, width):
    used = sum(piece.shape[1] for piece in pieces)
    rest = jnp.zeros((pieces[0].shape[0], width - used), pieces[0].dtype)
    return jnp.concatenate(list(pieces) + [rest], axis=1)


def start_reps(values, rep_place):
    buffer = jnp.zeros((lax.axis_size("rep"),) + values.shape, values.dtype)
    return lax.dynamic_update_slice_in_dim(buffer, values[None], rep_place, 0)


def reps_step(buffer, rep_place, bit):
    base = (rep_place // bit) * bit
    have = lax.dynamic_slice_in_dim(buffer, base, bit, 0)
    return lax.dynamic_update_slice_in_dim(buffer, hop(have, "rep", bit), base ^ bit, 0)


def reps_rest(buffer, rep_place, bit):
    while bit < lax.axis_size("rep"):
        buffer = reps_step(buffer, rep_place, bit)
        bit *= 2
    return buffer


def send_sums(everyone, chosen, place):
    group = lax.axis_size("shard")
    per = chosen.shape[1] // group
    sent = []
    for j in range(group):
        marks = lax.dynamic_slice_in_dim(chosen, (place ^ j) * per, per, 1)
        sums = jnp.sum(marks[:, :, None, None] * everyone[:, None].astype(F32), axis=0).astype(BF16)
        sent.append(hop(sums, "shard", j) if j else sums)
    return sent


def arrange_sums(sent, place):
    got = jnp.zeros((len(sent),) + sent[0].shape, BF16)
    for j, piece in enumerate(sent):
        got = lax.dynamic_update_slice_in_dim(got, piece[None], place ^ j, 0)
    return got


def add_relative(values, other, bit):
    blocks = rows_of(other, 4)
    other = jnp.concatenate([blocks[i ^ bit] for i in range(4)])
    return (values.astype(F32) + other.astype(F32)).astype(BF16)


def chip_picked(bank, pick, place):
    per = bank.shape[1]
    rank = bank.shape[2]
    owner = pick // per
    mine = lax.dynamic_index_in_dim(bank, pick % per, 1, keepdims=False)
    mine = jnp.where(owner == place, mine, jnp.zeros_like(mine))
    chip = mine + core(mine)
    return chip, lax.dynamic_slice_in_dim(chip, (place % 2) * (rank // 2), rank // 2, 1)


def whole_picked(chip, far, place):
    other = core(far)
    low = jnp.where(place % 2 == 0, far, other)
    high = jnp.where(place % 2 == 0, other, far)
    return chip + jnp.concatenate([low, high], axis=1)


def after(value, *others):
    return lax.optimization_barrier((value, others))[0]


def leaving(weight, size, place, rep_place):
    quarter = weight.shape[1] // 4
    part = rep_place % 4
    return [
        lax.dynamic_slice(
            weight, (0, part * quarter, (place ^ j) * size), (weight.shape[0], quarter, size)
        )
        for j in (2, 3)
    ]


def finish(weight, size, first, second, third, place, rep_place, near):
    rows = weight.shape[1]
    quarter = rows // 4
    part = rep_place % 4
    own = lax.dynamic_slice_in_dim(weight, place * size, size, 2)
    pieces = [(place * rows, own), ((place ^ 1) * rows, near)]
    for number, (j, one, two) in enumerate(((2, 2, 1), (3, 1, 2))):
        parts = (first[number], second[number], *third[number])
        for bits, piece in zip((0, one, two, one ^ two), parts):
            pieces.append(((place ^ j) * rows + (part ^ bits) * quarter, piece))
    offsets = jnp.stack([row.astype(jnp.int32) for row, _ in pieces])
    return offsets, [piece for _, piece in pieces]


def near_columns(weight, size, place):
    return core(lax.dynamic_slice_in_dim(weight, (place ^ 1) * size, size, 2))


def load_pieces(offsets, pieces, whole, sems):
    copies = []
    for number, piece in enumerate(pieces):
        start = pl.multiple_of(offsets[number], 16)
        target = whole.at[:, pl.ds(start, piece.shape[1]), :]
        copy = pltpu.make_async_copy(piece, target, sems.at[number])
        copy.start()
        copies.append(copy)
    return copies


def vmem():
    return pl.BlockSpec(memory_space=pltpu.VMEM)


def smem():
    return pl.BlockSpec(memory_space=pltpu.SMEM)


def anywhere():
    return pl.BlockSpec(memory_space=pl.ANY)


def call(kernel, outs, in_specs, out_specs, scratch, flops, moved, name, **more):
    return pl.pallas_call(
        kernel,
        out_shape=outs,
        in_specs=in_specs,
        out_specs=out_specs,
        scratch_shapes=scratch,
        compiler_params=pltpu.CompilerParams(vmem_limit_bytes=VMEM_LIMIT),
        cost_estimate=pl.CostEstimate(flops=flops, bytes_accessed=moved, transcendentals=0),
        name=name,
        **more,
    )


def turn(values, cosine, sine):
    half = HDIM // 2
    turned = jnp.concatenate([-values[:, half:], values[:, :half]], axis=1)
    return values * cosine + turned * sine


def project(blocks, place, offsets, pieces, a_first, b_first, cosine, sine):
    rows, width = blocks[0].shape
    count = len(blocks)
    size = pieces[0].shape[2]
    heads = size // HDIM
    rank = b_first.shape[1]
    n = len(pieces)

    def kernel(place_ref, offsets_ref, *refs):
        x_refs, refs = refs[:count], refs[count:]
        piece_refs, refs = refs[:n], refs[n:]
        a_ref, b_ref, cos_ref, sin_ref, q_ref, k_ref, v_ref, narrow_ref, whole, sems = refs
        copies = load_pieces(offsets_ref, piece_refs, whole, sems)
        for block in range(count):
            narrow = dot_t(x_refs[block][...], a_ref[...]).astype(BF16)
            narrow_ref[pl.ds(block * rows, rows), :] = narrow
        for copy in copies:
            copy.wait()
        for block in range(count):
            start = pl.multiple_of((place_ref[0] ^ block) * rows, rows)
            x = x_refs[block][...]
            narrow = narrow_ref[pl.ds(block * rows, rows), :]
            cosine_here = cos_ref[pl.ds(start, rows), :]
            sine_here = sin_ref[pl.ds(start, rows), :]
            for number, out in enumerate((q_ref, k_ref, v_ref)):
                pre = dot(x, whole[number]) + dot(
                    narrow[:, number * rank : (number + 1) * rank], b_ref[number]
                )
                for head in range(heads):
                    part = pre[:, head * HDIM : (head + 1) * HDIM]
                    if number < 2:
                        part = turn(part, cosine_here, sine_here)
                    out[head, pl.ds(start, rows), :] = part.astype(BF16)

    by_heads = jax.ShapeDtypeStruct((heads, rows * count, HDIM), BF16)
    return call(
        kernel,
        [by_heads] * 3 + [jax.ShapeDtypeStruct((rows * count, 3 * rank), BF16)],
        [smem(), smem()] + [vmem()] * count + [anywhere()] * n + [vmem()] * 4,
        [vmem()] * 4,
        [pltpu.VMEM((3, width, size), BF16), pltpu.SemaphoreType.DMA((n,))],
        2 * rows * count * width * 3 * size,
        2 * (rows * count * width + 3 * width * size + 6 * rows * count * size),
        "project",
    )(place[None], offsets, *blocks, *pieces, a_first, b_first, cosine, sine)


def label_of(positions, starts_ref):
    label = jnp.full(positions.shape, -1, jnp.int32)
    for number in range(starts_ref.shape[0]):
        inside = (positions >= starts_ref[number]) & (positions < starts_ref[number] + SPAN)
        label = jnp.where(inside, jnp.int32(number), label)
    return label


def hidden_bias(query_at, key_at, starts_ref):
    query_label = label_of(query_at, starts_ref)
    key_label = label_of(key_at, starts_ref)
    visible = (key_at <= query_at) | (query_label == key_label) & (query_label >= 0)
    return jnp.where(visible, 0.0, -1e30)


def crosses(starts_ref, edge, rows):
    hit = None
    for number in range(starts_ref.shape[0]):
        start = starts_ref[number]
        here = (start < edge) & (start + SPAN > edge)
        hit = here if hit is None else hit | here
    return hit


def attend(starts, query, key, value, rows):
    heads, length, _ = query.shape
    count = length // rows
    factor = LOG2E / math.sqrt(HDIM)

    def kernel(starts_ref, q_ref, k_ref, v_ref, o_ref, bias):
        @pl.when(pl.program_id(0) == 0)
        def _():
            for block in range(count):
                shape = (rows, 2 * rows)
                query_at = block * rows + lax.broadcasted_iota(jnp.int32, shape, 0)
                key_at = block * rows + lax.broadcasted_iota(jnp.int32, shape, 1)
                bias[block] = hidden_bias(query_at, key_at, starts_ref)

        def one(block, extra):
            low, high = block * rows, (block + 1 + extra) * rows
            q = q_ref[0, low : low + rows, :]
            edge = dot_t(q, k_ref[0, low:high, :]) + bias[block, :, : high - low]
            top = jnp.max(edge, axis=1, keepdims=True)
            if block:
                before = dot_t(q, k_ref[0, :low, :])
                top = jnp.maximum(top, jnp.max(before, axis=1, keepdims=True))
            shift = top * factor
            weight = jnp.exp2(edge * factor - shift)
            total = jnp.sum(weight, axis=1, keepdims=True)
            out = dot(weight.astype(BF16), v_ref[0, low:high, :])
            if block:
                weight = jnp.exp2(before * factor - shift)
                total = total + jnp.sum(weight, axis=1, keepdims=True)
                out = out + dot(weight.astype(BF16), v_ref[0, :low, :])
            o_ref[0, low : low + rows, :] = (out / total).astype(BF16)

        for block in range(count):
            if block == count - 1:
                one(block, 0)
                continue
            wide = crosses(starts_ref, (block + 1) * rows, rows)
            pl.when(wide)(functools.partial(one, block, 1))
            pl.when(jnp.logical_not(wide))(functools.partial(one, block, 0))

    spec = pl.BlockSpec((1, length, HDIM), lambda h: (h, 0, 0))
    return call(
        kernel,
        jax.ShapeDtypeStruct(query.shape, BF16),
        [smem(), spec, spec, spec],
        spec,
        [pltpu.VMEM((count, rows, 2 * rows), F32)],
        4 * heads * length * length * HDIM * 4,
        16 * heads * length * HDIM,
        "attend",
        grid=(heads,),
    )(starts, query, key, value)


def attend_back(starts, place, query, key, value, near, far, cosine, sine, rows, first, heads):
    length = query.shape[1]
    count = length // rows
    scale = 1.0 / math.sqrt(HDIM)
    factor = LOG2E * scale

    def kernel(
        starts_ref, place_ref, q_ref, k_ref, v_ref, near_ref, far_ref, cos_ref, sin_ref, dq_ref, dk_ref, dv_ref,
        bias, key_sum, value_sum, key_turned,
    ):
        @pl.when(pl.program_id(0) == 0)
        def _():
            for block in range(count):
                shape = (2 * rows, rows)
                query_at = block * rows + lax.broadcasted_iota(jnp.int32, shape, 1)
                key_at = block * rows + lax.broadcasted_iota(jnp.int32, shape, 0)
                bias[block] = hidden_bias(query_at, key_at, starts_ref)

        key_sum[...] = jnp.zeros_like(key_sum)
        value_sum[...] = jnp.zeros_like(value_sum)
        key_turned[...] = k_ref[0].astype(F32).T.astype(BF16)

        def one(block, extra):
            low, high = block * rows, (block + 1 + extra) * rows
            q = q_ref[0, low : low + rows, :]
            relative = place_ref[0] ^ block
            at = pl.multiple_of((relative % 2) * rows, rows)
            g = jnp.where(relative < 2, near_ref[0, pl.ds(at, rows), :], far_ref[0, pl.ds(at, rows), :])
            raw = dot_t(k_ref[0, low:high, :], q) + bias[block, : high - low, :]
            if block:
                raw = jnp.concatenate([dot_t(k_ref[0, :low, :], q), raw], axis=0)
            top = jnp.max(raw, axis=0, keepdims=True)
            weight = jnp.exp2(raw * factor - top * factor)
            probs = weight * (1.0 / jnp.sum(weight, axis=0, keepdims=True))
            grad_probs = dot_t(v_ref[0, :high, :], g)
            inner = jnp.sum(grad_probs * probs, axis=0, keepdims=True)
            grad_scores = (probs * (grad_probs - inner)).astype(BF16)
            value_sum[:high, :] += dot(probs.astype(BF16), g)
            key_sum[:high, :] += dot(grad_scores, q)
            turned = dot(key_turned[:, :high], grad_scores)
            back = turned.T * scale
            dq_ref[0, low : low + rows, :] = turn(
                back, cos_ref[low : low + rows, :], -sin_ref[low : low + rows, :]
            ).astype(BF16)

        for block in range(count):
            if block == count - 1:
                one(block, 0)
                continue
            wide = crosses(starts_ref, (block + 1) * rows, rows)
            pl.when(wide)(functools.partial(one, block, 1))
            pl.when(jnp.logical_not(wide))(functools.partial(one, block, 0))
        dk_ref[0] = turn(key_sum[...] * scale, cos_ref[...], -sin_ref[...]).astype(BF16)
        dv_ref[0] = value_sum[...].astype(BF16)

    spec = pl.BlockSpec((1, length, HDIM), lambda h: (first + h, 0, 0))
    half = pl.BlockSpec((1, length // 2, HDIM), lambda h: (first + h, 0, 0))
    out = pl.BlockSpec((1, length, HDIM), lambda h: (h, 0, 0))
    table = pl.BlockSpec((length, HDIM), lambda h: (0, 0))
    return call(
        kernel,
        [jax.ShapeDtypeStruct((heads, length, HDIM), BF16)] * 3,
        [smem(), smem(), spec, spec, spec, half, half, table, table],
        [out] * 3,
        [
            pltpu.VMEM((count, 2 * rows, rows), F32),
            pltpu.VMEM((length, HDIM), F32),
            pltpu.VMEM((length, HDIM), F32),
            pltpu.VMEM((HDIM, length), BF16),
        ],
        10 * heads * length * length * HDIM * 4,
        32 * heads * length * HDIM,
        "attend_back",
        grid=(heads,),
    )(starts, place[None], query, key, value, near, far, cosine, sine)


def rows_by_heads(refs, start, rows):
    return jnp.concatenate(
        [ref[head, pl.ds(start, rows), :] for ref in refs for head in range(ref.shape[0])], axis=1
    )


def close_attention(mixed, place, weight, a_out, wanted, rows):
    size, width = weight.shape
    rank = a_out.shape[0]

    def kernel(place_ref, m_ref, w_ref, a_ref, *outs):
        for block, out in zip(wanted, outs):
            start = pl.multiple_of((place_ref[0] ^ block) * rows, rows)
            here = rows_by_heads([m_ref], start, rows)
            out[:, :width] = dot(here, w_ref[...]).astype(BF16)
            narrow = dot_t(here, a_ref[...]).astype(BF16)
            out[:, width:] = jnp.concatenate(
                [narrow, jnp.zeros((rows, EXTRA - rank), BF16)], axis=1
            )

    return call(
        kernel,
        [jax.ShapeDtypeStruct((rows, width + EXTRA), BF16)] * len(wanted),
        [smem()] + [vmem()] * 3,
        [vmem()] * len(wanted),
        [],
        2 * rows * len(wanted) * size * width,
        2 * size * width + 2 * rows * len(wanted) * (width + size),
        "close_attention",
    )(place[None], mixed, weight, a_out)


def open_attention(blocks, wanted, place, mixed, weight, a_out, b_out):
    rows, width_ext = blocks[0].shape
    size, width = weight.shape
    rank = a_out.shape[0]
    count = len(blocks)
    heads = size // HDIM

    def kernel(place_ref, *refs):
        g_refs, refs = refs[:count], refs[count:]
        m_ref, w_ref, a_ref, b_ref, out, sum_ref = refs
        total = jnp.zeros((rank, size), F32)
        for block in range(count):
            start = pl.multiple_of((place_ref[0] ^ wanted[block]) * rows, rows)
            grad = g_refs[block][:, :width]
            narrow = dot_t(grad, b_ref[...]).astype(BF16)
            back = dot_t(grad, w_ref[...]) + dot(narrow, a_ref[...])
            for head in range(heads):
                part = back[:, head * HDIM : (head + 1) * HDIM]
                out[head, block * rows : (block + 1) * rows, :] = part.astype(BF16)
            total = total + t_dot(narrow, rows_by_heads([m_ref], start, rows))
        sum_ref[...] = total

    return call(
        kernel,
        [
            jax.ShapeDtypeStruct((heads, rows * count, HDIM), BF16),
            jax.ShapeDtypeStruct((rank, size), F32),
        ],
        [smem()] + [vmem()] * (count + 4),
        [vmem()] * 2,
        [],
        2 * rows * count * size * width,
        2 * size * width + 2 * rows * count * (width + 2 * size),
        "open_attention",
    )(place[None], *blocks, mixed, weight, a_out, b_out)


def feed_forward(blocks, grads, offsets, pieces, down, a_mlp, b_down, a_hidden, b_hidden):
    rows, width = blocks[0].shape
    count = len(blocks)
    size = down.shape[0]
    rank = b_down.shape[0]
    n = len(pieces)

    def kernel(offsets_ref, *refs):
        x_refs, refs = refs[:count], refs[count:]
        g_refs, refs = refs[:count], refs[count:]
        piece_refs, refs = refs[:n], refs[n:]
        down_hbm, am_ref, bd_ref, ah_ref, bh_ref = refs[:5]
        refs = refs[5:]
        feed_refs, refs = refs[:count], refs[count:]
        back_refs, refs = refs[:count], refs[count:]
        a_sum, b_sum, whole, down_ref, sems, down_sem = refs
        copies = load_pieces(offsets_ref, piece_refs, whole, sems)
        down_copy = pltpu.make_async_copy(down_hbm, down_ref, down_sem)
        down_copy.start()
        for copy in copies:
            copy.wait()
        pad = jnp.zeros((rows, EXTRA - rank), BF16)
        for block in range(count):
            x = x_refs[block][...]
            narrow = dot_t(x, am_ref[...]).astype(BF16)
            gate = dot(x, whole[0]) + dot(narrow[:, :rank], bh_ref[0])
            up = dot(x, whole[1]) + dot(narrow[:, rank:], bh_ref[1])
            sigmoid = 1.0 / (1.0 + jnp.exp(-gate))
            silu = gate * sigmoid
            hidden = (silu * up).astype(BF16)
            if block == 0:
                down_copy.wait()
            feed_refs[block][:, :width] = dot(hidden, down_ref[...]).astype(BF16)
            feed_refs[block][:, width:] = jnp.concatenate(
                [dot_t(hidden, ah_ref[...]).astype(BF16), pad], axis=1
            )
            grad = g_refs[block][...]
            grad_narrow = dot_t(grad, bd_ref[...]).astype(BF16)
            grad_hidden = dot_t(grad, down_ref[...]) + dot(grad_narrow, ah_ref[...])
            grad_hidden = grad_hidden.astype(BF16).astype(F32)
            grad_up = (grad_hidden * silu).astype(BF16)
            grad_gate = (grad_hidden * up * (sigmoid * (1.0 + gate * (1.0 - sigmoid)))).astype(BF16)
            back = dot_t(grad_gate, whole[0]) + dot_t(grad_up, whole[1])
            back_refs[block][:, :width] = back.astype(BF16)
            back_refs[block][:, width:] = jnp.concatenate(
                [
                    dot_t(grad_gate, bh_ref[0]).astype(BF16),
                    dot_t(grad_up, bh_ref[1]).astype(BF16),
                    pad[:, rank:],
                ],
                axis=1,
            )
            terms = (
                t_dot(grad_narrow, hidden),
                t_dot(narrow[:, :rank], grad_gate),
                t_dot(narrow[:, rank:], grad_up),
            )
            if block == 0:
                a_sum[...] = terms[0]
                b_sum[0] = terms[1]
                b_sum[1] = terms[2]
            else:
                a_sum[...] += terms[0]
                b_sum[0] += terms[1]
                b_sum[1] += terms[2]

    out = jax.ShapeDtypeStruct((rows, width + EXTRA), BF16)
    return call(
        kernel,
        [out] * (2 * count)
        + [jax.ShapeDtypeStruct((rank, size), F32), jax.ShapeDtypeStruct((2, rank, size), F32)],
        [smem()] + [vmem()] * (2 * count) + [anywhere()] * (n + 1) + [vmem()] * 4,
        [vmem()] * (2 * count + 2),
        [
            pltpu.VMEM((2, width, size), BF16),
            pltpu.VMEM((size, width), BF16),
            pltpu.SemaphoreType.DMA((n,)),
            pltpu.SemaphoreType.DMA,
        ],
        12 * rows * count * width * size,
        6 * width * size + 8 * rows * count * width,
        "feed_forward",
    )(offsets, *blocks, *grads, *pieces, down, a_mlp, b_down, a_hidden, b_hidden)


def thin_back(grads, place, narrow_first, b_first, rows):
    maps, rank, size = b_first.shape
    parts_each = len(grads) // maps
    count = narrow_first.shape[0] // rows

    def kernel(place_ref, *refs):
        g_refs, refs = refs[: len(grads)], refs[len(grads) :]
        narrow_ref, b_ref, thin_ref, sum_ref = refs
        for block in range(count):
            start = pl.multiple_of((place_ref[0] ^ block) * rows, rows)
            narrow = narrow_ref[block * rows : (block + 1) * rows, :]
            thin = []
            for number in range(maps):
                part = rows_by_heads(
                    g_refs[number * parts_each : (number + 1) * parts_each], start, rows
                )
                thin.append(dot_t(part, b_ref[number]))
                term = t_dot(narrow[:, number * rank : (number + 1) * rank], part)
                if block == 0:
                    sum_ref[number] = term
                else:
                    sum_ref[number] += term
            thin_ref[block * rows : (block + 1) * rows, :] = jnp.concatenate(thin, axis=1).astype(BF16)

    return call(
        kernel,
        [
            jax.ShapeDtypeStruct((rows * count, maps * rank), BF16),
            jax.ShapeDtypeStruct((maps, rank, size), F32),
        ],
        [smem()] + [vmem()] * (len(grads) + 2),
        [vmem()] * 2,
        [],
        4 * rows * count * maps * size * 128,
        4 * rows * count * maps * size,
        "thin_back",
    )(place[None], *grads, narrow_first, b_first)


def project_back(grads, place, offsets, pieces, wanted, rows):
    maps, _, size = pieces[0].shape
    width = 4 * pieces[0].shape[1]
    n = len(pieces)
    count = len(wanted)
    parts_each = len(grads) // maps

    def kernel(place_ref, offsets_ref, *refs):
        g_refs, refs = refs[: len(grads)], refs[len(grads) :]
        piece_refs, refs = refs[:n], refs[n:]
        back_refs, (whole, sems) = refs[:count], refs[count:]
        copies = load_pieces(offsets_ref, piece_refs, whole, sems)
        for copy in copies:
            copy.wait()
        for index, block in enumerate(wanted):
            start = pl.multiple_of((place_ref[0] ^ block) * rows, rows)
            back = None
            for number in range(maps):
                part = rows_by_heads(
                    g_refs[number * parts_each : (number + 1) * parts_each], start, rows
                )
                term = dot_t(part, whole[number])
                back = term if back is None else back + term
            back_refs[index][...] = back.astype(BF16)

    return call(
        kernel,
        [jax.ShapeDtypeStruct((rows, width), BF16)] * count,
        [smem(), smem()] + [vmem()] * len(grads) + [anywhere()] * n,
        [vmem()] * count,
        [pltpu.VMEM((maps, width, size), BF16), pltpu.SemaphoreType.DMA((n,))],
        2 * rows * count * width * maps * size,
        2 * (rows * count * (width + maps * size) + maps * width * size),
        "project_back",
    )(place[None], offsets, *grads, *pieces)


def shards(
    tokens,
    cotangent,
    sequence_adapter_index,
    image_span_start,
    attention_norm_gain,
    feedforward_norm_gain,
    query_key_value_weight,
    attention_output_weight,
    gate_up_projection_weight,
    down_projection_weight,
    adapter_model_input_maps,
    adapter_model_output_maps,
    adapter_hidden_input_map,
    adapter_hidden_output_maps,
):
    rows = tokens.shape[1]
    width = tokens.shape[2]
    rank = adapter_model_input_maps.shape[2]
    group = lax.axis_size("shard")
    place = lax.axis_index("shard").astype(jnp.int32)
    rep_place = lax.axis_index("rep").astype(jnp.int32)
    pick = sequence_adapter_index[0]
    starts = image_span_start[0]
    head_cols = width // group
    ff_cols = down_projection_weight.shape[0]

    gain_one = attention_norm_gain.astype(F32)
    gain_two = feedforward_norm_gain.astype(F32)
    residual_in = tokens[0].astype(F32)
    grad_out = cotangent[0].astype(F32)

    def own_columns(values, size):
        return lax.dynamic_slice_in_dim(values, place * size, size, values.ndim - 1)

    first_one = [hop(piece, "shard", j) for j, piece in zip(
        (2, 3), leaving(query_key_value_weight, head_cols, place, rep_place))]
    normed = norm_rows(residual_in, gain_one).astype(BF16)
    grad_feed = (BRANCH * grad_out).astype(BF16)
    normed_near = core(normed)
    first_near = near_columns(query_key_value_weight, head_cols, place)
    front_chip, front_part = chip_picked(
        jnp.concatenate([adapter_model_input_maps[0:3], adapter_model_output_maps[0:3]]), pick, place
    )
    front_far = across(after(front_part, first_one))
    first_two = [hop(first_one[0], "rep", 2), hop(first_one[1], "rep", 1)]
    normed_far = across(after(normed, front_far, first_two))
    front = whole_picked(front_chip, front_far, place)
    a_first = front[:3].reshape(3 * rank, width)
    b_first = own_columns(front[3:], head_cols)
    first_three = [
        [hop(first_one[0], "rep", 1), hop(first_two[0], "rep", 1)],
        [hop(first_one[1], "rep", 2), hop(first_two[1], "rep", 2)],
    ]
    half = HDIM // 2
    frequency = jnp.exp(jnp.arange(half, dtype=F32) * (-2.0 / HDIM) * math.log(THETA))
    angle = jnp.arange(rows * group, dtype=jnp.int32).astype(F32)[:, None] * frequency[None, :]
    cosine = jnp.concatenate([jnp.cos(angle), jnp.cos(angle)], axis=1)
    sine = jnp.concatenate([jnp.sin(angle), jnp.sin(angle)], axis=1)
    mlp_leaving = leaving(gate_up_projection_weight, ff_cols, place, rep_place)
    normed_far, front, mlp_leaving, first_three, cosine, sine = lax.optimization_barrier(
        (normed_far, front, mlp_leaving, first_three, cosine, sine)
    )
    first_blocks = (normed, normed_near, normed_far, core(normed_far))
    first_offsets, first_pieces = finish(
        query_key_value_weight, head_cols, first_one, first_two, first_three, place, rep_place,
        first_near,
    )

    mlp_one = [hop(piece, "shard", j) for j, piece in zip((2, 3), mlp_leaving)]
    rest_chip, rest_part = chip_picked(
        jnp.concatenate([adapter_model_input_maps[3:6], adapter_model_output_maps[3:5]]), pick, place
    )
    wide_chip, wide_part = chip_picked(
        jnp.concatenate([adapter_hidden_input_map[None], adapter_hidden_output_maps]), pick, place
    )
    rest_far = across(after(rest_part, normed_far))
    wide_far = across(after(wide_part, normed_far))
    query, key, value, narrow_first = project(
        first_blocks, place, first_offsets, first_pieces, a_first, b_first, cosine, sine
    )
    query, mlp_one[0], rest_far = lax.optimization_barrier((query, mlp_one[0], rest_far))
    mlp_two = [hop(mlp_one[0], "rep", 2), None]
    rest = whole_picked(rest_chip, rest_far, place)
    mixed = attend(starts, query, key, value, rows)
    mixed, mlp_one[1], mlp_two[0], wide_far, rest = lax.optimization_barrier(
        (mixed, mlp_one[1], mlp_two[0], wide_far, rest)
    )
    a_out = own_columns(rest[0], head_cols)
    a_mlp = rest[1:3].reshape(2 * rank, width)
    b_out, b_down = rest[3], rest[4]
    mlp_two[1] = hop(mlp_one[1], "rep", 1)
    feed_far_in = across(after(grad_feed, mixed))
    feed_near_in = core(grad_feed)
    hidden_one = whole_picked(wide_chip, wide_far, place)
    hidden_cols = own_columns(hidden_one, ff_cols)
    a_hidden, b_hidden = hidden_cols[0], hidden_cols[1:]
    mlp_near = near_columns(gate_up_projection_weight, ff_cols, place)

    far_out = close_attention(mixed, place, attention_output_weight, a_out, (2, 3), rows)
    far_sum = (far_out[0].astype(F32) + core(far_out[1]).astype(F32)).astype(BF16)
    far_sum, mixed_here, mlp_two[1] = lax.optimization_barrier((far_sum, mixed, mlp_two[1]))
    branch_far = across(far_sum)
    mlp_three = [
        [hop(mlp_one[0], "rep", 1), hop(mlp_two[0], "rep", 1)],
        [hop(mlp_one[1], "rep", 2), hop(mlp_two[1], "rep", 2)],
    ]
    near_out = close_attention(mixed_here, place, attention_output_weight, a_out, (0, 1), rows)
    branch_own = near_out[0].astype(F32) + core(near_out[1]).astype(F32) + branch_far.astype(F32)
    narrow_out = branch_own[:, width : width + rank].astype(BF16)
    branch = branch_own[:, :width] + dot(narrow_out, b_out)
    middle = residual_in + BRANCH * branch
    normed_second = norm_rows(middle, gain_two).astype(BF16)
    second_far = across(normed_second)
    second_near = core(normed_second)
    second_near, mlp_three, feed_near_in, feed_far_in, hidden_cols = lax.optimization_barrier(
        (second_near, mlp_three, feed_near_in, feed_far_in, hidden_cols)
    )
    a_hidden, b_hidden = hidden_cols[0], hidden_cols[1:]
    mlp_offsets, mlp_pieces = finish(
        gate_up_projection_weight, ff_cols, mlp_one, mlp_two, mlp_three, place, rep_place, mlp_near
    )
    feed_far_near = core(feed_far_in)
    *parts, a_near, b_near = feed_forward(
        (normed_second, second_near), (grad_feed, feed_near_in), mlp_offsets, mlp_pieces,
        down_projection_weight, a_mlp, b_down, a_hidden, b_hidden,
    )
    feed_near, back_near = parts[:2], parts[2:]
    second_far, feed_far_near, back_near = lax.optimization_barrier(
        (second_far, feed_far_near, back_near)
    )
    second_blocks = (normed_second, second_near, second_far, core(second_far))
    feed_blocks = (grad_feed, feed_near_in, feed_far_in, feed_far_near)
    back_here = core(back_near[1])
    *parts, a_far, b_far = feed_forward(
        second_blocks[2:], feed_blocks[2:], mlp_offsets, mlp_pieces, down_projection_weight,
        a_mlp, b_down, a_hidden, b_hidden,
    )
    feed_far, back_far = parts[:2], parts[2:]
    back_sum = (back_far[0].astype(F32) + core(back_far[1]).astype(F32)).astype(BF16)
    back_from_far = across(back_sum)
    feed_near, feed_far, back_sum = lax.optimization_barrier((feed_near, feed_far, back_sum))
    feed_here = feed_near[0].astype(F32) + core(feed_near[1]).astype(F32)
    feed_sum = (feed_far[0].astype(F32) + core(feed_far[1]).astype(F32)).astype(BF16)
    back_from_far, feed_here, feed_sum = lax.optimization_barrier((back_from_far, feed_here, feed_sum))
    second_own = back_near[0].astype(F32) + back_here.astype(F32) + back_from_far.astype(F32)
    grad_narrow_mlp = second_own[:, width : width + 2 * rank].astype(BF16)
    grad_normed_second = second_own[:, :width] + dot(grad_narrow_mlp, a_mlp)
    grad_middle = grad_out + norm_back(middle, gain_two, grad_normed_second)
    grad_branch = (BRANCH * grad_middle).astype(BF16)
    branch_rows = pad_columns([grad_branch, narrow_out, grad_narrow_mlp], width + EXTRA)
    branch_far_in = across(branch_rows)
    branch_near_in = core(branch_rows)

    mixed_near, grad_a_near = open_attention(
        (branch_rows, branch_near_in), (0, 1), place, mixed, attention_output_weight, a_out, b_out
    )
    branch_far_in, mixed_near = lax.optimization_barrier((branch_far_in, mixed_near))
    feed_from_far = across(after(feed_sum, branch_far_in))
    branch_blocks = (branch_rows, branch_near_in, branch_far_in, core(branch_far_in))
    mixed_far, grad_a_far = open_attention(
        branch_blocks[2:], (2, 3), place, mixed, attention_output_weight, a_out, b_out
    )

    def columns_product(thin, wide):
        total = sum(t_dot(left, right) for left, right in zip(thin, wide))
        return own_columns(total, head_cols)

    def attend_part(first, heads, starts):
        return attend_back(
            starts, place, query, key, value, mixed_near, mixed_far, cosine, sine, rows, first, heads
        )

    heads = query.shape[0]
    third = heads // 3
    part_one = attend_part(0, third, starts)
    part_one, feed_from_far, starts_two = lax.optimization_barrier((part_one, feed_from_far, starts))

    feed_own = feed_here + feed_from_far.astype(F32)
    narrow_down = feed_own[:, width : width + rank].astype(BF16)
    feed = feed_own[:, :width] + dot(narrow_down, b_down)
    output = (middle + BRANCH * feed).astype(BF16)
    down_far = across(narrow_down)
    down_near = core(narrow_down)
    wide_branch = [block[:, :width] for block in branch_blocks]
    thin_out = [block[:, width : width + rank] for block in branch_blocks]
    thin_mlp = [block[:, width + rank : width + 3 * rank] for block in branch_blocks]
    early_ready = jnp.concatenate(
        [
            grad_a_near + grad_a_far,
            columns_product(thin_mlp, second_blocks),
            columns_product(thin_out, wide_branch),
        ]
    )
    output, down_far, down_near, early_ready, starts_two = lax.optimization_barrier(
        (output, down_far, down_near, early_ready, starts_two)
    )
    narrow_down_blocks = (narrow_down, down_near, down_far, core(down_far))
    mark = jnp.full((rank, head_cols), pick.astype(F32))
    early = jnp.concatenate(
        [
            early_ready,
            columns_product(narrow_down_blocks, feed_blocks),
            (a_near + a_far).reshape(-1, head_cols),
            (b_near + b_far).reshape(-1, head_cols),
            mark,
        ]
    ).astype(BF16)
    early_all = start_reps(early, rep_place)
    early_one = reps_step(early_all, rep_place, 1)
    early_two = reps_step(early_one, rep_place, 2)
    early_two, starts_two = lax.optimization_barrier((early_two, starts_two))
    early_rest = reps_rest(early_two, rep_place, 4)
    part_two = attend_part(third, third, starts_two)
    early_rest, part_two, starts_three = lax.optimization_barrier((early_rest, part_two, starts_two))
    picks = early_rest[:, -1, :1].astype(F32)
    adapters = adapter_model_input_maps.shape[1] * group
    chosen = (picks == jnp.arange(adapters, dtype=jnp.int32).astype(F32)[None, :]).astype(F32)
    early_sent = send_sums(early_rest[:, :-rank], chosen, place)
    part_three = attend_part(2 * third, heads - 2 * third, starts_three)
    early_sent, part_three = lax.optimization_barrier((early_sent, part_three))
    early_got = arrange_sums(early_sent, place)
    first_grads = [part[number] for number in range(3) for part in (part_one, part_two, part_three)]

    thin, grad_b_first = thin_back(first_grads, place, narrow_first, b_first, rows)
    first_grads, thin = lax.optimization_barrier((first_grads, thin))
    thin_one = add_relative(thin, core(thin), 1)
    back_rows_far = project_back(first_grads, place, first_offsets, first_pieces, (2, 3), rows)
    sum_far = (back_rows_far[0].astype(F32) + core(back_rows_far[1]).astype(F32)).astype(BF16)
    thin_one, sum_far, grads_here = lax.optimization_barrier((thin_one, sum_far, first_grads))
    thin_far = across(thin_one)
    back_far_in = across(sum_far)
    back_rows_near = project_back(grads_here, place, first_offsets, first_pieces, (0, 1), rows)
    thin_far, back_rows_near = lax.optimization_barrier((thin_far, back_rows_near))
    grad_narrow_first = add_relative(thin_one, thin_far, 2)
    back_here = back_rows_near[0].astype(F32) + core(back_rows_near[1]).astype(F32)

    late = jnp.concatenate(
        [
            columns_product(rows_of(grad_narrow_first, group), first_blocks),
            grad_b_first.reshape(3 * rank, head_cols),
        ]
    ).astype(BF16)
    late_all = reps_rest(start_reps(late, rep_place), rep_place, 1)
    late_sent = send_sums(late_all, chosen, place)
    late_sent, back_far_in = lax.optimization_barrier((late_sent, back_far_in))
    late_got = arrange_sums(late_sent, place)
    grad_normed = back_here + back_far_in.astype(F32) + dot(grad_narrow_first[:rows], a_first)
    input_grad = grad_middle + norm_back(residual_in, gain_one, grad_normed)

    def whole_maps(got, low, high, n):
        group_size, per = got.shape[:2]
        part = got[:, :, low:high].reshape(group_size, per, -1, rank, n)
        part = jnp.concatenate([part[i] for i in range(group_size)], axis=-1)
        return part.transpose(1, 0, 2, 3).astype(F32)

    split = 5 * rank
    hidden_rows = rank * ff_cols // head_cols
    grad_a_model = jnp.concatenate(
        [whole_maps(late_got, 0, 3 * rank, head_cols), whole_maps(early_got, 0, 3 * rank, head_cols)]
    )
    grad_b_model = jnp.concatenate(
        [
            whole_maps(late_got, 3 * rank, 6 * rank, head_cols),
            whole_maps(early_got, 3 * rank, split, head_cols),
        ]
    )
    grad_hidden_maps = whole_maps(early_got, split, split + 3 * hidden_rows, ff_cols)
    return (
        output[None], input_grad[None], grad_a_model, grad_b_model, grad_hidden_maps[0],
        grad_hidden_maps[1:3],
    )


def solution(mesh):
    in_specs = (
        P("rep", "shard", None),
        P("rep", "shard", None),
        P("rep"),
        P("rep", None),
        P(),
        P(),
        P(None, "shard", None),
        P("shard", None),
        P(None, "shard", None),
        P("shard", None),
        P(None, "shard", None, None),
        P(None, "shard", None, None),
        P("shard", None, None),
        P(None, "shard", None, None),
    )
    out_specs = (
        P("rep", "shard", None),
        P("rep", "shard", None),
        P(None, "shard", None, None),
        P(None, "shard", None, None),
        P("shard", None, None),
        P(None, "shard", None, None),
    )
    return jax.shard_map(shards, mesh=mesh, in_specs=in_specs, out_specs=out_specs, check_vma=False)
```

```python
import functools
import math

import jax
import jax.numpy as jnp
from jax import lax
from jax.experimental import pallas as pl
from jax.experimental.pallas import tpu as pltpu
from jax.sharding import PartitionSpec as P

HDIM = 64
SPAN = 256
EPS = 1e-05
THETA = 10000.0
BRANCH = 1.4 / math.sqrt(40.0)
EXTRA = 128
F32 = jnp.float32
BF16 = jnp.bfloat16
LOG2E = math.log2(math.e)


def hop(values, axis, bit):
    size = lax.axis_size(axis)
    return lax.ppermute(values, axis, [(i, i ^ bit) for i in range(size)])


def core(values):
    return hop(values, "shard", 1)


def across(values):
    return hop(values, "shard", 2)


def rows_of(values, count):
    size = values.shape[0] // count
    return tuple(values[i * size : (i + 1) * size] for i in range(count))


def norm_rows(values, gain):
    return values * lax.rsqrt(jnp.mean(values * values, axis=-1, keepdims=True) + EPS) * gain


def norm_back(values, gain, grad):
    width = values.shape[-1]
    scale = lax.rsqrt(jnp.mean(values * values, axis=-1, keepdims=True) + EPS)
    moved = grad * gain
    inner = jnp.sum(values * moved, axis=-1, keepdims=True) / width
    return scale * moved - values * (scale * scale * scale) * inner


def dot(left, right):
    return jnp.dot(left, right, preferred_element_type=F32)


def dot_t(left, right):
    return lax.dot_general(left, right, (((1,), (1,)), ((), ())), preferred_element_type=F32)


def t_dot(left, right):
    return lax.dot_general(left, right, (((0,), (0,)), ((), ())), preferred_element_type=F32)


def pad_columns(pieces, width):
    used = sum(piece.shape[1] for piece in pieces)
    rest = jnp.zeros((pieces[0].shape[0], width - used), pieces[0].dtype)
    return jnp.concatenate(list(pieces) + [rest], axis=1)


def reps_bits():
    bits = []
    bit = 2
    while bit < lax.axis_size("rep"):
        bits.append(bit)
        bit *= 2
    return bits + [1]


def both(held, arrived, rep_place, bit):
    low = jnp.concatenate([held, arrived])
    high = jnp.concatenate([arrived, held])
    return jnp.where((rep_place // bit) % 2 == 0, low, high)


def send_sums(everyone, chosen, place):
    group = lax.axis_size("shard")
    per = chosen.shape[1] // group
    sent = []
    for j in range(group):
        marks = lax.dynamic_slice_in_dim(chosen, (place ^ j) * per, per, 1)
        sums = jnp.sum(marks[:, :, None, None] * everyone[:, None].astype(F32), axis=0).astype(BF16)
        sent.append(hop(sums, "shard", j) if j else sums)
    return sent


def chip_picked(bank, pick, place):
    per = bank.shape[1]
    rank = bank.shape[2]
    owner = pick // per
    mine = lax.dynamic_index_in_dim(bank, pick % per, 1, keepdims=False)
    mine = jnp.where(owner == place, mine, jnp.zeros_like(mine))
    chip = mine + core(mine)
    return chip, lax.dynamic_slice_in_dim(chip, (place % 2) * (rank // 2), rank // 2, 1)


def whole_picked(chip, far, place):
    other = core(far)
    low = jnp.where(place % 2 == 0, far, other)
    high = jnp.where(place % 2 == 0, other, far)
    return chip + jnp.concatenate([low, high], axis=1)


def after(value, *others):
    return lax.optimization_barrier((value, others))[0]


def side(weight, row, count, owner, size):
    return lax.dynamic_slice(weight, (0, row, owner * size), (weight.shape[0], count, size))


def sides(weight, row, count, place, size, wanted, name):
    maps, _, columns = weight.shape

    def kernel(where_ref, w_ref, *refs):
        outs, (held, sem) = refs[:-2], refs[-2:]
        start = pl.multiple_of(where_ref[1], 16)
        copy = pltpu.make_async_copy(w_ref.at[:, pl.ds(start, count), :], held, sem)
        copy.start()
        copy.wait()

        def write(out, owner):
            out[...] = jnp.concatenate(
                [held[i, :, owner * size : (owner + 1) * size] for i in range(maps)], axis=1
            )

        for j, out in zip(wanted, outs):
            for owner in range(columns // size):
                pl.when((where_ref[0] ^ j) == owner)(functools.partial(write, out, owner))

    return call(
        kernel,
        [jax.ShapeDtypeStruct((count, maps * size), BF16)] * len(wanted),
        [smem(), anywhere()],
        [vmem()] * len(wanted),
        [pltpu.VMEM((maps, count, columns), BF16), pltpu.SemaphoreType.DMA],
        0,
        2 * maps * count * (columns + size * len(wanted)),
        name,
        limit=58,
    )(jnp.stack([place, jnp.asarray(row, jnp.int32)]), weight)


def arrange(rows, own, near, ways, place, rep_place):
    quarter = rows // 4
    part = rep_place % 4
    pieces = [(place * rows, own), ((place ^ 1) * rows, near)]
    for j, one, two, parts in zip((2, 3), (2, 1), (1, 2), ways):
        for bits, piece in zip((0, one, two, one ^ two), parts):
            pieces.append(((place ^ j) * rows + (part ^ bits) * quarter, piece))
    offsets = jnp.stack([row.astype(jnp.int32) for row, _ in pieces])
    return offsets, [piece for _, piece in pieces]


def fence(*values):
    return lax.optimization_barrier(values)


def load_pieces(offsets, pieces, whole, sems):
    copies = []
    for number, piece in enumerate(pieces):
        start = pl.multiple_of(offsets[number], 16)
        here = pl.ds(start, piece.shape[-2])
        target = whole.at[here, :] if len(piece.shape) == 2 else whole.at[:, here, :]
        copy = pltpu.make_async_copy(piece, target, sems.at[number])
        copy.start()
        copies.append(copy)
    return copies


def vmem():
    return pl.BlockSpec(memory_space=pltpu.VMEM)


def smem():
    return pl.BlockSpec(memory_space=pltpu.SMEM)


def anywhere():
    return pl.BlockSpec(memory_space=pl.ANY)


def call(kernel, outs, in_specs, out_specs, scratch, flops, moved, name, limit=56, **more):
    return pl.pallas_call(
        kernel,
        out_shape=outs,
        in_specs=in_specs,
        out_specs=out_specs,
        scratch_shapes=scratch,
        compiler_params=pltpu.CompilerParams(vmem_limit_bytes=limit << 20),
        cost_estimate=pl.CostEstimate(flops=flops, bytes_accessed=moved, transcendentals=0),
        name=name,
        **more,
    )


def turn(values, cosine, sine):
    half = HDIM // 2
    turned = jnp.concatenate([-values[:, half:], values[:, :half]], axis=1)
    return values * cosine + turned * sine


def project(blocks, place, offsets, pieces, a_first, b_first, cosine, sine):
    rows, width = blocks[0].shape
    count = len(blocks)
    size = pieces[0].shape[1]
    heads = size // (3 * HDIM)
    thin = a_first.shape[0]
    n = len(pieces)

    def kernel(place_ref, offsets_ref, *refs):
        x_refs, refs = refs[:count], refs[count:]
        piece_refs, refs = refs[:n], refs[n:]
        a_ref, b_ref, cos_ref, sin_ref, q_ref, k_ref, v_ref, narrow_ref, whole, sems = refs
        copies = load_pieces(offsets_ref, piece_refs, whole, sems)
        starts = [pl.multiple_of((place_ref[0] ^ block) * rows, rows) for block in range(count)]
        for block in range(count):
            narrow_ref[:, pl.ds(starts[block], rows)] = dot_t(a_ref[...], x_refs[block][...]).astype(BF16)
        for copy in copies:
            copy.wait()
        for block in range(count):
            start = starts[block]
            narrow = narrow_ref[:, pl.ds(start, rows)]
            pre = dot(x_refs[block][...], whole[...]) + t_dot(narrow, b_ref[...])
            cosine_here = cos_ref[pl.ds(start, rows), :]
            sine_here = sin_ref[pl.ds(start, rows), :]
            for number, out in enumerate((q_ref, k_ref, v_ref)):
                for head in range(heads):
                    at = (number * heads + head) * HDIM
                    part = pre[:, at : at + HDIM]
                    if number < 2:
                        part = turn(part, cosine_here, sine_here)
                    out[head, pl.ds(start, rows), :] = part.astype(BF16)

    by_heads = jax.ShapeDtypeStruct((heads, rows * count, HDIM), BF16)
    return call(
        kernel,
        [by_heads] * 3 + [jax.ShapeDtypeStruct((thin, rows * count), BF16)],
        [smem(), smem()] + [vmem()] * count + [anywhere()] * n + [vmem()] * 4,
        [vmem()] * 4,
        [pltpu.VMEM((width, size), BF16), pltpu.SemaphoreType.DMA((n,))],
        2 * rows * count * width * size,
        2 * (rows * count * width + width * size + 2 * rows * count * size),
        "project",
        limit=44,
    )(place[None], offsets, *blocks, *pieces, a_first, b_first, cosine, sine)


def label_of(positions, starts_ref):
    label = jnp.full(positions.shape, -1, jnp.int32)
    for number in range(starts_ref.shape[0]):
        inside = (positions >= starts_ref[number]) & (positions < starts_ref[number] + SPAN)
        label = jnp.where(inside, jnp.int32(number), label)
    return label


def hidden_bias(query_at, key_at, starts_ref):
    query_label = label_of(query_at, starts_ref)
    key_label = label_of(key_at, starts_ref)
    visible = (key_at <= query_at) | (query_label == key_label) & (query_label >= 0)
    return jnp.where(visible, 0.0, -1e30)


def crosses(starts_ref, edge, rows):
    hit = None
    for number in range(starts_ref.shape[0]):
        start = starts_ref[number]
        here = (start < edge) & (start + SPAN > edge)
        hit = here if hit is None else hit | here
    return hit


def attend(starts, query, key, value, rows):
    heads, length, _ = query.shape
    count = length // rows
    factor = LOG2E / math.sqrt(HDIM)

    def kernel(starts_ref, q_ref, k_ref, v_ref, o_ref, bias):
        @pl.when(pl.program_id(0) == 0)
        def _():
            for block in range(count):
                shape = (rows, 2 * rows)
                query_at = block * rows + lax.broadcasted_iota(jnp.int32, shape, 0)
                key_at = block * rows + lax.broadcasted_iota(jnp.int32, shape, 1)
                bias[block] = hidden_bias(query_at, key_at, starts_ref)

        def one(block, extra):
            low, high = block * rows, (block + 1 + extra) * rows
            q = q_ref[0, low : low + rows, :]
            edge = dot_t(q, k_ref[0, low:high, :]) + bias[block, :, : high - low]
            top = jnp.max(edge, axis=1, keepdims=True)
            if block:
                before = dot_t(q, k_ref[0, :low, :])
                top = jnp.maximum(top, jnp.max(before, axis=1, keepdims=True))
            shift = top * factor
            weight = jnp.exp2(edge * factor - shift)
            total = jnp.sum(weight, axis=1, keepdims=True)
            out = dot(weight.astype(BF16), v_ref[0, low:high, :])
            if block:
                weight = jnp.exp2(before * factor - shift)
                total = total + jnp.sum(weight, axis=1, keepdims=True)
                out = out + dot(weight.astype(BF16), v_ref[0, :low, :])
            o_ref[0, low : low + rows, :] = (out / total).astype(BF16)

        for block in range(count):
            if block == count - 1:
                one(block, 0)
                continue
            wide = crosses(starts_ref, (block + 1) * rows, rows)
            pl.when(wide)(functools.partial(one, block, 1))
            pl.when(jnp.logical_not(wide))(functools.partial(one, block, 0))

    spec = pl.BlockSpec((1, length, HDIM), lambda h: (h, 0, 0))
    return call(
        kernel,
        jax.ShapeDtypeStruct(query.shape, BF16),
        [smem(), spec, spec, spec],
        spec,
        [pltpu.VMEM((count, rows, 2 * rows), F32)],
        4 * heads * length * length * HDIM * 4,
        16 * heads * length * HDIM,
        "attend",
        limit=20,
        grid=(heads,),
    )(starts, query, key, value)


def attend_back(
    starts, place, query, key, value, near, far, cosine, sine, narrow, b_heads, rows, first, heads
):
    length = query.shape[1]
    thin = narrow.shape[0]
    rank = thin // 3
    count = length // rows
    scale = 1.0 / math.sqrt(HDIM)
    factor = LOG2E * scale

    def kernel(
        starts_ref, place_ref, q_ref, k_ref, v_ref, near_ref, far_ref, cos_ref, sin_ref,
        narrow_ref, b_ref, dq_ref, dk_ref, dv_ref, thin_ref, out_ref, bias, key_sum, value_sum, key_turned,
    ):
        @pl.when(pl.program_id(0) == 0)
        def _():
            for block in range(count):
                shape = (2 * rows, rows)
                query_at = block * rows + lax.broadcasted_iota(jnp.int32, shape, 1)
                key_at = block * rows + lax.broadcasted_iota(jnp.int32, shape, 0)
                bias[block] = hidden_bias(query_at, key_at, starts_ref)

            thin_ref[...] = jnp.zeros_like(thin_ref)

        key_sum[...] = jnp.zeros_like(key_sum)
        value_sum[...] = jnp.zeros_like(value_sum)
        key_turned[...] = k_ref[0].astype(F32).T.astype(BF16)

        def one(block, extra):
            low, high = block * rows, (block + 1 + extra) * rows
            q = q_ref[0, low : low + rows, :]
            relative = place_ref[0] ^ block
            at = pl.multiple_of((relative % 2) * rows, rows)
            g = jnp.where(relative < 2, near_ref[0, pl.ds(at, rows), :], far_ref[0, pl.ds(at, rows), :])
            raw = dot_t(k_ref[0, low:high, :], q) + bias[block, : high - low, :]
            if block:
                raw = jnp.concatenate([dot_t(k_ref[0, :low, :], q), raw], axis=0)
            top = jnp.max(raw, axis=0, keepdims=True)
            weight = jnp.exp2(raw * factor - top * factor)
            probs = weight * (1.0 / jnp.sum(weight, axis=0, keepdims=True))
            grad_probs = dot_t(v_ref[0, :high, :], g)
            inner = jnp.sum(grad_probs * probs, axis=0, keepdims=True)
            grad_scores = (probs * (grad_probs - inner)).astype(BF16)
            value_sum[:high, :] += dot(probs.astype(BF16), g)
            key_sum[:high, :] += dot(grad_scores, q)
            turned = dot(key_turned[:, :high], grad_scores)
            back = turned.T * scale
            dq_ref[0, low : low + rows, :] = turn(
                back, cos_ref[low : low + rows, :], -sin_ref[low : low + rows, :]
            ).astype(BF16)

        for block in range(count):
            if block == count - 1:
                one(block, 0)
                continue
            wide = crosses(starts_ref, (block + 1) * rows, rows)
            pl.when(wide)(functools.partial(one, block, 1))
            pl.when(jnp.logical_not(wide))(functools.partial(one, block, 0))
        dk_ref[0] = turn(key_sum[...] * scale, cos_ref[...], -sin_ref[...]).astype(BF16)
        dv_ref[0] = value_sum[...].astype(BF16)
        for number, ref in enumerate((dq_ref, dk_ref, dv_ref)):
            here = slice(number * rank, (number + 1) * rank)
            thin_ref[here, :] += dot_t(b_ref[0, here, :], ref[0])
            out_ref[0, here, :] = dot(narrow_ref[here, :], ref[0])

    spec = pl.BlockSpec((1, length, HDIM), lambda h: (first + h, 0, 0))
    half = pl.BlockSpec((1, length // 2, HDIM), lambda h: (first + h, 0, 0))
    out = pl.BlockSpec((1, length, HDIM), lambda h: (h, 0, 0))
    table = pl.BlockSpec((length, HDIM), lambda h: (0, 0))
    return call(
        kernel,
        [jax.ShapeDtypeStruct((heads, length, HDIM), BF16)] * 3
        + [
            jax.ShapeDtypeStruct((thin, length), F32),
            jax.ShapeDtypeStruct((heads, thin, HDIM), F32),
        ],
        [smem(), smem(), spec, spec, spec, half, half, table, table]
        + [
            pl.BlockSpec((thin, length), lambda h: (0, 0)),
            pl.BlockSpec((1, thin, HDIM), lambda h: (first + h, 0, 0)),
        ],
        [out] * 3
        + [
            pl.BlockSpec((thin, length), lambda h: (0, 0)),
            pl.BlockSpec((1, thin, HDIM), lambda h: (h, 0, 0)),
        ],
        [
            pltpu.VMEM((count, 2 * rows, rows), F32),
            pltpu.VMEM((length, HDIM), F32),
            pltpu.VMEM((length, HDIM), F32),
            pltpu.VMEM((HDIM, length), BF16),
        ],
        10 * heads * length * length * HDIM * 4,
        32 * heads * length * HDIM,
        "attend_back",
        limit=24,
        grid=(heads,),
    )(starts, place[None], query, key, value, near, far, cosine, sine, narrow, b_heads)


def rows_by_heads(refs, start, rows):
    return jnp.concatenate(
        [ref[head, pl.ds(start, rows), :] for ref in refs for head in range(ref.shape[0])], axis=1
    )


def close_attention(mixed, place, weight, a_out, wanted, rows):
    size, width = weight.shape
    rank = a_out.shape[0]

    def kernel(place_ref, m_ref, w_ref, a_ref, *outs):
        for block, out in zip(wanted, outs):
            start = pl.multiple_of((place_ref[0] ^ block) * rows, rows)
            here = rows_by_heads([m_ref], start, rows)
            out[:, :width] = dot(here, w_ref[...]).astype(BF16)
            narrow = dot_t(here, a_ref[...]).astype(BF16)
            out[:, width:] = jnp.concatenate(
                [narrow, jnp.zeros((rows, EXTRA - rank), BF16)], axis=1
            )

    return call(
        kernel,
        [jax.ShapeDtypeStruct((rows, width + EXTRA), BF16)] * len(wanted),
        [smem()] + [vmem()] * 3,
        [vmem()] * len(wanted),
        [],
        2 * rows * len(wanted) * size * width,
        2 * size * width + 2 * rows * len(wanted) * (width + size),
        "close_attention",
        limit=28,
    )(place[None], mixed, weight, a_out)


def open_attention(blocks, seconds, wanted, place, mixed, weight, a_out, b_out):
    rows, width_ext = blocks[0].shape
    size, width = weight.shape
    rank = a_out.shape[0]
    count = len(blocks)
    heads = size // HDIM

    def kernel(place_ref, *refs):
        g_refs, refs = refs[:count], refs[count:]
        s_refs, refs = refs[:count], refs[count:]
        m_ref, w_ref, a_ref, b_ref, out, sum_ref, wide_ref = refs
        total, branch, second = None, None, None
        for block in range(count):
            start = pl.multiple_of((place_ref[0] ^ wanted[block]) * rows, rows)
            grad = g_refs[block][:, :width]
            thin = g_refs[block][:, width:]
            narrow = dot_t(grad, b_ref[...]).astype(BF16)
            back = dot_t(grad, w_ref[...]) + dot(narrow, a_ref[...])
            for head in range(heads):
                part = back[:, head * HDIM : (head + 1) * HDIM]
                out[head, block * rows : (block + 1) * rows, :] = part.astype(BF16)
            terms = (
                t_dot(narrow, rows_by_heads([m_ref], start, rows)),
                t_dot(thin, grad)[:rank],
                t_dot(thin, s_refs[block][...])[rank : 3 * rank],
            )
            if block == 0:
                total, branch, second = terms
            else:
                total, branch, second = total + terms[0], branch + terms[1], second + terms[2]
        sum_ref[...] = total
        wide_ref[:rank, :] = branch
        wide_ref[rank:, :] = second

    return call(
        kernel,
        [
            jax.ShapeDtypeStruct((heads, rows * count, HDIM), BF16),
            jax.ShapeDtypeStruct((rank, size), F32),
            jax.ShapeDtypeStruct((3 * rank, width), F32),
        ],
        [smem()] + [vmem()] * (2 * count + 4),
        [vmem()] * 3,
        [],
        2 * rows * count * size * width,
        2 * size * width + 2 * rows * count * (2 * width + 2 * size),
        "open_attention",
        limit=32,
    )(place[None], *blocks, *seconds, mixed, weight, a_out, b_out)


def feed_forward(blocks, grads, offsets, pieces, down, a_mlp, b_down, a_hidden, b_hidden):
    rows, width = blocks[0].shape
    count = len(blocks)
    size = down.shape[0]
    rank = b_down.shape[0]
    n = len(pieces)

    def kernel(offsets_ref, *refs):
        x_refs, refs = refs[:count], refs[count:]
        g_refs, refs = refs[:count], refs[count:]
        piece_refs, refs = refs[:n], refs[n:]
        down_hbm, am_ref, bd_ref, ah_ref, bh_ref = refs[:5]
        refs = refs[5:]
        feed_refs, refs = refs[:count], refs[count:]
        back_refs, refs = refs[:count], refs[count:]
        sum_ref, whole, down_ref, grad_ref, sems, down_sem = refs
        down_copy = pltpu.make_async_copy(down_hbm, down_ref, down_sem)
        down_copy.start()
        copies = load_pieces(offsets_ref, piece_refs, whole, sems)
        narrows = [dot_t(x_refs[block][...], am_ref[...]).astype(BF16) for block in range(count)]
        thins = [dot_t(g_refs[block][...], bd_ref[...]).astype(BF16) for block in range(count)]
        down_copy.wait()
        for block in range(count):
            grad_ref[block] = (
                dot_t(g_refs[block][...], down_ref[...]) + dot(thins[block], ah_ref[...])
            ).astype(BF16)
        for copy in copies:
            copy.wait()
        pad = jnp.zeros((rows, EXTRA - rank), BF16)
        for block in range(count):
            x = x_refs[block][...]
            narrow = narrows[block]
            gate = dot(x, whole[0]) + dot(narrow[:, :rank], bh_ref[0])
            up = dot(x, whole[1]) + dot(narrow[:, rank:], bh_ref[1])
            sigmoid = 0.5 + 0.5 * jnp.tanh(0.5 * gate)
            silu = gate * sigmoid
            hidden = (silu * up).astype(BF16)
            grad_hidden = grad_ref[block].astype(F32)
            grad_up = (grad_hidden * silu).astype(BF16)
            grad_gate = (grad_hidden * up * (sigmoid + silu * (1.0 - sigmoid))).astype(BF16)
            feed_refs[block][:, :width] = dot(hidden, down_ref[...]).astype(BF16)
            feed_refs[block][:, width:] = jnp.concatenate(
                [dot_t(hidden, ah_ref[...]).astype(BF16), pad], axis=1
            )
            back = dot_t(grad_gate, whole[0]) + dot_t(grad_up, whole[1])
            back_refs[block][:, :width] = back.astype(BF16)
            back_refs[block][:, width:] = jnp.concatenate(
                [
                    dot_t(grad_gate, bh_ref[0]).astype(BF16),
                    dot_t(grad_up, bh_ref[1]).astype(BF16),
                    pad[:, rank:],
                ],
                axis=1,
            )
            terms = (
                t_dot(thins[block], hidden),
                t_dot(narrow[:, :rank], grad_gate),
                t_dot(narrow[:, rank:], grad_up),
            )
            for number, term in enumerate(terms):
                here = slice(number * rank, (number + 1) * rank)
                if block == 0:
                    sum_ref[here, :] = term
                else:
                    sum_ref[here, :] += term

    out = jax.ShapeDtypeStruct((rows, width + EXTRA), BF16)
    return call(
        kernel,
        [out] * (2 * count)
        + [jax.ShapeDtypeStruct((3 * rank, size), F32)],
        [smem()] + [vmem()] * (2 * count) + [anywhere()] * (n + 1) + [vmem()] * 4,
        [vmem()] * (2 * count + 1),
        [
            pltpu.VMEM((2, width, size), BF16),
            pltpu.VMEM((size, width), BF16),
            pltpu.VMEM((count, rows, size), BF16),
            pltpu.SemaphoreType.DMA((n,)),
            pltpu.SemaphoreType.DMA,
        ],
        12 * rows * count * width * size,
        6 * width * size + 8 * rows * count * width,
        "feed_forward",
    )(offsets, *blocks, *grads, *pieces, down, a_mlp, b_down, a_hidden, b_hidden)


def project_back(grads, place, offsets, pieces, wanted, rows):
    size = pieces[0].shape[1]
    width = 4 * pieces[0].shape[0]
    n = len(pieces)
    count = len(wanted)

    def kernel(place_ref, offsets_ref, *refs):
        g_refs, refs = refs[: len(grads)], refs[len(grads) :]
        piece_refs, refs = refs[:n], refs[n:]
        back_refs, (whole, sems) = refs[:count], refs[count:]
        copies = load_pieces(offsets_ref, piece_refs, whole, sems)
        starts = [pl.multiple_of((place_ref[0] ^ block) * rows, rows) for block in wanted]
        parts = [rows_by_heads(g_refs, start, rows) for start in starts]
        for copy in copies:
            copy.wait()
        for part, back in zip(parts, back_refs):
            back[...] = dot_t(part, whole[...]).astype(BF16)

    return call(
        kernel,
        [jax.ShapeDtypeStruct((rows, width), BF16)] * count,
        [smem(), smem()] + [vmem()] * len(grads) + [anywhere()] * n,
        [vmem()] * count,
        [pltpu.VMEM((width, size), BF16), pltpu.SemaphoreType.DMA((n,))],
        2 * rows * count * width * size,
        2 * (rows * count * (width + size) + width * size),
        "project_back",
        limit=56,
    )(place[None], offsets, *grads, *pieces)


def thin_product(thin, place, blocks):
    rows, width = blocks[0].shape
    count = len(blocks)

    def kernel(place_ref, thin_ref, *refs):
        total = None
        for block in range(count):
            start = pl.multiple_of((place_ref[0] ^ block) * rows, rows)
            term = dot(thin_ref[:, pl.ds(start, rows)], refs[block][...])
            total = term if total is None else total + term
        refs[count][...] = total

    return call(
        kernel,
        jax.ShapeDtypeStruct((thin.shape[0], width), F32),
        [smem()] + [vmem()] * (count + 1),
        vmem(),
        [],
        2 * 128 * rows * count * width,
        2 * rows * count * width,
        "thin_product",
        limit=24,
    )(place[None], thin, *blocks)


def shards(
    tokens,
    cotangent,
    sequence_adapter_index,
    image_span_start,
    attention_norm_gain,
    feedforward_norm_gain,
    query_key_value_weight,
    attention_output_weight,
    gate_up_projection_weight,
    down_projection_weight,
    adapter_model_input_maps,
    adapter_model_output_maps,
    adapter_hidden_input_map,
    adapter_hidden_output_maps,
):
    rows = tokens.shape[1]
    width = tokens.shape[2]
    rank = adapter_model_input_maps.shape[2]
    group = lax.axis_size("shard")
    place = lax.axis_index("shard").astype(jnp.int32)
    rep_place = lax.axis_index("rep").astype(jnp.int32)
    pick = sequence_adapter_index[0]
    starts = image_span_start[0]
    head_cols = width // group
    ff_cols = down_projection_weight.shape[0]
    k_rows = query_key_value_weight.shape[1]

    gain_one = attention_norm_gain.astype(F32)
    gain_two = feedforward_norm_gain.astype(F32)
    residual_in = tokens[0].astype(F32)
    grad_out = cotangent[0].astype(F32)

    def own_columns(values, size):
        return lax.dynamic_slice_in_dim(values, place * size, size, values.ndim - 1)

    quarter = k_rows // 4
    quarter_one, quarter_two = sides(
        query_key_value_weight, rep_place % 4 * quarter, quarter, place, head_cols, (2, 3), "sides_far"
    )
    first_a = hop(quarter_one, "shard", 2)
    first_b = hop(quarter_two, "shard", 3)
    normed = norm_rows(residual_in, gain_one).astype(BF16)
    normed_near = core(normed)
    front_chip, front_part = chip_picked(
        jnp.concatenate([adapter_model_input_maps[0:3], adapter_model_output_maps[0:3]]), pick, place
    )
    first_own, near_out = sides(
        query_key_value_weight, 0, k_rows, place, head_cols, (0, 1), "sides_near"
    )
    first_near = core(near_out)
    first_a, front_part, normed, first_own = fence(first_a, front_part, normed, first_own)
    first_a_two, first_a_three = hop(first_a, "rep", 2), hop(first_a, "rep", 1)
    front_far = across(front_part)
    first_b, first_a_two, first_a_three, normed = fence(first_b, first_a_two, first_a_three, normed)
    first_b_two, first_b_three = hop(first_b, "rep", 1), hop(first_b, "rep", 2)
    normed_far = across(normed)
    first_b_two, first_b_three, front_far, gate_up, grad_out, front_chip = fence(
        first_b_two, first_b_three, front_far, gate_up_projection_weight, grad_out, front_chip
    )
    first_a_four, first_b_four = hop(first_a_two, "rep", 1), hop(first_b_two, "rep", 2)
    mlp_leaving = [side(gate_up, rep_place % 4 * quarter, quarter, place ^ j, ff_cols) for j in (2, 3)]
    grad_feed = (BRANCH * grad_out).astype(BF16)
    half = HDIM // 2
    frequency = jnp.exp(jnp.arange(half, dtype=F32) * (-2.0 / HDIM) * math.log(THETA))
    angle = jnp.arange(rows * group, dtype=jnp.int32).astype(F32)[:, None] * frequency[None, :]
    cosine = jnp.concatenate([jnp.cos(angle), jnp.cos(angle)], axis=1)
    sine = jnp.concatenate([jnp.sin(angle), jnp.sin(angle)], axis=1)
    front = whole_picked(front_chip, front_far, place)
    a_first = front[:3].reshape(3 * rank, width)
    b_first = own_columns(front[3:], head_cols)
    b_wide = jnp.concatenate(
        [jnp.pad(b_first[i], ((0, 0), (i * head_cols, (2 - i) * head_cols))) for i in range(3)]
    )
    normed_far, first_a_four, first_b_four, mlp_leaving, grad_feed, cosine, sine, b_wide, a_first = fence(
        normed_far, first_a_four, first_b_four, mlp_leaving, grad_feed, cosine, sine, b_wide, a_first
    )
    first_blocks = (normed, normed_near, normed_far, core(normed_far))
    first_offsets, first_pieces = arrange(
        k_rows, first_own, first_near,
        (
            (first_a, first_a_two, first_a_three, first_a_four),
            (first_b, first_b_two, first_b_three, first_b_four),
        ),
        place, rep_place,
    )

    mlp_a, mlp_b = hop(mlp_leaving[0], "shard", 2), hop(mlp_leaving[1], "shard", 3)
    query, key, value, narrow_first = project(
        first_blocks, place, first_offsets, first_pieces, a_first, b_wide, cosine, sine
    )
    query, mlp_a, rest_bank, wide_bank = fence(
        query, mlp_a,
        (adapter_model_input_maps[3:6], adapter_model_output_maps[3:5]),
        (adapter_hidden_input_map[None], adapter_hidden_output_maps),
    )
    mlp_a_two, mlp_a_three = hop(mlp_a, "rep", 2), hop(mlp_a, "rep", 1)
    rest_chip, rest_part = chip_picked(jnp.concatenate(rest_bank), pick, place)
    wide_chip, wide_part = chip_picked(jnp.concatenate(wide_bank), pick, place)
    rest_part, wide_part, query = fence(rest_part, wide_part, query)
    rest_far, wide_far = across(rest_part), across(wide_part)
    mixed = attend(starts, query, key, value, rows)
    mixed, mlp_b, mlp_a_two, mlp_a_three, rest_far = fence(
        mixed, mlp_b, mlp_a_two, mlp_a_three, rest_far
    )
    mlp_b_two, mlp_b_three = hop(mlp_b, "rep", 1), hop(mlp_b, "rep", 2)
    rest = whole_picked(rest_chip, rest_far, place)
    a_out = own_columns(rest[0], head_cols)
    a_mlp = rest[1:3].reshape(2 * rank, width)
    b_out, b_down = rest[3], rest[4]
    far_out = close_attention(mixed, place, attention_output_weight, a_out, (2, 3), rows)
    far_sum = (far_out[0].astype(F32) + core(far_out[1]).astype(F32)).astype(BF16)
    far_sum, mixed_here, grad_feed, wide_far = fence(far_sum, mixed, grad_feed, wide_far)
    branch_far = across(far_sum)
    feed_near_in = core(grad_feed)
    near_out = close_attention(mixed_here, place, attention_output_weight, a_out, (0, 1), rows)
    near_out, mlp_b_two, mlp_b_three, gate_up = fence(near_out, mlp_b_two, mlp_b_three, gate_up)
    mlp_a_four, mlp_b_four = hop(mlp_a_two, "rep", 1), hop(mlp_b_two, "rep", 2)
    near_here = core(near_out[1])
    mlp_near = core(side(gate_up, 0, k_rows, place ^ 1, ff_cols))
    mlp_own = side(gate_up, 0, k_rows, place, ff_cols)
    hidden_cols = own_columns(whole_picked(wide_chip, wide_far, place), ff_cols)
    near_here, branch_far, hidden_cols, mlp_own, mlp_a_four, mlp_b_four = fence(
        near_here, branch_far, hidden_cols, mlp_own, mlp_a_four, mlp_b_four
    )
    feed_far_in = across(after(grad_feed, branch_far))
    a_hidden, b_hidden = hidden_cols[0], hidden_cols[1:]
    branch_own = near_out[0].astype(F32) + near_here.astype(F32) + branch_far.astype(F32)
    narrow_out = branch_own[:, width : width + rank].astype(BF16)
    branch = branch_own[:, :width] + dot(narrow_out, b_out)
    middle = residual_in + BRANCH * branch
    normed_second = norm_rows(middle, gain_two).astype(BF16)
    second_far = across(normed_second)
    second_near = core(normed_second)
    second_near, feed_near_in, mlp_near = fence(second_near, feed_near_in, mlp_near)
    mlp_offsets, mlp_pieces = arrange(
        k_rows, mlp_own, mlp_near,
        (
            (mlp_a, mlp_a_two, mlp_a_three, mlp_a_four),
            (mlp_b, mlp_b_two, mlp_b_three, mlp_b_four),
        ),
        place, rep_place,
    )
    *parts, sum_near = feed_forward(
        (normed_second, second_near), (grad_feed, feed_near_in), mlp_offsets, mlp_pieces,
        down_projection_weight, a_mlp, b_down, a_hidden, b_hidden,
    )
    feed_near, back_near = parts[:2], parts[2:]
    second_far, feed_far_in, back_near, feed_near = fence(second_far, feed_far_in, back_near, feed_near)
    second_blocks = (normed_second, second_near, second_far, core(second_far))
    feed_blocks = (grad_feed, feed_near_in, feed_far_in, core(feed_far_in))
    *parts, sum_far = feed_forward(
        second_blocks[2:], feed_blocks[2:], mlp_offsets, mlp_pieces, down_projection_weight,
        a_mlp, b_down, a_hidden, b_hidden,
    )
    feed_far, back_far = parts[:2], parts[2:]
    back_sum = (back_far[0].astype(F32) + core(back_far[1]).astype(F32)).astype(BF16)
    back_sum, back_near, feed_near, feed_far, sum_near = fence(
        back_sum, back_near, feed_near, feed_far, sum_near
    )
    back_from_far = across(back_sum)

    bits = reps_bits()
    back_here = core(back_near[1])
    feed_here = core(feed_near[1])
    feed_mate = core(feed_far[1])
    mark = jnp.full((rank, ff_cols), pick.astype(F32))
    wide_all = jnp.concatenate([sum_near + sum_far, mark]).astype(BF16)[None]
    wide_hop = hop(wide_all, "rep", bits[0])
    feed_here = feed_near[0].astype(F32) + feed_here.astype(F32)
    feed_sum = (feed_far[0].astype(F32) + feed_mate.astype(F32)).astype(BF16)
    back_from_far, feed_here, feed_sum, back_here, wide_hop = fence(
        back_from_far, feed_here, feed_sum, back_here, wide_hop
    )
    second_own = back_near[0].astype(F32) + back_here.astype(F32) + back_from_far.astype(F32)
    grad_narrow_mlp = second_own[:, width : width + 2 * rank].astype(BF16)
    grad_normed_second = second_own[:, :width] + dot(grad_narrow_mlp, a_mlp)
    grad_middle = grad_out + norm_back(middle, gain_two, grad_normed_second)
    grad_branch = (BRANCH * grad_middle).astype(BF16)
    branch_rows = pad_columns([grad_branch, narrow_out, grad_narrow_mlp], width + EXTRA)
    branch_rows, wide_hop = fence(branch_rows, wide_hop)
    branch_far_in = across(branch_rows)
    branch_near_in = core(branch_rows)
    wide_all = both(wide_all, wide_hop, rep_place, bits[0])
    for bit in bits[1:-2]:
        wide_all = both(wide_all, hop(wide_all, "rep", bit), rep_place, bit)
    wide_hop = hop(wide_all, "rep", bits[-2])
    branch_near_in, wide_all = fence(branch_near_in, wide_all)
    mixed_near, grad_a_near, thin_near = open_attention(
        (branch_rows, branch_near_in), second_blocks[:2], (0, 1), place, mixed,
        attention_output_weight, a_out, b_out,
    )
    branch_far_in, mixed_near = fence(branch_far_in, mixed_near)
    feed_from_far = across(after(feed_sum, branch_far_in))
    mixed_far, grad_a_far, thin_far = open_attention(
        (branch_far_in, core(branch_far_in)), second_blocks[2:], (2, 3), place, mixed,
        attention_output_weight, a_out, b_out,
    )

    b_heads = b_first.reshape(3 * rank, head_cols // HDIM, HDIM).transpose(1, 0, 2)

    def attend_part(first, heads, starts):
        return attend_back(
            starts, place, query, key, value, mixed_near, mixed_far, cosine, sine, narrow_first, b_heads,
            rows, first, heads,
        )

    mixed_far, wide_hop = fence(mixed_far, wide_hop)
    wide_all = both(wide_all, wide_hop, rep_place, bits[-2])
    wide_hop = hop(wide_all, "rep", bits[-1])
    wide_all, starts_one = fence(wide_all, starts)
    heads = query.shape[0]
    third = heads // 3
    part_one = attend_part(0, third, starts_one)
    part_one, feed_from_far, wide_hop, starts_two = fence(part_one, feed_from_far, wide_hop, starts_one)
    wide_all = both(wide_all, wide_hop, rep_place, bits[-1])
    picks = wide_all[:, -1, :1].astype(F32)
    adapters = adapter_model_input_maps.shape[1] * group
    chosen = (picks == jnp.arange(adapters, dtype=jnp.int32).astype(F32)[None, :]).astype(F32)
    wide_sent = send_sums(wide_all[:, :-rank], chosen, place)
    early_all = jnp.concatenate(
        [grad_a_near + grad_a_far, own_columns(thin_near + thin_far, head_cols)]
    ).astype(BF16)[None]
    early_hop = hop(early_all, "rep", bits[0])
    feed_own = feed_here + feed_from_far.astype(F32)
    narrow_down = feed_own[:, width : width + rank].astype(BF16)
    down_far = across(narrow_down)
    down_near = core(narrow_down)
    starts_two, narrow_down, early_all = fence(starts_two, narrow_down, early_all)
    part_two = attend_part(third, third, starts_two)
    part_two, wide_sent, early_hop, down_far, down_near, starts_three = fence(
        part_two, wide_sent, early_hop, down_far, down_near, starts_two
    )
    early_all = both(early_all, early_hop, rep_place, bits[0])
    for bit in bits[1:-2]:
        early_all = both(early_all, hop(early_all, "rep", bit), rep_place, bit)
    early_hop = hop(early_all, "rep", bits[-2])
    down_far_near = core(down_far)
    early_all, starts_three = fence(early_all, starts_three)
    part_three = attend_part(2 * third, heads - 2 * third, starts_three)
    part_three, early_hop, down_far_near = fence(part_three, early_hop, down_far_near)
    parts = (part_one, part_two, part_three)
    first_grads = [part[number] for number in range(3) for part in parts]
    thin = (part_one[3] + part_two[3] + part_three[3]).astype(BF16)
    thin_hop = core(thin)
    early_all = both(early_all, early_hop, rep_place, bits[-2])
    early_hop = hop(early_all, "rep", bits[-1])
    early_all, first_grads = fence(early_all, first_grads)
    back_rows_far = project_back(first_grads, place, first_offsets, first_pieces, (2, 3), rows)
    back_rows_far, thin_hop, early_hop = fence(back_rows_far, thin_hop, early_hop)
    back_mate = core(back_rows_far[1])
    thin = (thin.astype(F32) + thin_hop.astype(F32)).astype(BF16)
    thin_hop = across(thin)
    back_sum = (back_rows_far[0].astype(F32) + back_mate.astype(F32)).astype(BF16)
    thin_hop, back_sum, grad_b_heads = fence(thin_hop, back_sum, [part[4] for part in parts])
    back_far_in = across(back_sum)
    grad_narrow = (thin.astype(F32) + thin_hop.astype(F32)).astype(BF16)
    grad_b_first = jnp.concatenate(grad_b_heads).transpose(1, 0, 2).reshape(3 * rank, head_cols)
    down_thin = (narrow_down, down_near, down_far, down_far_near)
    grad_b_down = sum(t_dot(left, right) for left, right in zip(down_thin, feed_blocks))
    late_all = jnp.concatenate(
        [
            own_columns(thin_product(grad_narrow, place, first_blocks), head_cols),
            grad_b_first,
            own_columns(grad_b_down, head_cols),
        ]
    ).astype(BF16)[None]
    late_all, grads_here = fence(late_all, first_grads)
    late_hop = hop(late_all, "rep", bits[0])
    back_rows_near = project_back(grads_here, place, first_offsets, first_pieces, (0, 1), rows)
    late_hop, back_rows_near = fence(late_hop, back_rows_near)
    back_rows_here = core(back_rows_near[1])
    late_all = both(late_all, late_hop, rep_place, bits[0])
    for bit in bits[1:-2]:
        late_all = both(late_all, hop(late_all, "rep", bit), rep_place, bit)
    late_hop = hop(late_all, "rep", bits[-2])
    late_all, early_hop, early_all = fence(late_all, early_hop, early_all)
    early_sent = send_sums(both(early_all, early_hop, rep_place, bits[-1]), chosen, place)

    def whole_maps(stacked, low, high, n):
        part = stacked[:, :, low:high].reshape(group, stacked.shape[1], -1, rank, n)
        pieces = [lax.dynamic_index_in_dim(part, place ^ i, 0, keepdims=False) for i in range(group)]
        return jnp.concatenate(pieces, axis=-1).transpose(1, 0, 2, 3).astype(F32)

    feed = feed_here[:, :width] + feed_from_far[:, :width].astype(F32) + dot(narrow_down, b_down)
    output = (middle + BRANCH * feed).astype(BF16)
    late_hop, output = fence(late_hop, output)
    late_all = both(late_all, late_hop, rep_place, bits[-2])
    late_hop = hop(late_all, "rep", bits[-1])
    hidden_maps = whole_maps(jnp.stack(wide_sent), 0, 3 * rank, ff_cols)
    late_hop, hidden_maps, back_far_in = fence(late_hop, hidden_maps, back_far_in)
    late_sent = send_sums(both(late_all, late_hop, rep_place, bits[-1]), chosen, place)
    narrow_own = lax.dynamic_slice_in_dim(grad_narrow, place * rows, rows, 1)
    grad_normed = (
        back_rows_near[0].astype(F32) + back_rows_here.astype(F32) + back_far_in.astype(F32)
        + t_dot(narrow_own, a_first)
    )
    input_grad = grad_middle + norm_back(residual_in, gain_one, grad_normed)
    early_got = jnp.stack(early_sent)
    late_sent, input_grad, early_got = fence(late_sent, input_grad, early_got)
    late_got = jnp.stack(late_sent)
    grad_a_model = jnp.concatenate(
        [
            whole_maps(late_got, 0, 3 * rank, head_cols),
            whole_maps(early_got, 0, rank, head_cols),
            whole_maps(early_got, 2 * rank, 4 * rank, head_cols),
        ]
    )
    grad_b_model = jnp.concatenate(
        [
            whole_maps(late_got, 3 * rank, 6 * rank, head_cols),
            whole_maps(early_got, rank, 2 * rank, head_cols),
            whole_maps(late_got, 6 * rank, 7 * rank, head_cols),
        ]
    )
    return (
        output[None], input_grad[None], grad_a_model, grad_b_model, hidden_maps[0], hidden_maps[1:3],
    )


def solution(mesh):
    in_specs = (
        P("rep", "shard", None),
        P("rep", "shard", None),
        P("rep"),
        P("rep", None),
        P(),
        P(),
        P(None, "shard", None),
        P("shard", None),
        P(None, "shard", None),
        P("shard", None),
        P(None, "shard", None, None),
        P(None, "shard", None, None),
        P("shard", None, None),
        P(None, "shard", None, None),
    )
    out_specs = (
        P("rep", "shard", None),
        P("rep", "shard", None),
        P(None, "shard", None, None),
        P(None, "shard", None, None),
        P("shard", None, None),
        P(None, "shard", None, None),
    )
    return jax.shard_map(shards, mesh=mesh, in_specs=in_specs, out_specs=out_specs, check_vma=False)
```

```python
import functools
import math

import jax
import jax.numpy as jnp
from jax import lax
from jax.experimental import pallas as pl
from jax.experimental.pallas import tpu as pltpu
from jax.sharding import PartitionSpec as P

HDIM = 64
SPAN = 256
EPS = 1e-05
THETA = 10000.0
BRANCH = 1.4 / math.sqrt(40.0)
EXTRA = 128
F32 = jnp.float32
BF16 = jnp.bfloat16
LOG2E = math.log2(math.e)


def hop(values, axis, bit):
    size = lax.axis_size(axis)
    return lax.ppermute(values, axis, [(i, i ^ bit) for i in range(size)])


def core(values):
    return hop(values, "shard", 1)


def across(values):
    return hop(values, "shard", 2)


def rows_of(values, count):
    size = values.shape[0] // count
    return tuple(values[i * size : (i + 1) * size] for i in range(count))


def norm_rows(values, gain):
    return values * lax.rsqrt(jnp.mean(values * values, axis=-1, keepdims=True) + EPS) * gain


def norm_back(values, gain, grad):
    width = values.shape[-1]
    scale = lax.rsqrt(jnp.mean(values * values, axis=-1, keepdims=True) + EPS)
    moved = grad * gain
    inner = jnp.sum(values * moved, axis=-1, keepdims=True) / width
    return scale * moved - values * (scale * scale * scale) * inner


def dot(left, right):
    return jnp.dot(left, right, preferred_element_type=F32)


def dot_t(left, right):
    return lax.dot_general(left, right, (((1,), (1,)), ((), ())), preferred_element_type=F32)


def t_dot(left, right):
    return lax.dot_general(left, right, (((0,), (0,)), ((), ())), preferred_element_type=F32)


def pad_columns(pieces, width):
    used = sum(piece.shape[1] for piece in pieces)
    rest = jnp.zeros((pieces[0].shape[0], width - used), pieces[0].dtype)
    return jnp.concatenate(list(pieces) + [rest], axis=1)


def reps_bits():
    bits = []
    bit = 2
    while bit < lax.axis_size("rep"):
        bits.append(bit)
        bit *= 2
    return bits + [1]


def both(held, arrived, rep_place, bit):
    low = jnp.concatenate([held, arrived])
    high = jnp.concatenate([arrived, held])
    return jnp.where((rep_place // bit) % 2 == 0, low, high)


def send_sums(everyone, chosen, place):
    group = lax.axis_size("shard")
    per = chosen.shape[1] // group
    sent = []
    for j in range(group):
        marks = lax.dynamic_slice_in_dim(chosen, (place ^ j) * per, per, 1)
        sums = jnp.sum(marks[:, :, None, None] * everyone[:, None].astype(F32), axis=0).astype(BF16)
        sent.append(hop(sums, "shard", j) if j else sums)
    return sent


def chip_picked(bank, pick, place):
    per = bank.shape[1]
    rank = bank.shape[2]
    owner = pick // per
    mine = lax.dynamic_index_in_dim(bank, pick % per, 1, keepdims=False)
    mine = jnp.where(owner == place, mine, jnp.zeros_like(mine))
    chip = mine + core(mine)
    return chip, lax.dynamic_slice_in_dim(chip, (place % 2) * (rank // 2), rank // 2, 1)


def whole_picked(chip, far, place):
    other = core(far)
    low = jnp.where(place % 2 == 0, far, other)
    high = jnp.where(place % 2 == 0, other, far)
    return chip + jnp.concatenate([low, high], axis=1)


def after(value, *others):
    return lax.optimization_barrier((value, others))[0]


def side(weight, row, count, owner, size):
    return lax.dynamic_slice(weight, (0, row, owner * size), (weight.shape[0], count, size))


def sides(weight, row, count, place, size, wanted, name):
    maps, _, columns = weight.shape

    def kernel(where_ref, w_ref, *refs):
        outs, (held, sem) = refs[:-2], refs[-2:]
        start = pl.multiple_of(where_ref[1], 16)
        copy = pltpu.make_async_copy(w_ref.at[:, pl.ds(start, count), :], held, sem)
        copy.start()
        copy.wait()

        def write(out, owner):
            out[...] = jnp.concatenate(
                [held[i, :, owner * size : (owner + 1) * size] for i in range(maps)], axis=1
            )

        for j, out in zip(wanted, outs):
            for owner in range(columns // size):
                pl.when((where_ref[0] ^ j) == owner)(functools.partial(write, out, owner))

    return call(
        kernel,
        [jax.ShapeDtypeStruct((count, maps * size), BF16)] * len(wanted),
        [smem(), anywhere()],
        [vmem()] * len(wanted),
        [pltpu.VMEM((maps, count, columns), BF16), pltpu.SemaphoreType.DMA],
        0,
        2 * maps * count * (columns + size * len(wanted)),
        name,
        limit=58,
    )(jnp.stack([place, jnp.asarray(row, jnp.int32)]), weight)


def arrange(rows, own, near, ways, place, rep_place):
    quarter = rows // 4
    part = rep_place % 4
    pieces = [(place * rows, own), ((place ^ 1) * rows, near)]
    for j, one, two, parts in zip((2, 3), (2, 1), (1, 2), ways):
        for bits, piece in zip((0, one, two, one ^ two), parts):
            pieces.append(((place ^ j) * rows + (part ^ bits) * quarter, piece))
    offsets = jnp.stack([row.astype(jnp.int32) for row, _ in pieces])
    return offsets, [piece for _, piece in pieces]


def fence(*values):
    return lax.optimization_barrier(values)


def load_pieces(offsets, pieces, whole, sems):
    copies = []
    for number, piece in enumerate(pieces):
        start = pl.multiple_of(offsets[number], 16)
        here = pl.ds(start, piece.shape[-2])
        target = whole.at[here, :] if len(piece.shape) == 2 else whole.at[:, here, :]
        copy = pltpu.make_async_copy(piece, target, sems.at[number])
        copy.start()
        copies.append(copy)
    return copies


def vmem():
    return pl.BlockSpec(memory_space=pltpu.VMEM)


def smem():
    return pl.BlockSpec(memory_space=pltpu.SMEM)


def anywhere():
    return pl.BlockSpec(memory_space=pl.ANY)


def call(kernel, outs, in_specs, out_specs, scratch, flops, moved, name, limit=56, **more):
    return pl.pallas_call(
        kernel,
        out_shape=outs,
        in_specs=in_specs,
        out_specs=out_specs,
        scratch_shapes=scratch,
        compiler_params=pltpu.CompilerParams(vmem_limit_bytes=limit << 20),
        cost_estimate=pl.CostEstimate(flops=flops, bytes_accessed=moved, transcendentals=0),
        name=name,
        **more,
    )


def turn(values, cosine, sine):
    half = HDIM // 2
    turned = jnp.concatenate([-values[:, half:], values[:, :half]], axis=1)
    return values * cosine + turned * sine


def project(blocks, place, offsets, pieces, a_first, b_first, cosine_pair, sine_pair):
    rows, width = blocks[0].shape
    count = len(blocks)
    size = pieces[0].shape[1]
    heads = size // (3 * HDIM)
    thin = a_first.shape[0]
    n = len(pieces)

    def kernel(place_ref, offsets_ref, *refs):
        x_refs, refs = refs[:count], refs[count:]
        piece_refs, refs = refs[:n], refs[n:]
        a_ref, b_ref, cos_ref, sin_ref, q_ref, k_ref, v_ref, narrow_ref, whole, sems = refs
        copies = load_pieces(offsets_ref, piece_refs, whole, sems)
        starts = [pl.multiple_of((place_ref[0] ^ block) * rows, rows) for block in range(count)]
        for block in range(count):
            narrow_ref[:, pl.ds(starts[block], rows)] = dot_t(a_ref[...], x_refs[block][...]).astype(BF16)
        for copy in copies:
            copy.wait()
        both = 2 * heads * HDIM
        lane = lax.broadcasted_iota(jnp.int32, (rows, both), 1) % HDIM
        lower = lane < HDIM // 2
        for block in range(count):
            start = starts[block]
            narrow = narrow_ref[:, pl.ds(start, rows)]
            pre = dot(x_refs[block][...], whole[...]) + t_dot(narrow, b_ref[...])
            flat = pre[:, :both]
            cosine_here = jnp.tile(cos_ref[pl.ds(start, rows), :], (1, both // (2 * HDIM)))
            sine_here = jnp.tile(sin_ref[pl.ds(start, rows), :], (1, both // (2 * HDIM)))
            other = jnp.where(
                lower, pltpu.roll(flat, both - HDIM // 2, 1), pltpu.roll(flat, HDIM // 2, 1)
            )
            turned = (flat * cosine_here + other * sine_here).astype(BF16)
            straight = pre[:, both:].astype(BF16)
            for number, out in enumerate((q_ref, k_ref, v_ref)):
                for head in range(heads):
                    at = (number % 2 * heads + head) * HDIM
                    source = turned if number < 2 else straight
                    out[head, pl.ds(start, rows), :] = source[:, at : at + HDIM]

    by_heads = jax.ShapeDtypeStruct((heads, rows * count, HDIM), BF16)
    return call(
        kernel,
        [by_heads] * 3 + [jax.ShapeDtypeStruct((thin, rows * count), BF16)],
        [smem(), smem()] + [vmem()] * count + [anywhere()] * n + [vmem()] * 4,
        [vmem()] * 4,
        [pltpu.VMEM((width, size), BF16), pltpu.SemaphoreType.DMA((n,))],
        2 * rows * count * width * size,
        2 * (rows * count * width + width * size + 2 * rows * count * size),
        "project",
        limit=56,
    )(place[None], offsets, *blocks, *pieces, a_first, b_first, cosine_pair, sine_pair)


def label_of(positions, starts_ref):
    label = jnp.full(positions.shape, -1, jnp.int32)
    for number in range(starts_ref.shape[0]):
        inside = (positions >= starts_ref[number]) & (positions < starts_ref[number] + SPAN)
        label = jnp.where(inside, jnp.int32(number), label)
    return label


def hidden_bias(query_at, key_at, starts_ref):
    query_label = label_of(query_at, starts_ref)
    key_label = label_of(key_at, starts_ref)
    visible = (key_at <= query_at) | (query_label == key_label) & (query_label >= 0)
    return jnp.where(visible, 0.0, -1e30)


def crosses(starts_ref, edge):
    hit = None
    for number in range(starts_ref.shape[0]):
        start = starts_ref[number]
        here = (start < edge) & (start + SPAN > edge)
        hit = here if hit is None else hit | here
    return hit


def fill_bias(bias, starts_ref, rows):
    for block in range(bias.shape[0]):
        shape = (2 * rows, rows)
        query_at = block * rows + lax.broadcasted_iota(jnp.int32, shape, 1)
        key_at = block * rows + lax.broadcasted_iota(jnp.int32, shape, 0)
        bias[block] = hidden_bias(query_at, key_at, starts_ref)


def attend(starts, query, key, value, rows):
    heads, length, _ = query.shape
    count = length // rows
    factor = LOG2E / math.sqrt(HDIM)
    each = 3

    def kernel(starts_ref, q_ref, k_ref, v_ref, o_ref, log_ref, bias):
        @pl.when(pl.program_id(0) == 0)
        def _():
            for block in range(count):
                shape = (rows, 2 * rows)
                query_at = block * rows + lax.broadcasted_iota(jnp.int32, shape, 0)
                key_at = block * rows + lax.broadcasted_iota(jnp.int32, shape, 1)
                bias[block] = hidden_bias(query_at, key_at, starts_ref)

        def one(block, extra):
            low, high = block * rows, (block + 1 + extra) * rows
            here = slice(low, low + rows)
            states = []
            for head in range(each):
                q = q_ref[head, here, :]
                edge = dot_t(q, k_ref[head, low:high, :]) + bias[block, :, : high - low]
                before = dot_t(q, k_ref[head, :low, :]) if block else None
                states.append((edge, before))
            for head, (edge, before) in enumerate(states):
                top = jnp.max(edge, axis=1, keepdims=True)
                if block:
                    top = jnp.maximum(top, jnp.max(before, axis=1, keepdims=True))
                shift = top * factor
                weight = jnp.exp2(edge * factor - shift)
                total = jnp.sum(weight, axis=1, keepdims=True)
                out = dot(weight.astype(BF16), v_ref[head, low:high, :])
                if block:
                    weight = jnp.exp2(before * factor - shift)
                    total = total + jnp.sum(weight, axis=1, keepdims=True)
                    out = out + dot(weight.astype(BF16), v_ref[head, :low, :])
                o_ref[head, here, :] = (out * (1.0 / total)).astype(BF16)
                logs = jnp.broadcast_to(shift + jnp.log2(total), (rows, 128))
                log_ref[head, :, here] = logs.T[:1]

        for block in range(count):
            if block == count - 1:
                one(block, 0)
                continue
            wide = crosses(starts_ref, (block + 1) * rows)
            pl.when(wide)(functools.partial(one, block, 1))
            pl.when(jnp.logical_not(wide))(functools.partial(one, block, 0))

    spec = pl.BlockSpec((each, length, HDIM), lambda h: (h, 0, 0))
    return call(
        kernel,
        [jax.ShapeDtypeStruct(query.shape, BF16), jax.ShapeDtypeStruct((heads, 1, length), F32)],
        [smem(), spec, spec, spec],
        [spec, pl.BlockSpec((each, 1, length), lambda h: (h, 0, 0))],
        [pltpu.VMEM((count, rows, 2 * rows), F32)],
        4 * heads * length * length * HDIM * 4,
        16 * heads * length * HDIM,
        "attend",
        limit=32,
        grid=(heads // each,),
    )(starts, query, key, value)


def attend_back(
    starts, place, query, key, value, mixed, logs, near, far, cosine, sine, narrow, b_heads, rows, first, heads
):
    length = query.shape[1]
    thin = narrow.shape[0]
    rank = thin // 3
    count = length // rows
    scale = 1.0 / math.sqrt(HDIM)
    factor = LOG2E * scale

    def kernel(
        starts_ref, place_ref, q_ref, k_ref, v_ref, o_ref, log_ref, near_ref, far_ref, cos_ref, sin_ref,
        narrow_ref, b_ref, dq_ref, dk_ref, dv_ref, thin_ref, out_ref,
        bias, key_sum, value_sum, key_turned, query_sum,
    ):
        fill_bias(bias, starts_ref, rows)
        ones = jnp.ones((8, HDIM), BF16)
        for head in range(heads):
            key_turned[head] = k_ref[head].astype(F32).T.astype(BF16)

        def pair(head, query, keys, mask, new):
            q, g, logs, inner = query
            here = slice(keys * rows, (keys + 1) * rows)
            raw = dot_t(k_ref[head, here, :], q)
            if mask is not None:
                raw = raw + mask
            probs = jnp.exp2(raw * factor - logs)
            grad_probs = dot_t(v_ref[head, here, :], g)
            grad_scores = (probs * (grad_probs - inner)).astype(BF16)
            value_term = dot(probs.astype(BF16), g)
            key_term = dot(grad_scores, q)
            if new:
                value_sum[head, here, :] = value_term
                key_sum[head, here, :] = key_term
            else:
                value_sum[head, here, :] += value_term
                key_sum[head, here, :] += key_term
            return dot(key_turned[head, :, here], grad_scores)

        for block in reversed(range(count)):
            here = slice(block * rows, (block + 1) * rows)
            relative = place_ref[0] ^ block
            at = pl.multiple_of((relative % 2) * rows, rows)
            queries = []
            for head in range(heads):
                g = jnp.where(
                    relative < 2, near_ref[head, pl.ds(at, rows), :], far_ref[head, pl.ds(at, rows), :]
                )
                product = g.astype(F32) * o_ref[head, here, :].astype(F32)
                high = product.astype(BF16)
                low = (product - high.astype(F32)).astype(BF16)
                inner = (dot_t(ones, high) + dot_t(ones, low))[:1]
                queries.append((q_ref[head, here, :], g, log_ref[head, :, here], inner))
            last = block == count - 1
            totals = [pair(head, queries[head], block, bias[block, :rows, :], last) for head in range(heads)]
            for keys in range(block):
                for head in range(heads):
                    totals[head] = totals[head] + pair(head, queries[head], keys, None, last)
            if not last:
                for head in range(heads):
                    query_sum[head] = totals[head]

                @pl.when(crosses(starts_ref, (block + 1) * rows))
                def _():
                    for head in range(heads):
                        query_sum[head] += pair(head, queries[head], block + 1, bias[block, rows:, :], False)

                totals = [query_sum[head] for head in range(heads)]
            for head in range(heads):
                dq_ref[head, here, :] = turn(
                    totals[head].T * scale, cos_ref[here, :], -sin_ref[here, :]
                ).astype(BF16)
        thins = [None] * 3
        for head in range(heads):
            dk_ref[head] = turn(key_sum[head] * scale, cos_ref[...], -sin_ref[...]).astype(BF16)
            dv_ref[head] = value_sum[head].astype(BF16)
            for number, ref in enumerate((dq_ref, dk_ref, dv_ref)):
                here = slice(number * rank, (number + 1) * rank)
                term = dot_t(b_ref[head, here, :], ref[head])
                thins[number] = term if head == 0 else thins[number] + term
                out_ref[head, here, :] = dot(narrow_ref[here, :], ref[head])
        for number in range(3):
            thin_ref[number * rank : (number + 1) * rank, :] = thins[number]

    step = first // heads
    spec = pl.BlockSpec((heads, length, HDIM), lambda h: (step, 0, 0))
    half = pl.BlockSpec((heads, length // 2, HDIM), lambda h: (step, 0, 0))
    out = pl.BlockSpec((heads, length, HDIM), lambda h: (0, 0, 0))
    table = pl.BlockSpec((length, HDIM), lambda h: (0, 0))
    thin_spec = pl.BlockSpec((thin, length), lambda h: (0, 0))
    return call(
        kernel,
        [jax.ShapeDtypeStruct((heads, length, HDIM), BF16)] * 3
        + [
            jax.ShapeDtypeStruct((thin, length), F32),
            jax.ShapeDtypeStruct((heads, thin, HDIM), F32),
        ],
        [smem(), smem(), spec, spec, spec, spec]
        + [pl.BlockSpec((heads, 1, length), lambda h: (step, 0, 0)), half, half, table, table, thin_spec]
        + [pl.BlockSpec((heads, thin, HDIM), lambda h: (step, 0, 0))],
        [out] * 3 + [thin_spec, pl.BlockSpec((heads, thin, HDIM), lambda h: (0, 0, 0))],
        [
            pltpu.VMEM((count, 2 * rows, rows), F32),
            pltpu.VMEM((heads, length, HDIM), F32),
            pltpu.VMEM((heads, length, HDIM), F32),
            pltpu.VMEM((heads, HDIM, length), BF16),
            pltpu.VMEM((heads, HDIM, rows), F32),
        ],
        10 * heads * length * length * HDIM * 4,
        32 * heads * length * HDIM,
        "attend_back",
        limit=32,
        grid=(1,),
    )(
        starts, place[None], query, key, value, mixed, logs, near, far, cosine, sine, narrow, b_heads
    )


def rows_by_heads(refs, start, rows):
    return jnp.concatenate(
        [ref[head, pl.ds(start, rows), :] for ref in refs for head in range(ref.shape[0])], axis=1
    )


def close_attention(mixed, place, weight, a_out, wanted, rows):
    size, width = weight.shape
    rank = a_out.shape[0]

    def kernel(place_ref, m_ref, w_ref, a_ref, *outs):
        for block, out in zip(wanted, outs):
            start = pl.multiple_of((place_ref[0] ^ block) * rows, rows)
            here = rows_by_heads([m_ref], start, rows)
            out[:, :width] = dot(here, w_ref[...]).astype(BF16)
            narrow = dot_t(here, a_ref[...]).astype(BF16)
            out[:, width:] = jnp.concatenate(
                [narrow, jnp.zeros((rows, EXTRA - rank), BF16)], axis=1
            )

    return call(
        kernel,
        [jax.ShapeDtypeStruct((rows, width + EXTRA), BF16)] * len(wanted),
        [smem()] + [vmem()] * 3,
        [vmem()] * len(wanted),
        [],
        2 * rows * len(wanted) * size * width,
        2 * size * width + 2 * rows * len(wanted) * (width + size),
        "close_attention",
        limit=28,
    )(place[None], mixed, weight, a_out)


def open_attention(blocks, seconds, wanted, place, mixed, weight, a_out, b_out):
    rows, width_ext = blocks[0].shape
    size, width = weight.shape
    rank = a_out.shape[0]
    count = len(blocks)
    heads = size // HDIM

    def kernel(place_ref, *refs):
        g_refs, refs = refs[:count], refs[count:]
        s_refs, refs = refs[:count], refs[count:]
        m_ref, w_ref, a_ref, b_ref, out, sum_ref, wide_ref = refs
        total, branch, second = None, None, None
        for block in range(count):
            start = pl.multiple_of((place_ref[0] ^ wanted[block]) * rows, rows)
            grad = g_refs[block][:, :width]
            thin = g_refs[block][:, width:]
            narrow = dot_t(grad, b_ref[...]).astype(BF16)
            back = dot_t(grad, w_ref[...]) + dot(narrow, a_ref[...])
            for head in range(heads):
                part = back[:, head * HDIM : (head + 1) * HDIM]
                out[head, block * rows : (block + 1) * rows, :] = part.astype(BF16)
            terms = (
                t_dot(narrow, rows_by_heads([m_ref], start, rows)),
                t_dot(thin, grad)[:rank],
                t_dot(thin, s_refs[block][...])[rank : 3 * rank],
            )
            if block == 0:
                total, branch, second = terms
            else:
                total, branch, second = total + terms[0], branch + terms[1], second + terms[2]
        sum_ref[...] = total
        wide_ref[:rank, :] = branch
        wide_ref[rank:, :] = second

    return call(
        kernel,
        [
            jax.ShapeDtypeStruct((heads, rows * count, HDIM), BF16),
            jax.ShapeDtypeStruct((rank, size), F32),
            jax.ShapeDtypeStruct((3 * rank, width), F32),
        ],
        [smem()] + [vmem()] * (2 * count + 4),
        [vmem()] * 3,
        [],
        2 * rows * count * size * width,
        2 * size * width + 2 * rows * count * (2 * width + 2 * size),
        "open_attention",
        limit=32,
    )(place[None], *blocks, *seconds, mixed, weight, a_out, b_out)


def feed_forward(blocks, grads, offsets, pieces, down, a_mlp, b_down, a_hidden, b_hidden):
    rows, width = blocks[0].shape
    count = len(blocks)
    size = down.shape[0]
    rank = b_down.shape[0]
    n = len(pieces)

    def kernel(offsets_ref, *refs):
        x_refs, refs = refs[:count], refs[count:]
        g_refs, refs = refs[:count], refs[count:]
        piece_refs, refs = refs[:n], refs[n:]
        down_hbm, am_ref, bd_ref, ah_ref, bh_ref = refs[:5]
        refs = refs[5:]
        feed_refs, refs = refs[:count], refs[count:]
        back_refs, refs = refs[:count], refs[count:]
        sum_ref, whole, down_ref, grad_ref, sems, down_sem = refs
        down_copy = pltpu.make_async_copy(down_hbm, down_ref, down_sem)
        down_copy.start()
        copies = load_pieces(offsets_ref, piece_refs, whole, sems)
        x = jnp.concatenate([ref[...] for ref in x_refs], axis=0)
        grad = jnp.concatenate([ref[...] for ref in g_refs], axis=0)
        narrow = dot_t(x, am_ref[...]).astype(BF16)
        thin = dot_t(grad, bd_ref[...]).astype(BF16)
        down_copy.wait()
        grad_ref[...] = (dot_t(grad, down_ref[...]) + dot(thin, ah_ref[...])).astype(BF16)
        for copy in copies:
            copy.wait()
        gate = dot(x, whole[0]) + dot(narrow[:, :rank], bh_ref[0])
        up = dot(x, whole[1]) + dot(narrow[:, rank:], bh_ref[1])
        sigmoid = 0.5 + 0.5 * jnp.tanh(0.5 * gate)
        silu = gate * sigmoid
        hidden = (silu * up).astype(BF16)
        grad_hidden = grad_ref[...].astype(F32)
        grad_up = (grad_hidden * silu).astype(BF16)
        grad_gate = (grad_hidden * up * (sigmoid + silu * (1.0 - sigmoid))).astype(BF16)
        feed = dot(hidden, down_ref[...]).astype(BF16)
        feed_thin = dot_t(hidden, ah_ref[...]).astype(BF16)
        back = (dot_t(grad_gate, whole[0]) + dot_t(grad_up, whole[1])).astype(BF16)
        back_thin = jnp.concatenate(
            [dot_t(grad_gate, bh_ref[0]).astype(BF16), dot_t(grad_up, bh_ref[1]).astype(BF16)], axis=1
        )
        for block in range(count):
            here = slice(block * rows, (block + 1) * rows)
            feed_refs[block][:, :width] = feed[here]
            feed_refs[block][:, width:] = jnp.concatenate(
                [feed_thin[here], jnp.zeros((rows, EXTRA - rank), BF16)], axis=1
            )
            back_refs[block][:, :width] = back[here]
            back_refs[block][:, width:] = jnp.concatenate(
                [back_thin[here], jnp.zeros((rows, EXTRA - 2 * rank), BF16)], axis=1
            )
        sum_ref[:rank, :] = t_dot(thin, hidden)
        sum_ref[rank : 2 * rank, :] = t_dot(narrow[:, :rank], grad_gate)
        sum_ref[2 * rank :, :] = t_dot(narrow[:, rank:], grad_up)

    out = jax.ShapeDtypeStruct((rows, width + EXTRA), BF16)
    return call(
        kernel,
        [out] * (2 * count)
        + [jax.ShapeDtypeStruct((3 * rank, size), F32)],
        [smem()] + [vmem()] * (2 * count) + [anywhere()] * (n + 1) + [vmem()] * 4,
        [vmem()] * (2 * count + 1),
        [
            pltpu.VMEM((2, width, size), BF16),
            pltpu.VMEM((size, width), BF16),
            pltpu.VMEM((count * rows, size), BF16),
            pltpu.SemaphoreType.DMA((n,)),
            pltpu.SemaphoreType.DMA,
        ],
        12 * rows * count * width * size,
        6 * width * size + 8 * rows * count * width,
        "feed_forward",
    )(offsets, *blocks, *grads, *pieces, down, a_mlp, b_down, a_hidden, b_hidden)


def project_back(grads, place, offsets, pieces, wanted, rows):
    size = pieces[0].shape[1]
    width = 4 * pieces[0].shape[0]
    n = len(pieces)
    count = len(wanted)

    def kernel(place_ref, offsets_ref, *refs):
        g_refs, refs = refs[: len(grads)], refs[len(grads) :]
        piece_refs, refs = refs[:n], refs[n:]
        back_refs, (whole, sems) = refs[:count], refs[count:]
        copies = load_pieces(offsets_ref, piece_refs, whole, sems)
        starts = [pl.multiple_of((place_ref[0] ^ block) * rows, rows) for block in wanted]
        parts = [rows_by_heads(g_refs, start, rows) for start in starts]
        for copy in copies:
            copy.wait()
        for part, back in zip(parts, back_refs):
            back[...] = dot_t(part, whole[...]).astype(BF16)

    return call(
        kernel,
        [jax.ShapeDtypeStruct((rows, width), BF16)] * count,
        [smem(), smem()] + [vmem()] * len(grads) + [anywhere()] * n,
        [vmem()] * count,
        [pltpu.VMEM((width, size), BF16), pltpu.SemaphoreType.DMA((n,))],
        2 * rows * count * width * size,
        2 * (rows * count * (width + size) + width * size),
        "project_back",
        limit=56,
    )(place[None], offsets, *grads, *pieces)


def thin_product(thin, place, blocks):
    rows, width = blocks[0].shape
    count = len(blocks)

    def kernel(place_ref, thin_ref, *refs):
        total = None
        for block in range(count):
            start = pl.multiple_of((place_ref[0] ^ block) * rows, rows)
            term = dot(thin_ref[:, pl.ds(start, rows)], refs[block][...])
            total = term if total is None else total + term
        refs[count][...] = total

    return call(
        kernel,
        jax.ShapeDtypeStruct((thin.shape[0], width), F32),
        [smem()] + [vmem()] * (count + 1),
        vmem(),
        [],
        2 * 128 * rows * count * width,
        2 * rows * count * width,
        "thin_product",
        limit=24,
    )(place[None], thin, *blocks)


def shards(
    tokens,
    cotangent,
    sequence_adapter_index,
    image_span_start,
    attention_norm_gain,
    feedforward_norm_gain,
    query_key_value_weight,
    attention_output_weight,
    gate_up_projection_weight,
    down_projection_weight,
    adapter_model_input_maps,
    adapter_model_output_maps,
    adapter_hidden_input_map,
    adapter_hidden_output_maps,
):
    rows = tokens.shape[1]
    width = tokens.shape[2]
    rank = adapter_model_input_maps.shape[2]
    group = lax.axis_size("shard")
    place = lax.axis_index("shard").astype(jnp.int32)
    rep_place = lax.axis_index("rep").astype(jnp.int32)
    pick = sequence_adapter_index[0]
    starts = image_span_start[0]
    head_cols = width // group
    ff_cols = down_projection_weight.shape[0]
    k_rows = query_key_value_weight.shape[1]

    gain_one = attention_norm_gain.astype(F32)
    gain_two = feedforward_norm_gain.astype(F32)
    residual_in = tokens[0].astype(F32)
    grad_out = cotangent[0].astype(F32)

    def own_columns(values, size):
        return lax.dynamic_slice_in_dim(values, place * size, size, values.ndim - 1)

    quarter = k_rows // 4
    quarter_one, quarter_two = sides(
        query_key_value_weight, rep_place % 4 * quarter, quarter, place, head_cols, (2, 3), "sides_far"
    )
    first_a = hop(quarter_one, "shard", 2)
    normed = norm_rows(residual_in, gain_one).astype(BF16)
    front_chip, front_part = chip_picked(
        jnp.concatenate([adapter_model_input_maps[0:3], adapter_model_output_maps[0:3]]), pick, place
    )
    first_a, front_part, quarter_two, normed, qkv = fence(
        first_a, front_part, quarter_two, normed, query_key_value_weight
    )
    first_b = hop(quarter_two, "shard", 3)
    first_a_two, first_a_three = hop(first_a, "rep", 2), hop(first_a, "rep", 1)
    first_own, near_out = sides(qkv, 0, k_rows, place, head_cols, (0, 1), "sides_near")
    normed_near = core(normed)
    first_b, front_part, near_out, rest_bank, wide_bank = fence(
        first_b, front_part, near_out,
        (adapter_model_input_maps[3:6], adapter_model_output_maps[3:5]),
        (adapter_hidden_input_map[None], adapter_hidden_output_maps),
    )
    front_far = across(front_part)
    first_b_two, first_b_three = hop(first_b, "rep", 1), hop(first_b, "rep", 2)
    front_far, normed, first_a_two, first_a_three = fence(front_far, normed, first_a_two, first_a_three)
    normed_far = across(normed)
    first_a_four = hop(first_a_two, "rep", 1)
    first_near = core(near_out)
    rest_chip, rest_part = chip_picked(jnp.concatenate(rest_bank), pick, place)
    wide_chip, wide_part = chip_picked(jnp.concatenate(wide_bank), pick, place)
    first_b_two, first_b_three, gate_up, grad_out, front_chip = fence(
        first_b_two, first_b_three, gate_up_projection_weight, grad_out, front_chip
    )
    first_b_four = hop(first_b_two, "rep", 2)
    mlp_leaving = [side(gate_up, rep_place % 4 * quarter, quarter, place ^ j, ff_cols) for j in (2, 3)]
    grad_feed = (BRANCH * grad_out).astype(BF16)
    half = HDIM // 2
    frequency = jnp.exp(jnp.arange(half, dtype=F32) * (-2.0 / HDIM) * math.log(THETA))
    angle = jnp.arange(rows * group, dtype=jnp.int32).astype(F32)[:, None] * frequency[None, :]
    cosine = jnp.concatenate([jnp.cos(angle), jnp.cos(angle)], axis=1)
    sine = jnp.concatenate([jnp.sin(angle), jnp.sin(angle)], axis=1)
    cosine_pair = jnp.concatenate([jnp.cos(angle)] * 4, axis=1)
    sine_pair = jnp.concatenate([-jnp.sin(angle), jnp.sin(angle)] * 2, axis=1)
    tables = (cosine, sine, cosine_pair, sine_pair)
    front = whole_picked(front_chip, front_far, place)
    a_first = front[:3].reshape(3 * rank, width)
    b_first = own_columns(front[3:], head_cols)
    b_wide = jnp.concatenate(
        [jnp.pad(b_first[i], ((0, 0), (i * head_cols, (2 - i) * head_cols))) for i in range(3)]
    )
    normed_far, first_a_four, first_b_four, mlp_leaving, grad_feed, b_wide, a_first, rest_part, wide_part, tables = fence(
        normed_far, first_a_four, first_b_four, mlp_leaving, grad_feed, b_wide, a_first, rest_part, wide_part, tables
    )
    cosine, sine, cosine_pair, sine_pair = tables
    first_blocks = (normed, normed_near, normed_far, core(normed_far))
    first_offsets, first_pieces = arrange(
        k_rows, first_own, first_near,
        (
            (first_a, first_a_two, first_a_three, first_a_four),
            (first_b, first_b_two, first_b_three, first_b_four),
        ),
        place, rep_place,
    )

    mlp_a, mlp_b = hop(mlp_leaving[0], "shard", 2), hop(mlp_leaving[1], "shard", 3)
    query, key, value, narrow_first = project(
        first_blocks, place, first_offsets, first_pieces, a_first, b_wide, cosine_pair, sine_pair
    )
    query, mlp_a, rest_part, wide_part = fence(query, mlp_a, rest_part, wide_part)
    mlp_a_two, mlp_a_three = hop(mlp_a, "rep", 2), hop(mlp_a, "rep", 1)
    rest_far, wide_far = across(rest_part), across(wide_part)
    mixed, logs = attend(starts, query, key, value, rows)
    mixed, mlp_b, mlp_a_two, mlp_a_three, rest_far = fence(
        mixed, mlp_b, mlp_a_two, mlp_a_three, rest_far
    )
    mlp_b_two, mlp_b_three = hop(mlp_b, "rep", 1), hop(mlp_b, "rep", 2)
    rest = whole_picked(rest_chip, rest_far, place)
    a_out = own_columns(rest[0], head_cols)
    a_mlp = rest[1:3].reshape(2 * rank, width)
    b_out, b_down = rest[3], rest[4]
    far_out = close_attention(mixed, place, attention_output_weight, a_out, (2, 3), rows)
    far_sum = (far_out[0].astype(F32) + core(far_out[1]).astype(F32)).astype(BF16)
    far_sum, mixed_here, grad_feed, wide_far, gate_up = fence(far_sum, mixed, grad_feed, wide_far, gate_up)
    branch_far = across(far_sum)
    mlp_near_out = side(gate_up, 0, k_rows, place ^ 1, ff_cols)
    mlp_own = side(gate_up, 0, k_rows, place, ff_cols)
    feed_near_in = core(grad_feed)
    near_out = close_attention(mixed_here, place, attention_output_weight, a_out, (0, 1), rows)
    near_out, mlp_b_two, mlp_b_three, mlp_near_out, mlp_own = fence(
        near_out, mlp_b_two, mlp_b_three, mlp_near_out, mlp_own
    )
    mlp_a_four, mlp_b_four = hop(mlp_a_two, "rep", 1), hop(mlp_b_two, "rep", 2)
    near_here = core(near_out[1])
    mlp_near = core(mlp_near_out)
    hidden_cols = own_columns(whole_picked(wide_chip, wide_far, place), ff_cols)
    near_here, branch_far, hidden_cols, mlp_own, mlp_a_four, mlp_b_four = fence(
        near_here, branch_far, hidden_cols, mlp_own, mlp_a_four, mlp_b_four
    )
    feed_far_in = across(after(grad_feed, branch_far))
    a_hidden, b_hidden = hidden_cols[0], hidden_cols[1:]
    branch_own = near_out[0].astype(F32) + near_here.astype(F32) + branch_far.astype(F32)
    narrow_out = branch_own[:, width : width + rank].astype(BF16)
    branch = branch_own[:, :width] + dot(narrow_out, b_out)
    middle = residual_in + BRANCH * branch
    normed_second = norm_rows(middle, gain_two).astype(BF16)
    second_far = across(normed_second)
    second_near = core(normed_second)
    second_near, feed_near_in, mlp_near = fence(second_near, feed_near_in, mlp_near)
    mlp_offsets, mlp_pieces = arrange(
        k_rows, mlp_own, mlp_near,
        (
            (mlp_a, mlp_a_two, mlp_a_three, mlp_a_four),
            (mlp_b, mlp_b_two, mlp_b_three, mlp_b_four),
        ),
        place, rep_place,
    )
    *parts, sum_near = feed_forward(
        (normed_second, second_near), (grad_feed, feed_near_in), mlp_offsets, mlp_pieces,
        down_projection_weight, a_mlp, b_down, a_hidden, b_hidden,
    )
    feed_near, back_near = parts[:2], parts[2:]
    second_far, feed_far_in, back_near, feed_near = fence(second_far, feed_far_in, back_near, feed_near)
    second_blocks = (normed_second, second_near, second_far, core(second_far))
    feed_blocks = (grad_feed, feed_near_in, feed_far_in, core(feed_far_in))
    *parts, sum_far = feed_forward(
        second_blocks[2:], feed_blocks[2:], mlp_offsets, mlp_pieces, down_projection_weight,
        a_mlp, b_down, a_hidden, b_hidden,
    )
    feed_far, back_far = parts[:2], parts[2:]
    back_sum = (back_far[0].astype(F32) + core(back_far[1]).astype(F32)).astype(BF16)
    back_sum, back_near, feed_near, feed_far, sum_near = fence(
        back_sum, back_near, feed_near, feed_far, sum_near
    )
    back_from_far = across(back_sum)

    bits = reps_bits()
    back_here = core(back_near[1])
    feed_here = core(feed_near[1])
    feed_mate = core(feed_far[1])
    mark = jnp.full((rank, ff_cols), pick.astype(F32))
    wide_all = jnp.concatenate([sum_near + sum_far, mark]).astype(BF16)[None]
    wide_hop = hop(wide_all, "rep", bits[0])
    feed_here = feed_near[0].astype(F32) + feed_here.astype(F32)
    feed_sum = (feed_far[0].astype(F32) + feed_mate.astype(F32)).astype(BF16)
    back_from_far, feed_here, feed_sum, back_here, wide_hop = fence(
        back_from_far, feed_here, feed_sum, back_here, wide_hop
    )
    second_own = back_near[0].astype(F32) + back_here.astype(F32) + back_from_far.astype(F32)
    grad_narrow_mlp = second_own[:, width : width + 2 * rank].astype(BF16)
    grad_normed_second = second_own[:, :width] + dot(grad_narrow_mlp, a_mlp)
    grad_middle = grad_out + norm_back(middle, gain_two, grad_normed_second)
    grad_branch = (BRANCH * grad_middle).astype(BF16)
    branch_rows = pad_columns([grad_branch, narrow_out, grad_narrow_mlp], width + EXTRA)
    branch_rows, wide_hop = fence(branch_rows, wide_hop)
    branch_far_in = across(branch_rows)
    branch_near_in = core(branch_rows)
    wide_all = both(wide_all, wide_hop, rep_place, bits[0])
    for bit in bits[1:-2]:
        wide_all = both(wide_all, hop(wide_all, "rep", bit), rep_place, bit)
    wide_hop = hop(wide_all, "rep", bits[-2])
    branch_near_in, wide_all = fence(branch_near_in, wide_all)
    mixed_near, grad_a_near, thin_near = open_attention(
        (branch_rows, branch_near_in), second_blocks[:2], (0, 1), place, mixed,
        attention_output_weight, a_out, b_out,
    )
    branch_far_in, mixed_near = fence(branch_far_in, mixed_near)
    feed_from_far = across(after(feed_sum, branch_far_in))
    mixed_far, grad_a_far, thin_far = open_attention(
        (branch_far_in, core(branch_far_in)), second_blocks[2:], (2, 3), place, mixed,
        attention_output_weight, a_out, b_out,
    )

    b_heads = b_first.reshape(3 * rank, head_cols // HDIM, HDIM).transpose(1, 0, 2)

    def attend_part(first, heads, starts):
        return attend_back(
            starts, place, query, key, value, mixed, logs, mixed_near, mixed_far, cosine, sine,
            narrow_first, b_heads, rows, first, heads,
        )

    mixed_far, starts_one = fence(mixed_far, starts)
    heads = query.shape[0]
    third = heads // 3
    part_one = attend_part(0, third, starts_one)
    part_one, feed_from_far, wide_hop, starts_two = fence(part_one, feed_from_far, wide_hop, starts_one)
    wide_all = both(wide_all, wide_hop, rep_place, bits[-2])
    wide_hop = hop(wide_all, "rep", bits[-1])
    feed_own = feed_here + feed_from_far.astype(F32)
    narrow_down = feed_own[:, width : width + rank].astype(BF16)
    down_far = across(narrow_down)
    down_near = core(narrow_down)
    starts_two, narrow_down = fence(starts_two, narrow_down)
    part_two = attend_part(third, third, starts_two)
    part_two, wide_hop, down_far, down_near, starts_three = fence(
        part_two, wide_hop, down_far, down_near, starts_two
    )
    down_thin = (narrow_down, down_near, down_far, core(down_far))
    wide_all = both(wide_all, wide_hop, rep_place, bits[-1])
    picks = wide_all[:, -1, :1].astype(F32)
    adapters = adapter_model_input_maps.shape[1] * group
    chosen = (picks == jnp.arange(adapters, dtype=jnp.int32).astype(F32)[None, :]).astype(F32)
    wide_sent = send_sums(wide_all[:, :-rank], chosen, place)
    grad_b_down = sum(t_dot(left, right) for left, right in zip(down_thin, feed_blocks))
    early_all = jnp.concatenate(
        [
            grad_a_near + grad_a_far,
            own_columns(jnp.concatenate([thin_near + thin_far, grad_b_down]), head_cols),
        ]
    ).astype(BF16)[None]
    early_hop = hop(early_all, "rep", bits[0])
    early_all, starts_three = fence(early_all, starts_three)
    part_three = attend_part(2 * third, heads - 2 * third, starts_three)
    part_three, early_hop, wide_sent = fence(part_three, early_hop, wide_sent)
    parts = (part_one, part_two, part_three)
    first_grads = [part[number] for number in range(3) for part in parts]
    thin = (part_one[3] + part_two[3] + part_three[3]).astype(BF16)
    thin_hop = core(thin)
    early_all = both(early_all, early_hop, rep_place, bits[0])
    for bit in bits[1:-2]:
        early_all = both(early_all, hop(early_all, "rep", bit), rep_place, bit)
    early_hop = hop(early_all, "rep", bits[-2])
    thin = (thin.astype(F32) + thin_hop.astype(F32)).astype(BF16)
    thin, first_grads, early_all = fence(thin, first_grads, early_all)
    thin_hop = across(thin)
    back_rows_far = project_back(first_grads, place, first_offsets, first_pieces, (2, 3), rows)
    back_rows_far, thin_hop, early_hop = fence(back_rows_far, thin_hop, early_hop)
    back_mate = core(back_rows_far[1])
    grad_narrow = (thin.astype(F32) + thin_hop.astype(F32)).astype(BF16)
    grad_b_first = jnp.concatenate([part[4] for part in parts]).transpose(1, 0, 2)
    late_all = jnp.concatenate(
        [
            own_columns(thin_product(grad_narrow, place, first_blocks), head_cols),
            grad_b_first.reshape(3 * rank, head_cols),
        ]
    ).astype(BF16)[None]
    late_all, grad_narrow, back_mate, early_all, early_hop = fence(
        late_all, grad_narrow, back_mate, early_all, early_hop
    )
    late_hop = hop(late_all, "rep", bits[0])
    back_sum = (back_rows_far[0].astype(F32) + back_mate.astype(F32)).astype(BF16)
    early_all = both(early_all, early_hop, rep_place, bits[-2])
    early_hop = hop(early_all, "rep", bits[-1])
    back_sum, grads_here, early_all = fence(back_sum, first_grads, early_all)
    back_far_in = across(back_sum)
    back_rows_near = project_back(grads_here, place, first_offsets, first_pieces, (0, 1), rows)
    late_hop, back_rows_near, early_hop = fence(late_hop, back_rows_near, early_hop)
    back_rows_here = core(back_rows_near[1])
    late_all = both(late_all, late_hop, rep_place, bits[0])
    for bit in bits[1:-2]:
        late_all = both(late_all, hop(late_all, "rep", bit), rep_place, bit)
    late_hop = hop(late_all, "rep", bits[-2])
    late_all, early_hop, early_all = fence(late_all, early_hop, early_all)
    early_sent = send_sums(both(early_all, early_hop, rep_place, bits[-1]), chosen, place)

    def whole_maps(stacked, low, high, n):
        part = stacked[:, :, low:high].reshape(group, stacked.shape[1], -1, rank, n)
        pieces = [lax.dynamic_index_in_dim(part, place ^ i, 0, keepdims=False) for i in range(group)]
        return jnp.concatenate(pieces, axis=-1).transpose(1, 0, 2, 3).astype(F32)

    feed = feed_here[:, :width] + feed_from_far[:, :width].astype(F32) + dot(narrow_down, b_down)
    output = (middle + BRANCH * feed).astype(BF16)
    late_hop, output = fence(late_hop, output)
    late_all = both(late_all, late_hop, rep_place, bits[-2])
    late_hop = hop(late_all, "rep", bits[-1])
    hidden_maps = whole_maps(jnp.stack(wide_sent), 0, 3 * rank, ff_cols)
    late_hop, hidden_maps, back_far_in = fence(late_hop, hidden_maps, back_far_in)
    late_sent = send_sums(both(late_all, late_hop, rep_place, bits[-1]), chosen, place)
    narrow_own = lax.dynamic_slice_in_dim(grad_narrow, place * rows, rows, 1)
    grad_normed = (
        back_rows_near[0].astype(F32) + back_rows_here.astype(F32) + back_far_in.astype(F32)
        + t_dot(narrow_own, a_first)
    )
    input_grad = grad_middle + norm_back(residual_in, gain_one, grad_normed)
    early_got = jnp.stack(early_sent)
    late_sent, input_grad, early_got = fence(late_sent, input_grad, early_got)
    late_got = jnp.stack(late_sent)
    grad_a_model = jnp.concatenate(
        [
            whole_maps(late_got, 0, 3 * rank, head_cols),
            whole_maps(early_got, 0, rank, head_cols),
            whole_maps(early_got, 2 * rank, 4 * rank, head_cols),
        ]
    )
    grad_b_model = jnp.concatenate(
        [
            whole_maps(late_got, 3 * rank, 6 * rank, head_cols),
            whole_maps(early_got, rank, 2 * rank, head_cols),
            whole_maps(early_got, 4 * rank, 5 * rank, head_cols),
        ]
    )
    return (
        output[None], input_grad[None], grad_a_model, grad_b_model, hidden_maps[0], hidden_maps[1:3],
    )


def solution(mesh):
    in_specs = (
        P("rep", "shard", None),
        P("rep", "shard", None),
        P("rep"),
        P("rep", None),
        P(),
        P(),
        P(None, "shard", None),
        P("shard", None),
        P(None, "shard", None),
        P("shard", None),
        P(None, "shard", None, None),
        P(None, "shard", None, None),
        P("shard", None, None),
        P(None, "shard", None, None),
    )
    out_specs = (
        P("rep", "shard", None),
        P("rep", "shard", None),
        P(None, "shard", None, None),
        P(None, "shard", None, None),
        P("shard", None, None),
        P(None, "shard", None, None),
    )
    return jax.shard_map(shards, mesh=mesh, in_specs=in_specs, out_specs=out_specs, check_vma=False)
```

```python
import functools
import math

import jax
import jax.numpy as jnp
from jax import lax
from jax.experimental import pallas as pl
from jax.experimental.pallas import tpu as pltpu
from jax.sharding import PartitionSpec as P

HDIM = 64
SPAN = 256
EPS = 1e-05
THETA = 10000.0
BRANCH = 1.4 / math.sqrt(40.0)
EXTRA = 128
F32 = jnp.float32
BF16 = jnp.bfloat16
LOG2E = math.log2(math.e)


def hop(values, axis, bit):
    size = lax.axis_size(axis)
    return lax.ppermute(values, axis, [(i, i ^ bit) for i in range(size)])


def core(values):
    return hop(values, "shard", 1)


def across(values):
    return hop(values, "shard", 2)


def rows_of(values, count):
    size = values.shape[0] // count
    return tuple(values[i * size : (i + 1) * size] for i in range(count))


def norm_rows(values, gain):
    return values * lax.rsqrt(jnp.mean(values * values, axis=-1, keepdims=True) + EPS) * gain


def norm_back(values, gain, grad):
    width = values.shape[-1]
    scale = lax.rsqrt(jnp.mean(values * values, axis=-1, keepdims=True) + EPS)
    moved = grad * gain
    inner = jnp.sum(values * moved, axis=-1, keepdims=True) / width
    return scale * moved - values * (scale * scale * scale) * inner


def dot(left, right):
    return jnp.dot(left, right, preferred_element_type=F32)


def dot_t(left, right):
    return lax.dot_general(left, right, (((1,), (1,)), ((), ())), preferred_element_type=F32)


def t_dot(left, right):
    return lax.dot_general(left, right, (((0,), (0,)), ((), ())), preferred_element_type=F32)


def pad_columns(pieces, width):
    used = sum(piece.shape[1] for piece in pieces)
    rest = jnp.zeros((pieces[0].shape[0], width - used), pieces[0].dtype)
    return jnp.concatenate(list(pieces) + [rest], axis=1)


def reps_bits():
    bits = []
    bit = 2
    while bit < lax.axis_size("rep"):
        bits.append(bit)
        bit *= 2
    return bits + [1]


def both(held, arrived, rep_place, bit):
    low = jnp.concatenate([held, arrived])
    high = jnp.concatenate([arrived, held])
    return jnp.where((rep_place // bit) % 2 == 0, low, high)


def send_sums(everyone, chosen, place):
    group = lax.axis_size("shard")
    per = chosen.shape[1] // group
    sent = []
    for j in range(group):
        marks = lax.dynamic_slice_in_dim(chosen, (place ^ j) * per, per, 1)
        sums = jnp.sum(marks[:, :, None, None] * everyone[:, None].astype(F32), axis=0).astype(BF16)
        sent.append(hop(sums, "shard", j) if j else sums)
    return sent


def chip_picked(bank, pick, place):
    per = bank.shape[1]
    rank = bank.shape[2]
    owner = pick // per
    mine = lax.dynamic_index_in_dim(bank, pick % per, 1, keepdims=False)
    mine = jnp.where(owner == place, mine, jnp.zeros_like(mine))
    chip = mine + core(mine)
    return chip, lax.dynamic_slice_in_dim(chip, (place % 2) * (rank // 2), rank // 2, 1)


def whole_picked(chip, far, place):
    other = core(far)
    low = jnp.where(place % 2 == 0, far, other)
    high = jnp.where(place % 2 == 0, other, far)
    return chip + jnp.concatenate([low, high], axis=1)


def after(value, *others):
    return lax.optimization_barrier((value, others))[0]


def side(weight, row, count, owner, size):
    return lax.dynamic_slice(weight, (0, row, owner * size), (weight.shape[0], count, size))


def sides(weight, row, count, place, size, wanted, name):
    maps, _, columns = weight.shape

    def kernel(where_ref, w_ref, *refs):
        outs, (held, sem) = refs[:-2], refs[-2:]
        start = pl.multiple_of(where_ref[1], 16)
        copy = pltpu.make_async_copy(w_ref.at[:, pl.ds(start, count), :], held, sem)
        copy.start()
        copy.wait()

        def write(out, owner):
            out[...] = jnp.concatenate(
                [held[i, :, owner * size : (owner + 1) * size] for i in range(maps)], axis=1
            )

        for j, out in zip(wanted, outs):
            for owner in range(columns // size):
                pl.when((where_ref[0] ^ j) == owner)(functools.partial(write, out, owner))

    return call(
        kernel,
        [jax.ShapeDtypeStruct((count, maps * size), BF16)] * len(wanted),
        [smem(), anywhere()],
        [vmem()] * len(wanted),
        [pltpu.VMEM((maps, count, columns), BF16), pltpu.SemaphoreType.DMA],
        0,
        2 * maps * count * (columns + size * len(wanted)),
        name,
        limit=58,
    )(jnp.stack([place, jnp.asarray(row, jnp.int32)]), weight)


def arrange(rows, own, near, ways, place, rep_place):
    quarter = rows // 4
    part = rep_place % 4
    pieces = [(place * rows, own), ((place ^ 1) * rows, near)]
    for j, one, two, parts in zip((2, 3), (2, 1), (1, 2), ways):
        for bits, piece in zip((0, one, two, one ^ two), parts):
            pieces.append(((place ^ j) * rows + (part ^ bits) * quarter, piece))
    offsets = jnp.stack([row.astype(jnp.int32) for row, _ in pieces])
    return offsets, [piece for _, piece in pieces]


def fence(*values):
    return lax.optimization_barrier(values)


def load_pieces(offsets, pieces, whole, sems):
    copies = []
    for number, piece in enumerate(pieces):
        start = pl.multiple_of(offsets[number], 16)
        here = pl.ds(start, piece.shape[-2])
        target = whole.at[here, :] if len(piece.shape) == 2 else whole.at[:, here, :]
        copy = pltpu.make_async_copy(piece, target, sems.at[number])
        copy.start()
        copies.append(copy)
    return copies


def vmem():
    return pl.BlockSpec(memory_space=pltpu.VMEM)


def smem():
    return pl.BlockSpec(memory_space=pltpu.SMEM)


def anywhere():
    return pl.BlockSpec(memory_space=pl.ANY)


def call(kernel, outs, in_specs, out_specs, scratch, flops, moved, name, limit=56, **more):
    return pl.pallas_call(
        kernel,
        out_shape=outs,
        in_specs=in_specs,
        out_specs=out_specs,
        scratch_shapes=scratch,
        compiler_params=pltpu.CompilerParams(vmem_limit_bytes=limit << 20),
        cost_estimate=pl.CostEstimate(flops=flops, bytes_accessed=moved, transcendentals=0),
        name=name,
        **more,
    )


def turn(values, cosine, sine):
    half = HDIM // 2
    turned = jnp.concatenate([-values[:, half:], values[:, :half]], axis=1)
    return values * cosine + turned * sine


def project(blocks, place, offsets, pieces, a_first, b_first, cosine_pair, sine_pair):
    rows, width = blocks[0].shape
    count = len(blocks)
    size = pieces[0].shape[1]
    heads = size // (3 * HDIM)
    thin = a_first.shape[0]
    n = len(pieces)

    def kernel(place_ref, offsets_ref, *refs):
        x_refs, refs = refs[:count], refs[count:]
        piece_refs, refs = refs[:n], refs[n:]
        a_ref, b_ref, cos_ref, sin_ref, q_ref, k_ref, v_ref, narrow_ref, whole, sems = refs
        copies = load_pieces(offsets_ref, piece_refs, whole, sems)
        starts = [pl.multiple_of((place_ref[0] ^ block) * rows, rows) for block in range(count)]
        for block in range(count):
            narrow_ref[:, pl.ds(starts[block], rows)] = dot_t(a_ref[...], x_refs[block][...]).astype(BF16)
        for copy in copies:
            copy.wait()
        both = 2 * heads * HDIM
        lane = lax.broadcasted_iota(jnp.int32, (rows, both), 1) % HDIM
        lower = lane < HDIM // 2
        for block in range(count):
            start = starts[block]
            narrow = narrow_ref[:, pl.ds(start, rows)]
            pre = dot(x_refs[block][...], whole[...]) + t_dot(narrow, b_ref[...])
            flat = pre[:, :both]
            cosine_here = jnp.tile(cos_ref[pl.ds(start, rows), :], (1, both // (2 * HDIM)))
            sine_here = jnp.tile(sin_ref[pl.ds(start, rows), :], (1, both // (2 * HDIM)))
            other = jnp.where(
                lower, pltpu.roll(flat, both - HDIM // 2, 1), pltpu.roll(flat, HDIM // 2, 1)
            )
            turned = (flat * cosine_here + other * sine_here).astype(BF16)
            straight = pre[:, both:].astype(BF16)
            for number, out in enumerate((q_ref, k_ref, v_ref)):
                for head in range(heads):
                    at = (number % 2 * heads + head) * HDIM
                    source = turned if number < 2 else straight
                    out[head, pl.ds(start, rows), :] = source[:, at : at + HDIM]

    by_heads = jax.ShapeDtypeStruct((heads, rows * count, HDIM), BF16)
    return call(
        kernel,
        [by_heads] * 3 + [jax.ShapeDtypeStruct((thin, rows * count), BF16)],
        [smem(), smem()] + [vmem()] * count + [anywhere()] * n + [vmem()] * 4,
        [vmem()] * 4,
        [pltpu.VMEM((width, size), BF16), pltpu.SemaphoreType.DMA((n,))],
        2 * rows * count * width * size,
        2 * (rows * count * width + width * size + 2 * rows * count * size),
        "project",
        limit=56,
    )(place[None], offsets, *blocks, *pieces, a_first, b_first, cosine_pair, sine_pair)


def label_of(positions, starts_ref):
    label = jnp.full(positions.shape, -1, jnp.int32)
    for number in range(starts_ref.shape[0]):
        inside = (positions >= starts_ref[number]) & (positions < starts_ref[number] + SPAN)
        label = jnp.where(inside, jnp.int32(number), label)
    return label


def hidden_bias(query_at, key_at, starts_ref):
    query_label = label_of(query_at, starts_ref)
    key_label = label_of(key_at, starts_ref)
    visible = (key_at <= query_at) | (query_label == key_label) & (query_label >= 0)
    return jnp.where(visible, 0.0, -1e30)


def crosses(starts_ref, edge):
    hit = None
    for number in range(starts_ref.shape[0]):
        start = starts_ref[number]
        here = (start < edge) & (start + SPAN > edge)
        hit = here if hit is None else hit | here
    return hit


def fill_bias(bias, starts_ref, rows):
    for block in range(bias.shape[0]):
        shape = (2 * rows, rows)
        query_at = block * rows + lax.broadcasted_iota(jnp.int32, shape, 1)
        key_at = block * rows + lax.broadcasted_iota(jnp.int32, shape, 0)
        bias[block] = hidden_bias(query_at, key_at, starts_ref)


def attend(starts, query, key, value, rows):
    heads, length, _ = query.shape
    count = length // rows
    factor = LOG2E / math.sqrt(HDIM)
    each = 3

    def kernel(starts_ref, q_ref, k_ref, v_ref, o_ref, log_ref, bias):
        @pl.when(pl.program_id(0) == 0)
        def _():
            for block in range(count):
                shape = (rows, 2 * rows)
                query_at = block * rows + lax.broadcasted_iota(jnp.int32, shape, 0)
                key_at = block * rows + lax.broadcasted_iota(jnp.int32, shape, 1)
                bias[block] = hidden_bias(query_at, key_at, starts_ref)

        def one(block, extra):
            low, high = block * rows, (block + 1 + extra) * rows
            here = slice(low, low + rows)
            states = []
            for head in range(each):
                q = q_ref[head, here, :]
                edge = dot_t(q, k_ref[head, low:high, :]) + bias[block, :, : high - low]
                before = dot_t(q, k_ref[head, :low, :]) if block else None
                states.append((edge, before))
            for head, (edge, before) in enumerate(states):
                top = jnp.max(edge, axis=1, keepdims=True)
                if block:
                    top = jnp.maximum(top, jnp.max(before, axis=1, keepdims=True))
                shift = top * factor
                weight = jnp.exp2(edge * factor - shift)
                total = jnp.sum(weight, axis=1, keepdims=True)
                out = dot(weight.astype(BF16), v_ref[head, low:high, :])
                if block:
                    weight = jnp.exp2(before * factor - shift)
                    total = total + jnp.sum(weight, axis=1, keepdims=True)
                    out = out + dot(weight.astype(BF16), v_ref[head, :low, :])
                o_ref[head, here, :] = (out * (1.0 / total)).astype(BF16)
                logs = jnp.broadcast_to(shift + jnp.log2(total), (rows, 128))
                log_ref[head, :, here] = logs.T[:1]

        for block in range(count):
            if block == count - 1:
                one(block, 0)
                continue
            wide = crosses(starts_ref, (block + 1) * rows)
            pl.when(wide)(functools.partial(one, block, 1))
            pl.when(jnp.logical_not(wide))(functools.partial(one, block, 0))

    spec = pl.BlockSpec((each, length, HDIM), lambda h: (h, 0, 0))
    return call(
        kernel,
        [jax.ShapeDtypeStruct(query.shape, BF16), jax.ShapeDtypeStruct((heads, 1, length), F32)],
        [smem(), spec, spec, spec],
        [spec, pl.BlockSpec((each, 1, length), lambda h: (h, 0, 0))],
        [pltpu.VMEM((count, rows, 2 * rows), F32)],
        4 * heads * length * length * HDIM * 4,
        16 * heads * length * HDIM,
        "attend",
        limit=56,
        grid=(heads // each,),
    )(starts, query, key, value)


def attend_back(
    starts, place, query, key, value, mixed, logs, near, far, cosine, sine, narrow, b_heads, rows, first, heads
):
    length = query.shape[1]
    thin = narrow.shape[0]
    rank = thin // 3
    count = length // rows
    scale = 1.0 / math.sqrt(HDIM)
    factor = LOG2E * scale

    def kernel(
        starts_ref, place_ref, q_ref, k_ref, v_ref, o_ref, log_ref, near_ref, far_ref, cos_ref, sin_ref,
        narrow_ref, b_ref, dq_ref, dk_ref, dv_ref, thin_ref, out_ref,
        bias, key_sum, value_sum, key_turned, query_sum,
    ):
        fill_bias(bias, starts_ref, rows)
        ones = jnp.ones((8, HDIM), BF16)
        for head in range(heads):
            key_turned[head] = k_ref[head].astype(F32).T.astype(BF16)

        def pair(head, query, keys, mask, new):
            q, g, logs, inner = query
            here = slice(keys * rows, (keys + 1) * rows)
            raw = dot_t(k_ref[head, here, :], q)
            if mask is not None:
                raw = raw + mask
            probs = jnp.exp2(raw * factor - logs)
            grad_probs = dot_t(v_ref[head, here, :], g)
            grad_scores = (probs * (grad_probs - inner)).astype(BF16)
            value_term = dot(probs.astype(BF16), g)
            key_term = dot(grad_scores, q)
            if new:
                value_sum[head, here, :] = value_term
                key_sum[head, here, :] = key_term
            else:
                value_sum[head, here, :] += value_term
                key_sum[head, here, :] += key_term
            return dot(key_turned[head, :, here], grad_scores)

        for block in reversed(range(count)):
            here = slice(block * rows, (block + 1) * rows)
            relative = place_ref[0] ^ block
            at = pl.multiple_of((relative % 2) * rows, rows)
            queries = []
            for head in range(heads):
                g = jnp.where(
                    relative < 2, near_ref[head, pl.ds(at, rows), :], far_ref[head, pl.ds(at, rows), :]
                )
                product = g.astype(F32) * o_ref[head, here, :].astype(F32)
                high = product.astype(BF16)
                low = (product - high.astype(F32)).astype(BF16)
                inner = (dot_t(ones, high) + dot_t(ones, low))[:1]
                queries.append((q_ref[head, here, :], g, log_ref[head, :, here], inner))
            last = block == count - 1
            totals = [pair(head, queries[head], block, bias[block, :rows, :], last) for head in range(heads)]
            for keys in range(block):
                for head in range(heads):
                    totals[head] = totals[head] + pair(head, queries[head], keys, None, last)
            if not last:
                for head in range(heads):
                    query_sum[head] = totals[head]

                @pl.when(crosses(starts_ref, (block + 1) * rows))
                def _():
                    for head in range(heads):
                        query_sum[head] += pair(head, queries[head], block + 1, bias[block, rows:, :], False)

                totals = [query_sum[head] for head in range(heads)]
            for head in range(heads):
                dq_ref[head, here, :] = turn(
                    totals[head].T * scale, cos_ref[here, :], -sin_ref[here, :]
                ).astype(BF16)
        thins = [None] * 3
        sums = [[], [], []]
        for head in range(heads):
            dk_ref[head] = turn(key_sum[head] * scale, cos_ref[...], -sin_ref[...]).astype(BF16)
            dv_ref[head] = value_sum[head].astype(BF16)
            for number, ref in enumerate((dq_ref, dk_ref, dv_ref)):
                here = slice(number * rank, (number + 1) * rank)
                term = dot_t(b_ref[head, here, :], ref[head])
                thins[number] = term if head == 0 else thins[number] + term
                sums[number].append(dot(narrow_ref[here, :], ref[head]))
        for number in range(3):
            here = slice(number * rank, (number + 1) * rank)
            thin_ref[here, :] = thins[number]
            out_ref[here, :] = jnp.concatenate(sums[number], axis=1)

    step = first // heads
    spec = pl.BlockSpec((heads, length, HDIM), lambda h: (step, 0, 0))
    half = pl.BlockSpec((heads, length // 2, HDIM), lambda h: (step, 0, 0))
    out = pl.BlockSpec((heads, length, HDIM), lambda h: (0, 0, 0))
    table = pl.BlockSpec((length, HDIM), lambda h: (0, 0))
    thin_spec = pl.BlockSpec((thin, length), lambda h: (0, 0))
    return call(
        kernel,
        [jax.ShapeDtypeStruct((heads, length, HDIM), BF16)] * 3
        + [
            jax.ShapeDtypeStruct((thin, length), F32),
            jax.ShapeDtypeStruct((thin, heads * HDIM), F32),
        ],
        [smem(), smem(), spec, spec, spec, spec]
        + [pl.BlockSpec((heads, 1, length), lambda h: (step, 0, 0)), half, half, table, table, thin_spec]
        + [pl.BlockSpec((heads, thin, HDIM), lambda h: (step, 0, 0))],
        [out] * 3 + [thin_spec, pl.BlockSpec((thin, heads * HDIM), lambda h: (0, 0))],
        [
            pltpu.VMEM((count, 2 * rows, rows), F32),
            pltpu.VMEM((heads, length, HDIM), F32),
            pltpu.VMEM((heads, length, HDIM), F32),
            pltpu.VMEM((heads, HDIM, length), BF16),
            pltpu.VMEM((heads, HDIM, rows), F32),
        ],
        10 * heads * length * length * HDIM * 4,
        32 * heads * length * HDIM,
        "attend_back",
        limit=32,
        grid=(1,),
    )(
        starts, place[None], query, key, value, mixed, logs, near, far, cosine, sine, narrow, b_heads
    )


def rows_by_heads(refs, start, rows):
    return jnp.concatenate(
        [ref[head, pl.ds(start, rows), :] for ref in refs for head in range(ref.shape[0])], axis=1
    )


def close_attention(mixed, place, weight, a_out, wanted, rows):
    size, width = weight.shape
    rank = a_out.shape[0]

    def kernel(place_ref, m_ref, w_ref, a_ref, *outs):
        for block, out in zip(wanted, outs):
            start = pl.multiple_of((place_ref[0] ^ block) * rows, rows)
            here = rows_by_heads([m_ref], start, rows)
            out[:, :width] = dot(here, w_ref[...]).astype(BF16)
            narrow = dot_t(here, a_ref[...]).astype(BF16)
            out[:, width:] = jnp.concatenate(
                [narrow, jnp.zeros((rows, EXTRA - rank), BF16)], axis=1
            )

    return call(
        kernel,
        [jax.ShapeDtypeStruct((rows, width + EXTRA), BF16)] * len(wanted),
        [smem()] + [vmem()] * 3,
        [vmem()] * len(wanted),
        [],
        2 * rows * len(wanted) * size * width,
        2 * size * width + 2 * rows * len(wanted) * (width + size),
        "close_attention",
        limit=28,
    )(place[None], mixed, weight, a_out)


def open_attention(blocks, seconds, wanted, place, mixed, weight, a_out, b_out):
    rows, width_ext = blocks[0].shape
    size, width = weight.shape
    rank = a_out.shape[0]
    count = len(blocks)
    heads = size // HDIM

    def kernel(place_ref, *refs):
        g_refs, refs = refs[:count], refs[count:]
        s_refs, refs = refs[:count], refs[count:]
        m_ref, w_ref, a_ref, b_ref, out, sum_ref, wide_ref = refs
        total, branch, second = None, None, None
        for block in range(count):
            start = pl.multiple_of((place_ref[0] ^ wanted[block]) * rows, rows)
            grad = g_refs[block][:, :width]
            thin = g_refs[block][:, width:]
            narrow = dot_t(grad, b_ref[...]).astype(BF16)
            back = dot_t(grad, w_ref[...]) + dot(narrow, a_ref[...])
            for head in range(heads):
                part = back[:, head * HDIM : (head + 1) * HDIM]
                out[head, block * rows : (block + 1) * rows, :] = part.astype(BF16)
            terms = (
                t_dot(narrow, rows_by_heads([m_ref], start, rows)),
                t_dot(thin, grad)[:rank],
                t_dot(thin, s_refs[block][...])[rank : 3 * rank],
            )
            if block == 0:
                total, branch, second = terms
            else:
                total, branch, second = total + terms[0], branch + terms[1], second + terms[2]
        sum_ref[...] = total
        wide_ref[:rank, :] = branch
        wide_ref[rank:, :] = second

    return call(
        kernel,
        [
            jax.ShapeDtypeStruct((heads, rows * count, HDIM), BF16),
            jax.ShapeDtypeStruct((rank, size), F32),
            jax.ShapeDtypeStruct((3 * rank, width), F32),
        ],
        [smem()] + [vmem()] * (2 * count + 4),
        [vmem()] * 3,
        [],
        2 * rows * count * size * width,
        2 * size * width + 2 * rows * count * (2 * width + 2 * size),
        "open_attention",
        limit=32,
    )(place[None], *blocks, *seconds, mixed, weight, a_out, b_out)


def feed_forward(blocks, grads, offsets, pieces, down, a_mlp, b_down, a_hidden, b_hidden):
    rows, width = blocks[0].shape
    count = len(blocks)
    size = down.shape[0]
    rank = b_down.shape[0]
    n = len(pieces)

    def kernel(offsets_ref, *refs):
        x_refs, refs = refs[:count], refs[count:]
        g_refs, refs = refs[:count], refs[count:]
        piece_refs, refs = refs[:n], refs[n:]
        down_hbm, am_ref, bd_ref, ah_ref, bh_ref = refs[:5]
        refs = refs[5:]
        feed_refs, refs = refs[:count], refs[count:]
        back_refs, refs = refs[:count], refs[count:]
        sum_ref, whole, down_ref, grad_ref, sems, down_sem = refs
        down_copy = pltpu.make_async_copy(down_hbm, down_ref, down_sem)
        down_copy.start()
        copies = load_pieces(offsets_ref, piece_refs, whole, sems)
        x = jnp.concatenate([ref[...] for ref in x_refs], axis=0)
        grad = jnp.concatenate([ref[...] for ref in g_refs], axis=0)
        narrow = dot_t(x, am_ref[...]).astype(BF16)
        thin = dot_t(grad, bd_ref[...]).astype(BF16)
        down_copy.wait()
        grad_ref[...] = (dot_t(grad, down_ref[...]) + dot(thin, ah_ref[...])).astype(BF16)
        for copy in copies:
            copy.wait()
        gate = dot(x, whole[0]) + dot(narrow[:, :rank], bh_ref[0])
        up = dot(x, whole[1]) + dot(narrow[:, rank:], bh_ref[1])
        sigmoid = 0.5 + 0.5 * jnp.tanh(0.5 * gate)
        silu = gate * sigmoid
        hidden = (silu * up).astype(BF16)
        grad_hidden = grad_ref[...].astype(F32)
        grad_up = (grad_hidden * silu).astype(BF16)
        grad_gate = (grad_hidden * up * (sigmoid + silu * (1.0 - sigmoid))).astype(BF16)
        feed = dot(hidden, down_ref[...]).astype(BF16)
        feed_thin = dot_t(hidden, ah_ref[...]).astype(BF16)
        back = (dot_t(grad_gate, whole[0]) + dot_t(grad_up, whole[1])).astype(BF16)
        back_thin = jnp.concatenate(
            [dot_t(grad_gate, bh_ref[0]).astype(BF16), dot_t(grad_up, bh_ref[1]).astype(BF16)], axis=1
        )
        for block in range(count):
            here = slice(block * rows, (block + 1) * rows)
            feed_refs[block][:, :width] = feed[here]
            feed_refs[block][:, width:] = jnp.concatenate(
                [feed_thin[here], jnp.zeros((rows, EXTRA - rank), BF16)], axis=1
            )
            back_refs[block][:, :width] = back[here]
            back_refs[block][:, width:] = jnp.concatenate(
                [back_thin[here], jnp.zeros((rows, EXTRA - 2 * rank), BF16)], axis=1
            )
        sum_ref[:rank, :] = t_dot(thin, hidden)
        sum_ref[rank : 2 * rank, :] = t_dot(narrow[:, :rank], grad_gate)
        sum_ref[2 * rank :, :] = t_dot(narrow[:, rank:], grad_up)

    out = jax.ShapeDtypeStruct((rows, width + EXTRA), BF16)
    return call(
        kernel,
        [out] * (2 * count)
        + [jax.ShapeDtypeStruct((3 * rank, size), F32)],
        [smem()] + [vmem()] * (2 * count) + [anywhere()] * (n + 1) + [vmem()] * 4,
        [vmem()] * (2 * count + 1),
        [
            pltpu.VMEM((2, width, size), BF16),
            pltpu.VMEM((size, width), BF16),
            pltpu.VMEM((count * rows, size), BF16),
            pltpu.SemaphoreType.DMA((n,)),
            pltpu.SemaphoreType.DMA,
        ],
        12 * rows * count * width * size,
        6 * width * size + 8 * rows * count * width,
        "feed_forward",
    )(offsets, *blocks, *grads, *pieces, down, a_mlp, b_down, a_hidden, b_hidden)


def project_back(grads, place, offsets, pieces, wanted, rows):
    size = pieces[0].shape[1]
    width = 4 * pieces[0].shape[0]
    n = len(pieces)
    count = len(wanted)

    def kernel(place_ref, offsets_ref, *refs):
        g_refs, refs = refs[: len(grads)], refs[len(grads) :]
        piece_refs, refs = refs[:n], refs[n:]
        back_refs, (whole, sems) = refs[:count], refs[count:]
        copies = load_pieces(offsets_ref, piece_refs, whole, sems)
        starts = [pl.multiple_of((place_ref[0] ^ block) * rows, rows) for block in wanted]
        parts = [rows_by_heads(g_refs, start, rows) for start in starts]
        for copy in copies:
            copy.wait()
        for part, back in zip(parts, back_refs):
            back[...] = dot_t(part, whole[...]).astype(BF16)

    return call(
        kernel,
        [jax.ShapeDtypeStruct((rows, width), BF16)] * count,
        [smem(), smem()] + [vmem()] * len(grads) + [anywhere()] * n,
        [vmem()] * count,
        [pltpu.VMEM((width, size), BF16), pltpu.SemaphoreType.DMA((n,))],
        2 * rows * count * width * size,
        2 * (rows * count * (width + size) + width * size),
        "project_back",
        limit=56,
    )(place[None], offsets, *grads, *pieces)


def thin_product(thin, place, blocks):
    rows, width = blocks[0].shape
    count = len(blocks)

    def kernel(place_ref, thin_ref, *refs):
        total = None
        for block in range(count):
            start = pl.multiple_of((place_ref[0] ^ block) * rows, rows)
            term = dot(thin_ref[:, pl.ds(start, rows)], refs[block][...])
            total = term if total is None else total + term
        refs[count][...] = total

    return call(
        kernel,
        jax.ShapeDtypeStruct((thin.shape[0], width), F32),
        [smem()] + [vmem()] * (count + 1),
        vmem(),
        [],
        2 * 128 * rows * count * width,
        2 * rows * count * width,
        "thin_product",
        limit=24,
    )(place[None], thin, *blocks)


def shards(
    tokens,
    cotangent,
    sequence_adapter_index,
    image_span_start,
    attention_norm_gain,
    feedforward_norm_gain,
    query_key_value_weight,
    attention_output_weight,
    gate_up_projection_weight,
    down_projection_weight,
    adapter_model_input_maps,
    adapter_model_output_maps,
    adapter_hidden_input_map,
    adapter_hidden_output_maps,
):
    rows = tokens.shape[1]
    width = tokens.shape[2]
    rank = adapter_model_input_maps.shape[2]
    group = lax.axis_size("shard")
    place = lax.axis_index("shard").astype(jnp.int32)
    rep_place = lax.axis_index("rep").astype(jnp.int32)
    pick = sequence_adapter_index[0]
    starts = image_span_start[0]
    head_cols = width // group
    ff_cols = down_projection_weight.shape[0]
    k_rows = query_key_value_weight.shape[1]

    gain_one = attention_norm_gain.astype(F32)
    gain_two = feedforward_norm_gain.astype(F32)
    residual_in = tokens[0].astype(F32)
    grad_out = cotangent[0].astype(F32)

    def own_columns(values, size):
        return lax.dynamic_slice_in_dim(values, place * size, size, values.ndim - 1)

    quarter = k_rows // 4
    quarter_one, quarter_two = sides(
        query_key_value_weight, rep_place % 4 * quarter, quarter, place, head_cols, (2, 3), "sides_far"
    )
    first_a = hop(quarter_one, "shard", 2)
    normed = norm_rows(residual_in, gain_one).astype(BF16)
    front_chip, front_part = chip_picked(
        jnp.concatenate([adapter_model_input_maps[0:3], adapter_model_output_maps[0:3]]), pick, place
    )
    first_a, front_part, quarter_two, normed, qkv = fence(
        first_a, front_part, quarter_two, normed, query_key_value_weight
    )
    first_b = hop(quarter_two, "shard", 3)
    first_a_two, first_a_three = hop(first_a, "rep", 2), hop(first_a, "rep", 1)
    first_own, near_out = sides(qkv, 0, k_rows, place, head_cols, (0, 1), "sides_near")
    normed_near = core(normed)
    first_b, front_part, near_out, rest_bank, wide_bank = fence(
        first_b, front_part, near_out,
        (adapter_model_input_maps[3:6], adapter_model_output_maps[3:5]),
        (adapter_hidden_input_map[None], adapter_hidden_output_maps),
    )
    front_far = across(front_part)
    first_b_two, first_b_three = hop(first_b, "rep", 1), hop(first_b, "rep", 2)
    front_far, normed, first_a_two, first_a_three = fence(front_far, normed, first_a_two, first_a_three)
    normed_far = across(normed)
    first_a_four = hop(first_a_two, "rep", 1)
    first_near = core(near_out)
    rest_chip, rest_part = chip_picked(jnp.concatenate(rest_bank), pick, place)
    wide_chip, wide_part = chip_picked(jnp.concatenate(wide_bank), pick, place)
    first_b_two, first_b_three, gate_up, grad_out, front_chip = fence(
        first_b_two, first_b_three, gate_up_projection_weight, grad_out, front_chip
    )
    first_b_four = hop(first_b_two, "rep", 2)
    mlp_leaving = [side(gate_up, rep_place % 4 * quarter, quarter, place ^ j, ff_cols) for j in (2, 3)]
    mlp_near_out = side(gate_up, 0, k_rows, place ^ 1, ff_cols)
    mlp_own = side(gate_up, 0, k_rows, place, ff_cols)
    grad_feed = (BRANCH * grad_out).astype(BF16)
    half = HDIM // 2
    frequency = jnp.exp(jnp.arange(half, dtype=F32) * (-2.0 / HDIM) * math.log(THETA))
    angle = jnp.arange(rows * group, dtype=jnp.int32).astype(F32)[:, None] * frequency[None, :]
    cosine = jnp.concatenate([jnp.cos(angle), jnp.cos(angle)], axis=1)
    sine = jnp.concatenate([jnp.sin(angle), jnp.sin(angle)], axis=1)
    cosine_pair = jnp.concatenate([jnp.cos(angle)] * 4, axis=1)
    sine_pair = jnp.concatenate([-jnp.sin(angle), jnp.sin(angle)] * 2, axis=1)
    tables = (cosine, sine, cosine_pair, sine_pair)
    front = whole_picked(front_chip, front_far, place)
    a_first = front[:3].reshape(3 * rank, width)
    b_first = own_columns(front[3:], head_cols)
    b_wide = jnp.concatenate(
        [jnp.pad(b_first[i], ((0, 0), (i * head_cols, (2 - i) * head_cols))) for i in range(3)]
    )
    (
        normed_far, first_a_four, first_b_four, mlp_leaving, mlp_near_out, mlp_own, grad_feed, b_wide, a_first,
        rest_part, wide_part, tables,
    ) = fence(
        normed_far, first_a_four, first_b_four, mlp_leaving, mlp_near_out, mlp_own, grad_feed, b_wide, a_first,
        rest_part, wide_part, tables,
    )
    cosine, sine, cosine_pair, sine_pair = tables
    first_blocks = (normed, normed_near, normed_far, core(normed_far))
    first_offsets, first_pieces = arrange(
        k_rows, first_own, first_near,
        (
            (first_a, first_a_two, first_a_three, first_a_four),
            (first_b, first_b_two, first_b_three, first_b_four),
        ),
        place, rep_place,
    )

    mlp_a, mlp_b = hop(mlp_leaving[0], "shard", 2), hop(mlp_leaving[1], "shard", 3)
    query, key, value, narrow_first = project(
        first_blocks, place, first_offsets, first_pieces, a_first, b_wide, cosine_pair, sine_pair
    )
    query, mlp_a, rest_part, wide_part = fence(query, mlp_a, rest_part, wide_part)
    mlp_a_two, mlp_a_three = hop(mlp_a, "rep", 2), hop(mlp_a, "rep", 1)
    rest_far, wide_far = across(rest_part), across(wide_part)
    mixed, logs = attend(starts, query, key, value, rows)
    mixed, mlp_b, mlp_a_two, mlp_a_three, rest_far = fence(
        mixed, mlp_b, mlp_a_two, mlp_a_three, rest_far
    )
    mlp_b_two, mlp_b_three = hop(mlp_b, "rep", 1), hop(mlp_b, "rep", 2)
    rest = whole_picked(rest_chip, rest_far, place)
    a_out = own_columns(rest[0], head_cols)
    a_mlp = rest[1:3].reshape(2 * rank, width)
    b_out, b_down = rest[3], rest[4]
    far_out = close_attention(mixed, place, attention_output_weight, a_out, (2, 3), rows)
    far_sum = (far_out[0].astype(F32) + core(far_out[1]).astype(F32)).astype(BF16)
    far_sum, mixed_here, grad_feed, wide_far, mlp_near_out = fence(
        far_sum, mixed, grad_feed, wide_far, mlp_near_out
    )
    branch_low, far_rest = across(far_sum[: rows // 2]), far_sum[rows // 2 :]
    feed_near_in = core(grad_feed)
    near_out = close_attention(mixed_here, place, attention_output_weight, a_out, (0, 1), rows)
    near_out, mlp_b_two, mlp_b_three, branch_low, far_rest = fence(
        near_out, mlp_b_two, mlp_b_three, branch_low, far_rest
    )
    mlp_a_four, mlp_b_four = hop(mlp_a_two, "rep", 1), hop(mlp_b_two, "rep", 2)
    branch_high = across(far_rest)
    near_here = core(near_out[1])
    mlp_near = core(mlp_near_out)
    hidden_cols = own_columns(whole_picked(wide_chip, wide_far, place), ff_cols)
    near_here, branch_high, hidden_cols, mlp_own = fence(near_here, branch_high, hidden_cols, mlp_own)
    branch_far = jnp.concatenate([branch_low, branch_high])
    feed_low = across(after(grad_feed[: rows // 2], branch_high))
    feed_rest = after(grad_feed[rows // 2 :], branch_high)
    a_hidden, b_hidden = hidden_cols[0], hidden_cols[1:]
    branch_own = near_out[0].astype(F32) + near_here.astype(F32) + branch_far.astype(F32)
    narrow_out = branch_own[:, width : width + rank].astype(BF16)
    branch = branch_own[:, :width] + dot(narrow_out, b_out)
    middle = residual_in + BRANCH * branch
    normed_second = norm_rows(middle, gain_two).astype(BF16)
    second_far = across(normed_second)
    second_near = core(normed_second)
    second_near, feed_near_in, mlp_near, mlp_a_four, mlp_b_four, feed_low = fence(
        second_near, feed_near_in, mlp_near, mlp_a_four, mlp_b_four, feed_low
    )
    feed_high = across(feed_rest)
    mlp_offsets, mlp_pieces = arrange(
        k_rows, mlp_own, mlp_near,
        (
            (mlp_a, mlp_a_two, mlp_a_three, mlp_a_four),
            (mlp_b, mlp_b_two, mlp_b_three, mlp_b_four),
        ),
        place, rep_place,
    )
    *parts, sum_near = feed_forward(
        (normed_second, second_near), (grad_feed, feed_near_in), mlp_offsets, mlp_pieces,
        down_projection_weight, a_mlp, b_down, a_hidden, b_hidden,
    )
    feed_near, back_near = parts[:2], parts[2:]
    second_far, feed_high, back_near, feed_near = fence(second_far, feed_high, back_near, feed_near)
    feed_far_in = jnp.concatenate([feed_low, feed_high])
    second_blocks = (normed_second, second_near, second_far, core(second_far))
    feed_blocks = (grad_feed, feed_near_in, feed_far_in, core(feed_far_in))
    *parts, sum_far = feed_forward(
        second_blocks[2:], feed_blocks[2:], mlp_offsets, mlp_pieces, down_projection_weight,
        a_mlp, b_down, a_hidden, b_hidden,
    )
    feed_far, back_far = parts[:2], parts[2:]
    back_sum = (back_far[0].astype(F32) + core(back_far[1]).astype(F32)).astype(BF16)
    back_sum, back_near, feed_near, feed_far, sum_near = fence(
        back_sum, back_near, feed_near, feed_far, sum_near
    )
    back_low, back_rest = across(back_sum[: rows // 2]), back_sum[rows // 2 :]

    bits = reps_bits()
    back_here = core(back_near[1])
    feed_here = core(feed_near[1])
    feed_mate = core(feed_far[1])
    mark = jnp.full((rank, ff_cols), pick.astype(F32))
    wide_all = jnp.concatenate([sum_near + sum_far, mark]).astype(BF16)[None]
    wide_hop = hop(wide_all, "rep", bits[0])
    back_low, feed_here, feed_mate, back_here, back_rest, sum_near = fence(
        back_low, feed_here, feed_mate, back_here, back_rest, sum_near
    )
    back_high = across(back_rest)
    feed_here = feed_near[0].astype(F32) + feed_here.astype(F32)
    feed_sum = (feed_far[0].astype(F32) + feed_mate.astype(F32)).astype(BF16)
    back_high, feed_here, feed_sum, back_here, wide_hop = fence(
        back_high, feed_here, feed_sum, back_here, wide_hop
    )
    back_from_far = jnp.concatenate([back_low, back_high])
    second_own = back_near[0].astype(F32) + back_here.astype(F32) + back_from_far.astype(F32)
    grad_narrow_mlp = second_own[:, width : width + 2 * rank].astype(BF16)
    grad_normed_second = second_own[:, :width] + dot(grad_narrow_mlp, a_mlp)
    grad_middle = grad_out + norm_back(middle, gain_two, grad_normed_second)
    grad_branch = (BRANCH * grad_middle).astype(BF16)
    branch_rows = pad_columns([grad_branch, narrow_out, grad_narrow_mlp], width + EXTRA)
    branch_rows, wide_hop = fence(branch_rows, wide_hop)
    branch_far_in = across(branch_rows)
    branch_near_in = core(branch_rows)
    wide_all = both(wide_all, wide_hop, rep_place, bits[0])
    for bit in bits[1:-2]:
        wide_all = both(wide_all, hop(wide_all, "rep", bit), rep_place, bit)
    wide_hop = hop(wide_all, "rep", bits[-2])
    branch_near_in, wide_all = fence(branch_near_in, wide_all)
    mixed_near, grad_a_near, thin_near = open_attention(
        (branch_rows, branch_near_in), second_blocks[:2], (0, 1), place, mixed,
        attention_output_weight, a_out, b_out,
    )
    branch_far_in, mixed_near, wide_hop = fence(branch_far_in, mixed_near, wide_hop)
    wide_all = both(wide_all, wide_hop, rep_place, bits[-2])
    wide_hop = hop(wide_all, "rep", bits[-1])
    feed_from_far = across(after(feed_sum, branch_far_in))
    mixed_far, grad_a_far, thin_far = open_attention(
        (branch_far_in, core(branch_far_in)), second_blocks[2:], (2, 3), place, mixed,
        attention_output_weight, a_out, b_out,
    )

    b_heads = b_first.reshape(3 * rank, head_cols // HDIM, HDIM).transpose(1, 0, 2)

    def attend_part(first, heads, starts):
        return attend_back(
            starts, place, query, key, value, mixed, logs, mixed_near, mixed_far, cosine, sine,
            narrow_first, b_heads, rows, first, heads,
        )

    mixed_far, starts_one, wide_all = fence(mixed_far, starts, wide_all)
    heads = query.shape[0]
    third = heads // 3
    part_one = attend_part(0, third, starts_one)
    part_one, feed_from_far, wide_hop, starts_two = fence(part_one, feed_from_far, wide_hop, starts_one)
    wide_all = both(wide_all, wide_hop, rep_place, bits[-1])
    picks = wide_all[:, -1, :1].astype(F32)
    adapters = adapter_model_input_maps.shape[1] * group
    chosen = (picks == jnp.arange(adapters, dtype=jnp.int32).astype(F32)[None, :]).astype(F32)
    wide_sent = send_sums(wide_all[:, :-rank], chosen, place)
    feed_own = feed_here + feed_from_far.astype(F32)
    narrow_down = feed_own[:, width : width + rank].astype(BF16)
    down_far = across(narrow_down)
    down_near = core(narrow_down)
    starts_two, narrow_down = fence(starts_two, narrow_down)
    part_two = attend_part(third, third, starts_two)
    part_two, down_far, down_near, starts_three, wide_sent = fence(
        part_two, down_far, down_near, starts_two, wide_sent
    )
    down_thin = (narrow_down, down_near, down_far, core(down_far))
    grad_b_down = sum(t_dot(left, right) for left, right in zip(down_thin, feed_blocks))
    early_all = jnp.concatenate(
        [
            grad_a_near + grad_a_far,
            own_columns(jnp.concatenate([thin_near + thin_far, grad_b_down]), head_cols),
        ]
    ).astype(BF16)[None]
    early_hop = hop(early_all, "rep", bits[0])
    early_all, starts_three = fence(early_all, starts_three)
    part_three = attend_part(2 * third, heads - 2 * third, starts_three)
    part_three, early_hop = fence(part_three, early_hop)
    parts = (part_one, part_two, part_three)
    first_grads = [part[number] for number in range(3) for part in parts]
    thin = (part_one[3] + part_two[3] + part_three[3]).astype(BF16)
    thin_hop = core(thin)
    early_all = both(early_all, early_hop, rep_place, bits[0])
    for bit in bits[1:-2]:
        early_all = both(early_all, hop(early_all, "rep", bit), rep_place, bit)
    grad_b_first = jnp.concatenate([part[4] for part in parts], axis=1)
    thin = (thin.astype(F32) + thin_hop.astype(F32)).astype(BF16)
    thin, early_all, grad_b_first = fence(thin, early_all, grad_b_first)
    thin_hop = across(thin)
    early_hop = hop(early_all, "rep", bits[-2])
    grad_narrow = (thin.astype(F32) + thin_hop.astype(F32)).astype(BF16)
    late_all = jnp.concatenate(
        [own_columns(thin_product(grad_narrow, place, first_blocks), head_cols), grad_b_first]
    ).astype(BF16)[None]
    late_all, first_grads = fence(late_all, first_grads)
    late_hop = hop(late_all, "rep", bits[0])
    back_rows_far = project_back(first_grads, place, first_offsets, first_pieces, (2, 3), rows)
    back_rows_far, late_hop, early_hop = fence(back_rows_far, late_hop, early_hop)
    back_mate = core(back_rows_far[1])
    late_all = both(late_all, late_hop, rep_place, bits[0])
    for bit in bits[1:-2]:
        late_all = both(late_all, hop(late_all, "rep", bit), rep_place, bit)
    late_hop = hop(late_all, "rep", bits[-2])
    early_all = both(early_all, early_hop, rep_place, bits[-2])
    early_hop = hop(early_all, "rep", bits[-1])
    back_sum = (back_rows_far[0].astype(F32) + back_mate.astype(F32)).astype(BF16)
    back_sum, first_grads, early_all, late_all = fence(back_sum, first_grads, early_all, late_all)
    back_low, back_high = across(back_sum[: rows // 2]), across(back_sum[rows // 2 :])
    back_rows_near = project_back(first_grads, place, first_offsets, first_pieces, (0, 1), rows)
    back_rows_near, late_hop, early_hop, back_low = fence(back_rows_near, late_hop, early_hop, back_low)
    back_rows_here = core(back_rows_near[1])
    late_all = both(late_all, late_hop, rep_place, bits[-2])
    late_all, early_hop, early_all = fence(late_all, early_hop, early_all)
    late_hop = hop(late_all, "rep", bits[-1])
    early_sent = send_sums(both(early_all, early_hop, rep_place, bits[-1]), chosen, place)

    def whole_maps(stacked, low, high, n):
        part = stacked[:, :, low:high].reshape(group, stacked.shape[1], -1, rank, n)
        pieces = [lax.dynamic_index_in_dim(part, place ^ i, 0, keepdims=False) for i in range(group)]
        return jnp.concatenate(pieces, axis=-1).transpose(1, 0, 2, 3).astype(F32)

    feed = feed_here[:, :width] + feed_from_far[:, :width].astype(F32) + dot(narrow_down, b_down)
    output = (middle + BRANCH * feed).astype(BF16)
    hidden_maps = whole_maps(jnp.stack(wide_sent), 0, 3 * rank, ff_cols)
    late_hop, hidden_maps, output, back_high, back_rows_here = fence(
        late_hop, hidden_maps, output, back_high, back_rows_here
    )
    back_far_in = jnp.concatenate([back_low, back_high])
    late_sent = send_sums(both(late_all, late_hop, rep_place, bits[-1]), chosen, place)
    narrow_own = lax.dynamic_slice_in_dim(grad_narrow, place * rows, rows, 1)
    grad_normed = (
        back_rows_near[0].astype(F32) + back_rows_here.astype(F32) + back_far_in.astype(F32)
        + t_dot(narrow_own, a_first)
    )
    input_grad = grad_middle + norm_back(residual_in, gain_one, grad_normed)
    late_sent, input_grad, early_sent = fence(late_sent, input_grad, early_sent)
    early_got = jnp.stack(early_sent)
    late_got = jnp.stack(late_sent)
    grad_a_model = jnp.concatenate(
        [
            whole_maps(late_got, 0, 3 * rank, head_cols),
            whole_maps(early_got, 0, rank, head_cols),
            whole_maps(early_got, 2 * rank, 4 * rank, head_cols),
        ]
    )
    grad_b_model = jnp.concatenate(
        [
            whole_maps(late_got, 3 * rank, 6 * rank, head_cols),
            whole_maps(early_got, rank, 2 * rank, head_cols),
            whole_maps(early_got, 4 * rank, 5 * rank, head_cols),
        ]
    )
    return (
        output[None], input_grad[None], grad_a_model, grad_b_model, hidden_maps[0], hidden_maps[1:3],
    )


def solution(mesh):
    in_specs = (
        P("rep", "shard", None),
        P("rep", "shard", None),
        P("rep"),
        P("rep", None),
        P(),
        P(),
        P(None, "shard", None),
        P("shard", None),
        P(None, "shard", None),
        P("shard", None),
        P(None, "shard", None, None),
        P(None, "shard", None, None),
        P("shard", None, None),
        P(None, "shard", None, None),
    )
    out_specs = (
        P("rep", "shard", None),
        P("rep", "shard", None),
        P(None, "shard", None, None),
        P(None, "shard", None, None),
        P("shard", None, None),
        P(None, "shard", None, None),
    )
    return jax.shard_map(shards, mesh=mesh, in_specs=in_specs, out_specs=out_specs, check_vma=False)
```

```python
import functools
import math

import jax
import jax.numpy as jnp
from jax import lax
from jax.experimental import pallas as pl
from jax.experimental.pallas import tpu as pltpu
from jax.sharding import PartitionSpec as P

HDIM = 64
SPAN = 256
EPS = 1e-05
THETA = 10000.0
BRANCH = 1.4 / math.sqrt(40.0)
EXTRA = 128
F32 = jnp.float32
BF16 = jnp.bfloat16
LOG2E = math.log2(math.e)


def hop(values, axis, bit):
    size = lax.axis_size(axis)
    return lax.ppermute(values, axis, [(i, i ^ bit) for i in range(size)])


def core(values):
    return hop(values, "shard", 1)


def across(values):
    return hop(values, "shard", 2)


def rows_of(values, count):
    size = values.shape[0] // count
    return tuple(values[i * size : (i + 1) * size] for i in range(count))


def norm_rows(values, gain):
    return values * lax.rsqrt(jnp.mean(values * values, axis=-1, keepdims=True) + EPS) * gain


def norm_back(values, gain, grad):
    width = values.shape[-1]
    scale = lax.rsqrt(jnp.mean(values * values, axis=-1, keepdims=True) + EPS)
    moved = grad * gain
    inner = jnp.sum(values * moved, axis=-1, keepdims=True) / width
    return scale * moved - values * (scale * scale * scale) * inner


def dot(left, right):
    return jnp.dot(left, right, preferred_element_type=F32)


def dot_t(left, right):
    return lax.dot_general(left, right, (((1,), (1,)), ((), ())), preferred_element_type=F32)


def t_dot(left, right):
    return lax.dot_general(left, right, (((0,), (0,)), ((), ())), preferred_element_type=F32)


def pad_columns(pieces, width):
    used = sum(piece.shape[1] for piece in pieces)
    rest = jnp.zeros((pieces[0].shape[0], width - used), pieces[0].dtype)
    return jnp.concatenate(list(pieces) + [rest], axis=1)


def reps_bits():
    bits = []
    bit = 2
    while bit < lax.axis_size("rep"):
        bits.append(bit)
        bit *= 2
    return bits + [1]


def both(held, arrived, rep_place, bit):
    low = jnp.concatenate([held, arrived])
    high = jnp.concatenate([arrived, held])
    return jnp.where((rep_place // bit) % 2 == 0, low, high)


def send_sums(everyone, chosen, place, rank):
    group = lax.axis_size("shard")
    everyone = everyone.reshape(everyone.shape[0], -1, rank, everyone.shape[2])
    per = chosen.shape[1] // group
    sent = []
    for j in range(group):
        marks = lax.dynamic_slice_in_dim(chosen, (place ^ j) * per, per, 1)
        sums = jnp.sum(
            marks[:, None, :, None, None] * everyone[:, :, None].astype(F32), axis=0
        ).astype(BF16)
        sent.append(hop(sums, "shard", j) if j else sums)
    return sent


def chip_picked(bank, pick, place):
    per = bank.shape[1]
    rank = bank.shape[2]
    owner = pick // per
    mine = lax.dynamic_index_in_dim(bank, pick % per, 1, keepdims=False)
    mine = jnp.where(owner == place, mine, jnp.zeros_like(mine))
    chip = mine + core(mine)
    return chip, lax.dynamic_slice_in_dim(chip, (place % 2) * (rank // 2), rank // 2, 1)


def whole_picked(chip, far, place):
    other = core(far)
    low = jnp.where(place % 2 == 0, far, other)
    high = jnp.where(place % 2 == 0, other, far)
    return chip + jnp.concatenate([low, high], axis=1)


def after(value, *others):
    return lax.optimization_barrier((value, others))[0]


def side(weight, row, count, owner, size):
    return lax.dynamic_slice(weight, (0, row, owner * size), (weight.shape[0], count, size))


def sides(weight, row, count, place, size, wanted, name):
    maps, _, columns = weight.shape

    def kernel(where_ref, w_ref, *refs):
        outs, (held, sem) = refs[:-2], refs[-2:]
        start = pl.multiple_of(where_ref[1], 16)
        copy = pltpu.make_async_copy(w_ref.at[:, pl.ds(start, count), :], held, sem)
        copy.start()
        copy.wait()

        def write(out, owner):
            out[...] = jnp.concatenate(
                [held[i, :, owner * size : (owner + 1) * size] for i in range(maps)], axis=1
            )

        for j, out in zip(wanted, outs):
            for owner in range(columns // size):
                pl.when((where_ref[0] ^ j) == owner)(functools.partial(write, out, owner))

    return call(
        kernel,
        [jax.ShapeDtypeStruct((count, maps * size), BF16)] * len(wanted),
        [smem(), anywhere()],
        [vmem()] * len(wanted),
        [pltpu.VMEM((maps, count, columns), BF16), pltpu.SemaphoreType.DMA],
        0,
        2 * maps * count * (columns + size * len(wanted)),
        name,
        limit=58,
    )(jnp.stack([place, jnp.asarray(row, jnp.int32)]), weight)


def arrange(rows, own, near, ways, place, rep_place):
    quarter = rows // 4
    part = rep_place % 4
    pieces = [(place * rows, own), ((place ^ 1) * rows, near)]
    for j, one, two, parts in zip((2, 3), (2, 1), (1, 2), ways):
        for bits, piece in zip((0, one, two, one ^ two), parts):
            pieces.append(((place ^ j) * rows + (part ^ bits) * quarter, piece))
    offsets = jnp.stack([row.astype(jnp.int32) for row, _ in pieces])
    return offsets, [piece for _, piece in pieces]


def fence(*values):
    return lax.optimization_barrier(values)


def load_pieces(offsets, pieces, whole, sems):
    copies = []
    for number, piece in enumerate(pieces):
        start = pl.multiple_of(offsets[number], 16)
        here = pl.ds(start, piece.shape[-2])
        target = whole.at[here, :] if len(piece.shape) == 2 else whole.at[:, here, :]
        copy = pltpu.make_async_copy(piece, target, sems.at[number])
        copy.start()
        copies.append(copy)
    return copies


def vmem():
    return pl.BlockSpec(memory_space=pltpu.VMEM)


def smem():
    return pl.BlockSpec(memory_space=pltpu.SMEM)


def anywhere():
    return pl.BlockSpec(memory_space=pl.ANY)


def call(kernel, outs, in_specs, out_specs, scratch, flops, moved, name, limit=56, **more):
    return pl.pallas_call(
        kernel,
        out_shape=outs,
        in_specs=in_specs,
        out_specs=out_specs,
        scratch_shapes=scratch,
        compiler_params=pltpu.CompilerParams(vmem_limit_bytes=limit << 20),
        cost_estimate=pl.CostEstimate(flops=flops, bytes_accessed=moved, transcendentals=0),
        name=name,
        **more,
    )


def turn(values, cosine, sine):
    half = HDIM // 2
    turned = jnp.concatenate([-values[:, half:], values[:, :half]], axis=1)
    return values * cosine + turned * sine


def project(blocks, place, offsets, pieces, a_first, b_first, cosine_pair, sine_pair):
    rows, width = blocks[0].shape
    count = len(blocks)
    size = pieces[0].shape[1]
    heads = size // (3 * HDIM)
    thin = a_first.shape[0]
    n = len(pieces)

    def kernel(place_ref, offsets_ref, *refs):
        x_refs, refs = refs[:count], refs[count:]
        piece_refs, refs = refs[:n], refs[n:]
        a_ref, b_ref, cos_ref, sin_ref, q_ref, k_ref, v_ref, narrow_ref, whole, sems = refs
        copies = load_pieces(offsets_ref, piece_refs, whole, sems)
        starts = [pl.multiple_of((place_ref[0] ^ block) * rows, rows) for block in range(count)]
        for block in range(count):
            narrow_ref[:, pl.ds(starts[block], rows)] = dot_t(a_ref[...], x_refs[block][...]).astype(BF16)
        for copy in copies:
            copy.wait()
        both = 2 * heads * HDIM
        lane = lax.broadcasted_iota(jnp.int32, (rows, both), 1) % HDIM
        lower = lane < HDIM // 2
        for block in range(count):
            start = starts[block]
            narrow = narrow_ref[:, pl.ds(start, rows)]
            pre = dot(x_refs[block][...], whole[...]) + t_dot(narrow, b_ref[...])
            flat = pre[:, :both]
            cosine_here = jnp.tile(cos_ref[pl.ds(start, rows), :], (1, both // (2 * HDIM)))
            sine_here = jnp.tile(sin_ref[pl.ds(start, rows), :], (1, both // (2 * HDIM)))
            other = jnp.where(
                lower, pltpu.roll(flat, both - HDIM // 2, 1), pltpu.roll(flat, HDIM // 2, 1)
            )
            turned = (flat * cosine_here + other * sine_here).astype(BF16)
            straight = pre[:, both:].astype(BF16)
            for number, out in enumerate((q_ref, k_ref, v_ref)):
                for head in range(heads):
                    at = (number % 2 * heads + head) * HDIM
                    source = turned if number < 2 else straight
                    out[head, pl.ds(start, rows), :] = source[:, at : at + HDIM]

    by_heads = jax.ShapeDtypeStruct((heads, rows * count, HDIM), BF16)
    return call(
        kernel,
        [by_heads] * 3 + [jax.ShapeDtypeStruct((thin, rows * count), BF16)],
        [smem(), smem()] + [vmem()] * count + [anywhere()] * n + [vmem()] * 4,
        [vmem()] * 4,
        [pltpu.VMEM((width, size), BF16), pltpu.SemaphoreType.DMA((n,))],
        2 * rows * count * width * size,
        2 * (rows * count * width + width * size + 2 * rows * count * size),
        "project",
        limit=56,
    )(place[None], offsets, *blocks, *pieces, a_first, b_first, cosine_pair, sine_pair)


def label_of(positions, starts_ref):
    label = jnp.full(positions.shape, -1, jnp.int32)
    for number in range(starts_ref.shape[0]):
        inside = (positions >= starts_ref[number]) & (positions < starts_ref[number] + SPAN)
        label = jnp.where(inside, jnp.int32(number), label)
    return label


def hidden_bias(query_at, key_at, starts_ref):
    query_label = label_of(query_at, starts_ref)
    key_label = label_of(key_at, starts_ref)
    visible = (key_at <= query_at) | (query_label == key_label) & (query_label >= 0)
    return jnp.where(visible, 0.0, -1e30)


def crosses(starts_ref, edge):
    hit = None
    for number in range(starts_ref.shape[0]):
        start = starts_ref[number]
        here = (start < edge) & (start + SPAN > edge)
        hit = here if hit is None else hit | here
    return hit


def fill_bias(bias, starts_ref, rows):
    for block in range(bias.shape[0]):
        shape = (2 * rows, rows)
        query_at = block * rows + lax.broadcasted_iota(jnp.int32, shape, 1)
        key_at = block * rows + lax.broadcasted_iota(jnp.int32, shape, 0)
        bias[block] = hidden_bias(query_at, key_at, starts_ref)


def attend(starts, query, key, value, rows):
    heads, length, _ = query.shape
    count = length // rows
    factor = LOG2E / math.sqrt(HDIM)
    each = 3

    def kernel(starts_ref, q_ref, k_ref, v_ref, o_ref, log_ref, bias):
        @pl.when(pl.program_id(0) == 0)
        def _():
            for block in range(count):
                shape = (rows, 2 * rows)
                query_at = block * rows + lax.broadcasted_iota(jnp.int32, shape, 0)
                key_at = block * rows + lax.broadcasted_iota(jnp.int32, shape, 1)
                bias[block] = hidden_bias(query_at, key_at, starts_ref)

        def one(block, extra):
            low, high = block * rows, (block + 1 + extra) * rows
            here = slice(low, low + rows)
            states = []
            for head in range(each):
                q = q_ref[head, here, :]
                edge = dot_t(q, k_ref[head, low:high, :]) + bias[block, :, : high - low]
                before = dot_t(q, k_ref[head, :low, :]) if block else None
                states.append((edge, before))
            for head, (edge, before) in enumerate(states):
                top = jnp.max(edge, axis=1, keepdims=True)
                if block:
                    top = jnp.maximum(top, jnp.max(before, axis=1, keepdims=True))
                shift = top * factor
                weight = jnp.exp2(edge * factor - shift)
                total = jnp.sum(weight, axis=1, keepdims=True)
                out = dot(weight.astype(BF16), v_ref[head, low:high, :])
                if block:
                    weight = jnp.exp2(before * factor - shift)
                    total = total + jnp.sum(weight, axis=1, keepdims=True)
                    out = out + dot(weight.astype(BF16), v_ref[head, :low, :])
                o_ref[head, here, :] = (out * (1.0 / total)).astype(BF16)
                logs = jnp.broadcast_to(shift + jnp.log2(total), (rows, 128))
                log_ref[head, :, here] = logs.T[:1]

        for block in range(count):
            if block == count - 1:
                one(block, 0)
                continue
            wide = crosses(starts_ref, (block + 1) * rows)
            pl.when(wide)(functools.partial(one, block, 1))
            pl.when(jnp.logical_not(wide))(functools.partial(one, block, 0))

    spec = pl.BlockSpec((each, length, HDIM), lambda h: (h, 0, 0))
    return call(
        kernel,
        [jax.ShapeDtypeStruct(query.shape, BF16), jax.ShapeDtypeStruct((heads, 1, length), F32)],
        [smem(), spec, spec, spec],
        [spec, pl.BlockSpec((each, 1, length), lambda h: (h, 0, 0))],
        [pltpu.VMEM((count, rows, 2 * rows), F32)],
        4 * heads * length * length * HDIM * 4,
        16 * heads * length * HDIM,
        "attend",
        limit=56,
        grid=(heads // each,),
    )(starts, query, key, value)


def attend_back(
    starts, place, query, key, value, mixed, logs, near, far, cosine, sine, narrow, b_heads, rows, first, heads
):
    length = query.shape[1]
    thin = narrow.shape[0]
    rank = thin // 3
    count = length // rows
    scale = 1.0 / math.sqrt(HDIM)
    factor = LOG2E * scale

    def kernel(
        starts_ref, place_ref, q_ref, k_ref, v_ref, o_ref, log_ref, near_ref, far_ref, cos_ref, sin_ref,
        narrow_ref, b_ref, dq_ref, dk_ref, dv_ref, thin_ref, out_ref,
        bias, key_sum, value_sum, key_turned, query_sum,
    ):
        fill_bias(bias, starts_ref, rows)
        ones = jnp.ones((8, HDIM), BF16)
        for head in range(heads):
            key_turned[head] = k_ref[head].astype(F32).T.astype(BF16)

        def pair(head, query, keys, mask, new):
            q, g, logs, inner = query
            here = slice(keys * rows, (keys + 1) * rows)
            raw = dot_t(k_ref[head, here, :], q)
            if mask is not None:
                raw = raw + mask
            probs = jnp.exp2(raw * factor - logs)
            grad_probs = dot_t(v_ref[head, here, :], g)
            grad_scores = (probs * (grad_probs - inner)).astype(BF16)
            value_term = dot(probs.astype(BF16), g)
            key_term = dot(grad_scores, q)
            if new:
                value_sum[head, here, :] = value_term
                key_sum[head, here, :] = key_term
            else:
                value_sum[head, here, :] += value_term
                key_sum[head, here, :] += key_term
            return dot(key_turned[head, :, here], grad_scores)

        for block in reversed(range(count)):
            here = slice(block * rows, (block + 1) * rows)
            relative = place_ref[0] ^ block
            at = pl.multiple_of((relative % 2) * rows, rows)
            queries = []
            for head in range(heads):
                g = jnp.where(
                    relative < 2, near_ref[head, pl.ds(at, rows), :], far_ref[head, pl.ds(at, rows), :]
                )
                product = g.astype(F32) * o_ref[head, here, :].astype(F32)
                high = product.astype(BF16)
                low = (product - high.astype(F32)).astype(BF16)
                inner = (dot_t(ones, high) + dot_t(ones, low))[:1]
                queries.append((q_ref[head, here, :], g, log_ref[head, :, here], inner))
            last = block == count - 1
            totals = [pair(head, queries[head], block, bias[block, :rows, :], last) for head in range(heads)]
            for keys in range(block):
                for head in range(heads):
                    totals[head] = totals[head] + pair(head, queries[head], keys, None, last)
            if not last:
                for head in range(heads):
                    query_sum[head] = totals[head]

                @pl.when(crosses(starts_ref, (block + 1) * rows))
                def _():
                    for head in range(heads):
                        query_sum[head] += pair(head, queries[head], block + 1, bias[block, rows:, :], False)

                totals = [query_sum[head] for head in range(heads)]
            for head in range(heads):
                dq_ref[head, here, :] = turn(
                    totals[head].T * scale, cos_ref[here, :], -sin_ref[here, :]
                ).astype(BF16)
        thins = [None] * 3
        sums = [[], [], []]
        for head in range(heads):
            dk_ref[head] = turn(key_sum[head] * scale, cos_ref[...], -sin_ref[...]).astype(BF16)
            dv_ref[head] = value_sum[head].astype(BF16)
            for number, ref in enumerate((dq_ref, dk_ref, dv_ref)):
                here = slice(number * rank, (number + 1) * rank)
                term = dot_t(b_ref[head, here, :], ref[head])
                thins[number] = term if head == 0 else thins[number] + term
                sums[number].append(dot(narrow_ref[here, :], ref[head]))
        for number in range(3):
            here = slice(number * rank, (number + 1) * rank)
            thin_ref[here, :] = thins[number]
            out_ref[here, :] = jnp.concatenate(sums[number], axis=1)

    step = first // heads
    spec = pl.BlockSpec((heads, length, HDIM), lambda h: (step, 0, 0))
    half = pl.BlockSpec((heads, length // 2, HDIM), lambda h: (step, 0, 0))
    out = pl.BlockSpec((heads, length, HDIM), lambda h: (0, 0, 0))
    table = pl.BlockSpec((length, HDIM), lambda h: (0, 0))
    thin_spec = pl.BlockSpec((thin, length), lambda h: (0, 0))
    return call(
        kernel,
        [jax.ShapeDtypeStruct((heads, length, HDIM), BF16)] * 3
        + [
            jax.ShapeDtypeStruct((thin, length), F32),
            jax.ShapeDtypeStruct((thin, heads * HDIM), F32),
        ],
        [smem(), smem(), spec, spec, spec, spec]
        + [pl.BlockSpec((heads, 1, length), lambda h: (step, 0, 0)), half, half, table, table, thin_spec]
        + [pl.BlockSpec((heads, thin, HDIM), lambda h: (step, 0, 0))],
        [out] * 3 + [thin_spec, pl.BlockSpec((thin, heads * HDIM), lambda h: (0, 0))],
        [
            pltpu.VMEM((count, 2 * rows, rows), F32),
            pltpu.VMEM((heads, length, HDIM), F32),
            pltpu.VMEM((heads, length, HDIM), F32),
            pltpu.VMEM((heads, HDIM, length), BF16),
            pltpu.VMEM((heads, HDIM, rows), F32),
        ],
        10 * heads * length * length * HDIM * 4,
        32 * heads * length * HDIM,
        "attend_back",
        limit=32,
        grid=(1,),
    )(
        starts, place[None], query, key, value, mixed, logs, near, far, cosine, sine, narrow, b_heads
    )


def rows_by_heads(refs, start, rows):
    return jnp.concatenate(
        [ref[head, pl.ds(start, rows), :] for ref in refs for head in range(ref.shape[0])], axis=1
    )


def close_attention(mixed, place, weight, a_out, wanted, rows):
    size, width = weight.shape
    rank = a_out.shape[0]

    def kernel(place_ref, m_ref, w_ref, a_ref, *outs):
        for block, out in zip(wanted, outs):
            start = pl.multiple_of((place_ref[0] ^ block) * rows, rows)
            here = rows_by_heads([m_ref], start, rows)
            out[:, :width] = dot(here, w_ref[...]).astype(BF16)
            narrow = dot_t(here, a_ref[...]).astype(BF16)
            out[:, width:] = jnp.concatenate(
                [narrow, jnp.zeros((rows, EXTRA - rank), BF16)], axis=1
            )

    return call(
        kernel,
        [jax.ShapeDtypeStruct((rows, width + EXTRA), BF16)] * len(wanted),
        [smem()] + [vmem()] * 3,
        [vmem()] * len(wanted),
        [],
        2 * rows * len(wanted) * size * width,
        2 * size * width + 2 * rows * len(wanted) * (width + size),
        "close_attention",
        limit=28,
    )(place[None], mixed, weight, a_out)


def open_attention(blocks, seconds, wanted, place, mixed, weight, a_out, b_out):
    rows, width_ext = blocks[0].shape
    size, width = weight.shape
    rank = a_out.shape[0]
    count = len(blocks)
    heads = size // HDIM

    def kernel(place_ref, *refs):
        g_refs, refs = refs[:count], refs[count:]
        s_refs, refs = refs[:count], refs[count:]
        m_ref, w_ref, a_ref, b_ref, out, sum_ref, wide_ref = refs
        total, branch, second = None, None, None
        for block in range(count):
            start = pl.multiple_of((place_ref[0] ^ wanted[block]) * rows, rows)
            grad = g_refs[block][:, :width]
            thin = g_refs[block][:, width:]
            narrow = dot_t(grad, b_ref[...]).astype(BF16)
            back = dot_t(grad, w_ref[...]) + dot(narrow, a_ref[...])
            for head in range(heads):
                part = back[:, head * HDIM : (head + 1) * HDIM]
                out[head, block * rows : (block + 1) * rows, :] = part.astype(BF16)
            terms = (
                t_dot(narrow, rows_by_heads([m_ref], start, rows)),
                t_dot(thin, grad)[:rank],
                t_dot(thin, s_refs[block][...])[rank : 3 * rank],
            )
            if block == 0:
                total, branch, second = terms
            else:
                total, branch, second = total + terms[0], branch + terms[1], second + terms[2]
        sum_ref[...] = total
        wide_ref[:rank, :] = branch
        wide_ref[rank:, :] = second

    return call(
        kernel,
        [
            jax.ShapeDtypeStruct((heads, rows * count, HDIM), BF16),
            jax.ShapeDtypeStruct((rank, size), F32),
            jax.ShapeDtypeStruct((3 * rank, width), F32),
        ],
        [smem()] + [vmem()] * (2 * count + 4),
        [vmem()] * 3,
        [],
        2 * rows * count * size * width,
        2 * size * width + 2 * rows * count * (2 * width + 2 * size),
        "open_attention",
        limit=32,
    )(place[None], *blocks, *seconds, mixed, weight, a_out, b_out)


def feed_forward(blocks, grads, offsets, pieces, down, a_mlp, b_down, a_hidden, b_hidden):
    rows, width = blocks[0].shape
    count = len(blocks)
    size = down.shape[0]
    rank = b_down.shape[0]
    n = len(pieces)

    def kernel(offsets_ref, *refs):
        x_refs, refs = refs[:count], refs[count:]
        g_refs, refs = refs[:count], refs[count:]
        piece_refs, refs = refs[:n], refs[n:]
        down_hbm, am_ref, bd_ref, ah_ref, bh_ref = refs[:5]
        refs = refs[5:]
        feed_refs, refs = refs[:count], refs[count:]
        back_refs, refs = refs[:count], refs[count:]
        sum_ref, whole, down_ref, grad_ref, sems, down_sem = refs
        down_copy = pltpu.make_async_copy(down_hbm, down_ref, down_sem)
        down_copy.start()
        copies = load_pieces(offsets_ref, piece_refs, whole, sems)
        x = jnp.concatenate([ref[...] for ref in x_refs], axis=0)
        grad = jnp.concatenate([ref[...] for ref in g_refs], axis=0)
        narrow = dot_t(x, am_ref[...]).astype(BF16)
        thin = dot_t(grad, bd_ref[...]).astype(BF16)
        down_copy.wait()
        grad_ref[...] = (dot_t(grad, down_ref[...]) + dot(thin, ah_ref[...])).astype(BF16)
        for copy in copies:
            copy.wait()
        gate = dot(x, whole[0]) + dot(narrow[:, :rank], bh_ref[0])
        up = dot(x, whole[1]) + dot(narrow[:, rank:], bh_ref[1])
        sigmoid = 0.5 + 0.5 * jnp.tanh(0.5 * gate)
        silu = gate * sigmoid
        hidden = (silu * up).astype(BF16)
        grad_hidden = grad_ref[...].astype(F32)
        grad_up = (grad_hidden * silu).astype(BF16)
        grad_gate = (grad_hidden * up * (sigmoid + silu * (1.0 - sigmoid))).astype(BF16)
        feed = dot(hidden, down_ref[...]).astype(BF16)
        feed_thin = dot_t(hidden, ah_ref[...]).astype(BF16)
        back = (dot_t(grad_gate, whole[0]) + dot_t(grad_up, whole[1])).astype(BF16)
        back_thin = jnp.concatenate(
            [dot_t(grad_gate, bh_ref[0]).astype(BF16), dot_t(grad_up, bh_ref[1]).astype(BF16)], axis=1
        )
        for block in range(count):
            here = slice(block * rows, (block + 1) * rows)
            feed_refs[block][:, :width] = feed[here]
            feed_refs[block][:, width:] = jnp.concatenate(
                [feed_thin[here], jnp.zeros((rows, EXTRA - rank), BF16)], axis=1
            )
            back_refs[block][:, :width] = back[here]
            back_refs[block][:, width:] = jnp.concatenate(
                [back_thin[here], jnp.zeros((rows, EXTRA - 2 * rank), BF16)], axis=1
            )
        sum_ref[:rank, :] = t_dot(thin, hidden)
        sum_ref[rank : 2 * rank, :] = t_dot(narrow[:, :rank], grad_gate)
        sum_ref[2 * rank :, :] = t_dot(narrow[:, rank:], grad_up)

    out = jax.ShapeDtypeStruct((rows, width + EXTRA), BF16)
    return call(
        kernel,
        [out] * (2 * count)
        + [jax.ShapeDtypeStruct((3 * rank, size), F32)],
        [smem()] + [vmem()] * (2 * count) + [anywhere()] * (n + 1) + [vmem()] * 4,
        [vmem()] * (2 * count + 1),
        [
            pltpu.VMEM((2, width, size), BF16),
            pltpu.VMEM((size, width), BF16),
            pltpu.VMEM((count * rows, size), BF16),
            pltpu.SemaphoreType.DMA((n,)),
            pltpu.SemaphoreType.DMA,
        ],
        12 * rows * count * width * size,
        6 * width * size + 8 * rows * count * width,
        "feed_forward",
    )(offsets, *blocks, *grads, *pieces, down, a_mlp, b_down, a_hidden, b_hidden)


def project_back(grads, place, offsets, pieces, wanted, rows):
    size = pieces[0].shape[1]
    width = 4 * pieces[0].shape[0]
    n = len(pieces)
    count = len(wanted)

    def kernel(place_ref, offsets_ref, *refs):
        g_refs, refs = refs[: len(grads)], refs[len(grads) :]
        piece_refs, refs = refs[:n], refs[n:]
        back_refs, (whole, sems) = refs[:count], refs[count:]
        copies = load_pieces(offsets_ref, piece_refs, whole, sems)
        starts = [pl.multiple_of((place_ref[0] ^ block) * rows, rows) for block in wanted]
        parts = [rows_by_heads(g_refs, start, rows) for start in starts]
        for copy in copies:
            copy.wait()
        for part, back in zip(parts, back_refs):
            back[...] = dot_t(part, whole[...]).astype(BF16)

    return call(
        kernel,
        [jax.ShapeDtypeStruct((rows, width), BF16)] * count,
        [smem(), smem()] + [vmem()] * len(grads) + [anywhere()] * n,
        [vmem()] * count,
        [pltpu.VMEM((width, size), BF16), pltpu.SemaphoreType.DMA((n,))],
        2 * rows * count * width * size,
        2 * (rows * count * (width + size) + width * size),
        "project_back",
        limit=56,
    )(place[None], offsets, *grads, *pieces)


def thin_product(thin, place, blocks):
    rows, width = blocks[0].shape
    count = len(blocks)

    def kernel(place_ref, thin_ref, *refs):
        total = None
        for block in range(count):
            start = pl.multiple_of((place_ref[0] ^ block) * rows, rows)
            term = dot(thin_ref[:, pl.ds(start, rows)], refs[block][...])
            total = term if total is None else total + term
        refs[count][...] = total

    return call(
        kernel,
        jax.ShapeDtypeStruct((thin.shape[0], width), F32),
        [smem()] + [vmem()] * (count + 1),
        vmem(),
        [],
        2 * 128 * rows * count * width,
        2 * rows * count * width,
        "thin_product",
        limit=24,
    )(place[None], thin, *blocks)


def shards(
    tokens,
    cotangent,
    sequence_adapter_index,
    image_span_start,
    attention_norm_gain,
    feedforward_norm_gain,
    query_key_value_weight,
    attention_output_weight,
    gate_up_projection_weight,
    down_projection_weight,
    adapter_model_input_maps,
    adapter_model_output_maps,
    adapter_hidden_input_map,
    adapter_hidden_output_maps,
):
    rows = tokens.shape[1]
    width = tokens.shape[2]
    rank = adapter_model_input_maps.shape[2]
    group = lax.axis_size("shard")
    place = lax.axis_index("shard").astype(jnp.int32)
    rep_place = lax.axis_index("rep").astype(jnp.int32)
    pick = sequence_adapter_index[0]
    starts = image_span_start[0]
    head_cols = width // group
    ff_cols = down_projection_weight.shape[0]
    k_rows = query_key_value_weight.shape[1]

    gain_one = attention_norm_gain.astype(F32)
    gain_two = feedforward_norm_gain.astype(F32)
    residual_in = tokens[0].astype(F32)
    grad_out = cotangent[0].astype(F32)

    def own_columns(values, size):
        return lax.dynamic_slice_in_dim(values, place * size, size, values.ndim - 1)

    quarter = k_rows // 4
    quarter_one, quarter_two = sides(
        query_key_value_weight, rep_place % 4 * quarter, quarter, place, head_cols, (2, 3), "sides_far"
    )
    first_a = hop(quarter_one, "shard", 2)
    normed = norm_rows(residual_in, gain_one).astype(BF16)
    front_chip, front_part = chip_picked(
        jnp.concatenate([adapter_model_input_maps[0:3], adapter_model_output_maps[0:3]]), pick, place
    )
    first_a, front_part, quarter_two, normed, qkv = fence(
        first_a, front_part, quarter_two, normed, query_key_value_weight
    )
    first_b = hop(quarter_two, "shard", 3)
    first_a_two, first_a_three = hop(first_a, "rep", 2), hop(first_a, "rep", 1)
    first_own, near_out = sides(qkv, 0, k_rows, place, head_cols, (0, 1), "sides_near")
    normed_near = core(normed)
    first_b, front_part, near_out, rest_bank, wide_bank = fence(
        first_b, front_part, near_out,
        (adapter_model_input_maps[3:6], adapter_model_output_maps[3:5]),
        (adapter_hidden_input_map[None], adapter_hidden_output_maps),
    )
    front_far = across(front_part)
    first_b_two, first_b_three = hop(first_b, "rep", 1), hop(first_b, "rep", 2)
    front_far, normed, first_a_two, first_a_three = fence(front_far, normed, first_a_two, first_a_three)
    normed_far = across(normed)
    first_a_four = hop(first_a_two, "rep", 1)
    first_near = core(near_out)
    rest_chip, rest_part = chip_picked(jnp.concatenate(rest_bank), pick, place)
    wide_chip, wide_part = chip_picked(jnp.concatenate(wide_bank), pick, place)
    first_b_two, first_b_three, gate_up, grad_out, front_chip = fence(
        first_b_two, first_b_three, gate_up_projection_weight, grad_out, front_chip
    )
    first_b_four = hop(first_b_two, "rep", 2)
    mlp_leaving = [side(gate_up, rep_place % 4 * quarter, quarter, place ^ j, ff_cols) for j in (2, 3)]
    grad_feed = (BRANCH * grad_out).astype(BF16)
    half = HDIM // 2
    frequency = jnp.exp(jnp.arange(half, dtype=F32) * (-2.0 / HDIM) * math.log(THETA))
    angle = jnp.arange(rows * group, dtype=jnp.int32).astype(F32)[:, None] * frequency[None, :]
    cosine = jnp.concatenate([jnp.cos(angle), jnp.cos(angle)], axis=1)
    sine = jnp.concatenate([jnp.sin(angle), jnp.sin(angle)], axis=1)
    cosine_pair = jnp.concatenate([jnp.cos(angle)] * 4, axis=1)
    sine_pair = jnp.concatenate([-jnp.sin(angle), jnp.sin(angle)] * 2, axis=1)
    tables = (cosine, sine, cosine_pair, sine_pair)
    front = whole_picked(front_chip, front_far, place)
    a_first = front[:3].reshape(3 * rank, width)
    b_first = own_columns(front[3:], head_cols)
    b_wide = jnp.concatenate(
        [jnp.pad(b_first[i], ((0, 0), (i * head_cols, (2 - i) * head_cols))) for i in range(3)]
    )
    (
        normed_far, first_a_four, first_b_four, mlp_leaving, grad_feed, b_wide, a_first, rest_part, wide_part,
        tables,
    ) = fence(
        normed_far, first_a_four, first_b_four, mlp_leaving, grad_feed, b_wide, a_first, rest_part, wide_part,
        tables,
    )
    cosine, sine, cosine_pair, sine_pair = tables
    first_blocks = (normed, normed_near, normed_far, core(normed_far))
    first_offsets, first_pieces = arrange(
        k_rows, first_own, first_near,
        (
            (first_a, first_a_two, first_a_three, first_a_four),
            (first_b, first_b_two, first_b_three, first_b_four),
        ),
        place, rep_place,
    )

    mlp_a, mlp_b = hop(mlp_leaving[0], "shard", 2), hop(mlp_leaving[1], "shard", 3)
    query, key, value, narrow_first = project(
        first_blocks, place, first_offsets, first_pieces, a_first, b_wide, cosine_pair, sine_pair
    )
    query, mlp_a, rest_part, wide_part = fence(query, mlp_a, rest_part, wide_part)
    mlp_a_two, mlp_a_three = hop(mlp_a, "rep", 2), hop(mlp_a, "rep", 1)
    rest_far, wide_far = across(rest_part), across(wide_part)
    mixed, logs = attend(starts, query, key, value, rows)
    mixed, mlp_b, mlp_a_two, mlp_a_three, rest_far = fence(
        mixed, mlp_b, mlp_a_two, mlp_a_three, rest_far
    )
    mlp_b_two, mlp_b_three = hop(mlp_b, "rep", 1), hop(mlp_b, "rep", 2)
    rest = whole_picked(rest_chip, rest_far, place)
    a_out = own_columns(rest[0], head_cols)
    a_mlp = rest[1:3].reshape(2 * rank, width)
    b_out, b_down = rest[3], rest[4]
    far_out = close_attention(mixed, place, attention_output_weight, a_out, (2, 3), rows)
    far_sum = (far_out[0].astype(F32) + core(far_out[1]).astype(F32)).astype(BF16)
    far_sum, mixed_here, grad_feed, wide_far = fence(far_sum, mixed, grad_feed, wide_far)
    branch_low, far_rest = across(far_sum[: rows // 2]), far_sum[rows // 2 :]
    feed_near_in = core(grad_feed)
    near_out = close_attention(mixed_here, place, attention_output_weight, a_out, (0, 1), rows)
    near_out, gate_up = fence(near_out, gate_up)
    mlp_near_out = side(gate_up, 0, k_rows, place ^ 1, ff_cols)
    mlp_own = side(gate_up, 0, k_rows, place, ff_cols)
    near_out, mlp_b_two, mlp_b_three, branch_low, far_rest, mlp_near_out, mlp_own = fence(
        near_out, mlp_b_two, mlp_b_three, branch_low, far_rest, mlp_near_out, mlp_own
    )
    mlp_a_four, mlp_b_four = hop(mlp_a_two, "rep", 1), hop(mlp_b_two, "rep", 2)
    branch_high = across(far_rest)
    near_here = core(near_out[1])
    mlp_near = core(mlp_near_out)
    hidden_cols = own_columns(whole_picked(wide_chip, wide_far, place), ff_cols)
    near_here, branch_high, hidden_cols, mlp_own = fence(near_here, branch_high, hidden_cols, mlp_own)
    branch_far = jnp.concatenate([branch_low, branch_high])
    feed_low = across(after(grad_feed[: rows // 2], branch_high))
    feed_rest = after(grad_feed[rows // 2 :], branch_high)
    a_hidden, b_hidden = hidden_cols[0], hidden_cols[1:]
    branch_own = near_out[0].astype(F32) + near_here.astype(F32) + branch_far.astype(F32)
    narrow_out = branch_own[:, width : width + rank].astype(BF16)
    branch = branch_own[:, :width] + dot(narrow_out, b_out)
    middle = residual_in + BRANCH * branch
    normed_second = norm_rows(middle, gain_two).astype(BF16)
    second_far = across(normed_second)
    second_near = core(normed_second)
    second_near, feed_near_in, mlp_near, mlp_a_four, mlp_b_four, feed_low = fence(
        second_near, feed_near_in, mlp_near, mlp_a_four, mlp_b_four, feed_low
    )
    feed_high = across(feed_rest)
    mlp_offsets, mlp_pieces = arrange(
        k_rows, mlp_own, mlp_near,
        (
            (mlp_a, mlp_a_two, mlp_a_three, mlp_a_four),
            (mlp_b, mlp_b_two, mlp_b_three, mlp_b_four),
        ),
        place, rep_place,
    )
    *parts, sum_near = feed_forward(
        (normed_second, second_near), (grad_feed, feed_near_in), mlp_offsets, mlp_pieces,
        down_projection_weight, a_mlp, b_down, a_hidden, b_hidden,
    )
    feed_near, back_near = parts[:2], parts[2:]
    second_far, feed_high, back_near, feed_near = fence(second_far, feed_high, back_near, feed_near)
    feed_far_in = jnp.concatenate([feed_low, feed_high])
    second_blocks = (normed_second, second_near, second_far, core(second_far))
    feed_blocks = (grad_feed, feed_near_in, feed_far_in, core(feed_far_in))
    *parts, sum_far = feed_forward(
        second_blocks[2:], feed_blocks[2:], mlp_offsets, mlp_pieces, down_projection_weight,
        a_mlp, b_down, a_hidden, b_hidden,
    )
    feed_far, back_far = parts[:2], parts[2:]
    back_sum = (back_far[0].astype(F32) + core(back_far[1]).astype(F32)).astype(BF16)
    back_sum, back_near, feed_near, feed_far, sum_near = fence(
        back_sum, back_near, feed_near, feed_far, sum_near
    )
    back_low, back_rest = across(back_sum[: rows // 2]), back_sum[rows // 2 :]

    bits = reps_bits()
    back_here = core(back_near[1])
    feed_here = core(feed_near[1])
    feed_mate = core(feed_far[1])
    mark = jnp.full((rank, ff_cols), pick.astype(F32))
    wide_all = jnp.concatenate([sum_near + sum_far, mark]).astype(BF16)[None]
    wide_hop = hop(wide_all, "rep", bits[0])
    back_low, feed_here, feed_mate, back_here, back_rest, sum_near = fence(
        back_low, feed_here, feed_mate, back_here, back_rest, sum_near
    )
    back_high = across(back_rest)
    feed_here = feed_near[0].astype(F32) + feed_here.astype(F32)
    feed_sum = (feed_far[0].astype(F32) + feed_mate.astype(F32)).astype(BF16)
    back_high, feed_here, feed_sum, back_here, wide_hop = fence(
        back_high, feed_here, feed_sum, back_here, wide_hop
    )
    back_from_far = jnp.concatenate([back_low, back_high])
    second_own = back_near[0].astype(F32) + back_here.astype(F32) + back_from_far.astype(F32)
    grad_narrow_mlp = second_own[:, width : width + 2 * rank].astype(BF16)
    grad_normed_second = second_own[:, :width] + dot(grad_narrow_mlp, a_mlp)
    grad_middle = grad_out + norm_back(middle, gain_two, grad_normed_second)
    grad_branch = (BRANCH * grad_middle).astype(BF16)
    branch_rows = pad_columns([grad_branch, narrow_out, grad_narrow_mlp], width + EXTRA)
    branch_rows, wide_hop = fence(branch_rows, wide_hop)
    branch_far_in = across(branch_rows)
    branch_near_in = core(branch_rows)
    wide_all = both(wide_all, wide_hop, rep_place, bits[0])
    for bit in bits[1:-2]:
        wide_all = both(wide_all, hop(wide_all, "rep", bit), rep_place, bit)
    wide_hop = hop(wide_all, "rep", bits[-2])
    branch_near_in, wide_all = fence(branch_near_in, wide_all)
    mixed_near, grad_a_near, thin_near = open_attention(
        (branch_rows, branch_near_in), second_blocks[:2], (0, 1), place, mixed,
        attention_output_weight, a_out, b_out,
    )
    mixed_near, wide_hop = fence(mixed_near, wide_hop)
    wide_all = both(wide_all, wide_hop, rep_place, bits[-2])
    wide_hop = hop(wide_all, "rep", bits[-1])
    branch_far_in, mixed_near, wide_all = fence(branch_far_in, mixed_near, wide_all)
    feed_from_far = across(after(feed_sum, branch_far_in))
    mixed_far, grad_a_far, thin_far = open_attention(
        (branch_far_in, core(branch_far_in)), second_blocks[2:], (2, 3), place, mixed,
        attention_output_weight, a_out, b_out,
    )

    b_heads = b_first.reshape(3 * rank, head_cols // HDIM, HDIM).transpose(1, 0, 2)

    def attend_part(first, heads, starts):
        return attend_back(
            starts, place, query, key, value, mixed, logs, mixed_near, mixed_far, cosine, sine,
            narrow_first, b_heads, rows, first, heads,
        )

    mixed_far, starts_one, wide_all = fence(mixed_far, starts, wide_all)
    heads = query.shape[0]
    third = heads // 3
    part_one = attend_part(0, third, starts_one)
    part_one, feed_from_far, wide_hop, starts_two = fence(part_one, feed_from_far, wide_hop, starts_one)
    wide_all = both(wide_all, wide_hop, rep_place, bits[-1])
    picks = wide_all[:, -1, :1].astype(F32)
    adapters = adapter_model_input_maps.shape[1] * group
    chosen = (picks == jnp.arange(adapters, dtype=jnp.int32).astype(F32)[None, :]).astype(F32)
    wide_sent = send_sums(wide_all[:, :-rank], chosen, place, rank)
    feed_own = feed_here + feed_from_far.astype(F32)
    narrow_down = feed_own[:, width : width + rank].astype(BF16)
    down_far = across(narrow_down)
    down_near = core(narrow_down)
    starts_two, narrow_down = fence(starts_two, narrow_down)
    part_two = attend_part(third, third, starts_two)
    part_two, down_far, down_near, starts_three, wide_sent = fence(
        part_two, down_far, down_near, starts_two, wide_sent
    )
    down_thin = (narrow_down, down_near, down_far, core(down_far))
    grad_b_down = sum(t_dot(left, right) for left, right in zip(down_thin, feed_blocks))
    early_all = jnp.concatenate(
        [
            grad_a_near + grad_a_far,
            own_columns(jnp.concatenate([thin_near + thin_far, grad_b_down]), head_cols),
        ]
    ).astype(BF16)[None]
    early_hop = hop(early_all, "rep", bits[0])
    early_all, starts_three = fence(early_all, starts_three)
    part_three = attend_part(2 * third, heads - 2 * third, starts_three)
    part_three, early_hop = fence(part_three, early_hop)
    parts = (part_one, part_two, part_three)
    first_grads = [part[number] for number in range(3) for part in parts]
    thin = (part_one[3] + part_two[3] + part_three[3]).astype(BF16)
    thin_hop = core(thin)
    early_all = both(early_all, early_hop, rep_place, bits[0])
    for bit in bits[1:-2]:
        early_all = both(early_all, hop(early_all, "rep", bit), rep_place, bit)
    grad_b_first = jnp.concatenate([part[4] for part in parts], axis=1)
    thin = (thin.astype(F32) + thin_hop.astype(F32)).astype(BF16)
    thin, early_all, grad_b_first = fence(thin, early_all, grad_b_first)
    thin_hop = across(thin)
    early_hop = hop(early_all, "rep", bits[-2])
    grad_narrow = (thin.astype(F32) + thin_hop.astype(F32)).astype(BF16)
    late_all = jnp.concatenate(
        [own_columns(thin_product(grad_narrow, place, first_blocks), head_cols), grad_b_first]
    ).astype(BF16)[None]
    late_all, first_grads = fence(late_all, first_grads)
    late_hop = hop(late_all, "rep", bits[0])
    back_rows_far = project_back(first_grads, place, first_offsets, first_pieces, (2, 3), rows)
    back_rows_far, late_hop, early_hop = fence(back_rows_far, late_hop, early_hop)
    back_mate = core(back_rows_far[1])
    late_all = both(late_all, late_hop, rep_place, bits[0])
    for bit in bits[1:-2]:
        late_all = both(late_all, hop(late_all, "rep", bit), rep_place, bit)
    late_hop = hop(late_all, "rep", bits[-2])
    early_all = both(early_all, early_hop, rep_place, bits[-2])
    early_hop = hop(early_all, "rep", bits[-1])
    back_sum = (back_rows_far[0].astype(F32) + back_mate.astype(F32)).astype(BF16)
    back_sum, first_grads, early_all, late_all = fence(back_sum, first_grads, early_all, late_all)
    back_low, back_high = across(back_sum[: rows // 2]), across(back_sum[rows // 2 :])
    back_rows_near = project_back(first_grads, place, first_offsets, first_pieces, (0, 1), rows)
    back_rows_near, late_hop, early_hop, back_low = fence(back_rows_near, late_hop, early_hop, back_low)
    back_rows_here = core(back_rows_near[1])
    late_all = both(late_all, late_hop, rep_place, bits[-2])
    late_all, early_hop, early_all = fence(late_all, early_hop, early_all)
    late_hop = hop(late_all, "rep", bits[-1])
    early_sent = send_sums(both(early_all, early_hop, rep_place, bits[-1]), chosen, place, rank)

    def whole_maps(stacked, low, high):
        part = stacked[:, low // rank : high // rank]
        pieces = [lax.dynamic_index_in_dim(part, place ^ i, 0, keepdims=False) for i in range(group)]
        return jnp.concatenate(pieces, axis=-1).astype(F32)

    feed = feed_here[:, :width] + feed_from_far[:, :width].astype(F32) + dot(narrow_down, b_down)
    output = (middle + BRANCH * feed).astype(BF16)
    hidden_maps = whole_maps(jnp.stack(wide_sent), 0, 3 * rank)
    late_hop, hidden_maps, output, back_high, back_rows_here = fence(
        late_hop, hidden_maps, output, back_high, back_rows_here
    )
    back_far_in = jnp.concatenate([back_low, back_high])
    late_sent = send_sums(both(late_all, late_hop, rep_place, bits[-1]), chosen, place, rank)
    narrow_own = lax.dynamic_slice_in_dim(grad_narrow, place * rows, rows, 1)
    grad_normed = (
        back_rows_near[0].astype(F32) + back_rows_here.astype(F32) + back_far_in.astype(F32)
        + t_dot(narrow_own, a_first)
    )
    input_grad = grad_middle + norm_back(residual_in, gain_one, grad_normed)
    late_sent, input_grad, early_sent = fence(late_sent, input_grad, early_sent)
    early_got = jnp.stack(early_sent)
    late_got = jnp.stack(late_sent)
    grad_a_model = jnp.concatenate(
        [
            whole_maps(late_got, 0, 3 * rank),
            whole_maps(early_got, 0, rank),
            whole_maps(early_got, 2 * rank, 4 * rank),
        ]
    )
    grad_b_model = jnp.concatenate(
        [
            whole_maps(late_got, 3 * rank, 6 * rank),
            whole_maps(early_got, rank, 2 * rank),
            whole_maps(early_got, 4 * rank, 5 * rank),
        ]
    )
    return (
        output[None], input_grad[None], grad_a_model, grad_b_model, hidden_maps[0], hidden_maps[1:3],
    )


def solution(mesh):
    in_specs = (
        P("rep", "shard", None),
        P("rep", "shard", None),
        P("rep"),
        P("rep", None),
        P(),
        P(),
        P(None, "shard", None),
        P("shard", None),
        P(None, "shard", None),
        P("shard", None),
        P(None, "shard", None, None),
        P(None, "shard", None, None),
        P("shard", None, None),
        P(None, "shard", None, None),
    )
    out_specs = (
        P("rep", "shard", None),
        P("rep", "shard", None),
        P(None, "shard", None, None),
        P(None, "shard", None, None),
        P("shard", None, None),
        P(None, "shard", None, None),
    )
    return jax.shard_map(shards, mesh=mesh, in_specs=in_specs, out_specs=out_specs, check_vma=False)
```

```python
import functools
import math

import jax
import jax.numpy as jnp
from jax import lax
from jax.experimental import pallas as pl
from jax.experimental.pallas import tpu as pltpu
from jax.sharding import PartitionSpec as P

HDIM = 64
SPAN = 256
EPS = 1e-05
THETA = 10000.0
BRANCH = 1.4 / math.sqrt(40.0)
EXTRA = 128
F32 = jnp.float32
BF16 = jnp.bfloat16
LOG2E = math.log2(math.e)


def hop(values, axis, bit):
    size = lax.axis_size(axis)
    return lax.ppermute(values, axis, [(i, i ^ bit) for i in range(size)])


def core(values):
    return hop(values, "shard", 1)


def across(values):
    return hop(values, "shard", 2)


def rows_of(values, count):
    size = values.shape[0] // count
    return tuple(values[i * size : (i + 1) * size] for i in range(count))


def norm_rows(values, gain):
    return values * lax.rsqrt(jnp.mean(values * values, axis=-1, keepdims=True) + EPS) * gain


def norm_back(values, gain, grad):
    width = values.shape[-1]
    scale = lax.rsqrt(jnp.mean(values * values, axis=-1, keepdims=True) + EPS)
    moved = grad * gain
    inner = jnp.sum(values * moved, axis=-1, keepdims=True) / width
    return scale * moved - values * (scale * scale * scale) * inner


def dot(left, right):
    return jnp.dot(left, right, preferred_element_type=F32)


def dot_t(left, right):
    return lax.dot_general(left, right, (((1,), (1,)), ((), ())), preferred_element_type=F32)


def t_dot(left, right):
    return lax.dot_general(left, right, (((0,), (0,)), ((), ())), preferred_element_type=F32)


def pad_columns(pieces, width):
    used = sum(piece.shape[1] for piece in pieces)
    rest = jnp.zeros((pieces[0].shape[0], width - used), pieces[0].dtype)
    return jnp.concatenate(list(pieces) + [rest], axis=1)


def reps_bits():
    bits = []
    bit = 2
    while bit < lax.axis_size("rep"):
        bits.append(bit)
        bit *= 2
    return bits + [1]


def both(held, arrived, rep_place, bit):
    low = jnp.concatenate([held, arrived])
    high = jnp.concatenate([arrived, held])
    return jnp.where((rep_place // bit) % 2 == 0, low, high)


def send_sums(everyone, chosen, place, rank):
    group = lax.axis_size("shard")
    everyone = everyone.reshape(everyone.shape[0], -1, rank, everyone.shape[2])
    per = chosen.shape[1] // group
    sent = []
    for j in range(group):
        marks = lax.dynamic_slice_in_dim(chosen, (place ^ j) * per, per, 1)
        sums = jnp.sum(
            marks[:, None, :, None, None] * everyone[:, :, None].astype(F32), axis=0
        ).astype(BF16)
        sent.append(hop(sums, "shard", j) if j else sums)
    return sent


def chip_picked(bank, pick, place):
    per = bank.shape[1]
    rank = bank.shape[2]
    owner = pick // per
    mine = lax.dynamic_index_in_dim(bank, pick % per, 1, keepdims=False)
    mine = jnp.where(owner == place, mine, jnp.zeros_like(mine))
    chip = mine + core(mine)
    return chip, lax.dynamic_slice_in_dim(chip, (place % 2) * (rank // 2), rank // 2, 1)


def whole_picked(chip, far, place):
    other = core(far)
    low = jnp.where(place % 2 == 0, far, other)
    high = jnp.where(place % 2 == 0, other, far)
    return chip + jnp.concatenate([low, high], axis=1)


def after(value, *others):
    return lax.optimization_barrier((value, others))[0]


def side(weight, row, count, owner, size):
    return lax.dynamic_slice(weight, (0, row, owner * size), (weight.shape[0], count, size))


def sides(weight, row, count, place, size, wanted, name):
    maps, _, columns = weight.shape

    def kernel(where_ref, w_ref, *refs):
        outs, (held, sem) = refs[:-2], refs[-2:]
        start = pl.multiple_of(where_ref[1], 16)
        copy = pltpu.make_async_copy(w_ref.at[:, pl.ds(start, count), :], held, sem)
        copy.start()
        copy.wait()

        def write(out, owner):
            out[...] = jnp.concatenate(
                [held[i, :, owner * size : (owner + 1) * size] for i in range(maps)], axis=1
            )

        for j, out in zip(wanted, outs):
            for owner in range(columns // size):
                pl.when((where_ref[0] ^ j) == owner)(functools.partial(write, out, owner))

    return call(
        kernel,
        [jax.ShapeDtypeStruct((count, maps * size), BF16)] * len(wanted),
        [smem(), anywhere()],
        [vmem()] * len(wanted),
        [pltpu.VMEM((maps, count, columns), BF16), pltpu.SemaphoreType.DMA],
        0,
        2 * maps * count * (columns + size * len(wanted)),
        name,
        limit=58,
    )(jnp.stack([place, jnp.asarray(row, jnp.int32)]), weight)


def arrange(rows, own, near, ways, place, rep_place):
    quarter = rows // 4
    part = rep_place % 4
    pieces = [(place * rows, own), ((place ^ 1) * rows, near)]
    for j, one, two, parts in zip((2, 3), (2, 1), (1, 2), ways):
        for bits, piece in zip((0, one, two, one ^ two), parts):
            pieces.append(((place ^ j) * rows + (part ^ bits) * quarter, piece))
    offsets = jnp.stack([row.astype(jnp.int32) for row, _ in pieces])
    return offsets, [piece for _, piece in pieces]


def fence(*values):
    return lax.optimization_barrier(values)


def load_pieces(offsets, pieces, whole, sems):
    copies = []
    for number, piece in enumerate(pieces):
        start = pl.multiple_of(offsets[number], 16)
        here = pl.ds(start, piece.shape[-2])
        target = whole.at[here, :] if len(piece.shape) == 2 else whole.at[:, here, :]
        copy = pltpu.make_async_copy(piece, target, sems.at[number])
        copy.start()
        copies.append(copy)
    return copies


def vmem():
    return pl.BlockSpec(memory_space=pltpu.VMEM)


def smem():
    return pl.BlockSpec(memory_space=pltpu.SMEM)


def anywhere():
    return pl.BlockSpec(memory_space=pl.ANY)


def call(kernel, outs, in_specs, out_specs, scratch, flops, moved, name, limit=56, **more):
    return pl.pallas_call(
        kernel,
        out_shape=outs,
        in_specs=in_specs,
        out_specs=out_specs,
        scratch_shapes=scratch,
        compiler_params=pltpu.CompilerParams(vmem_limit_bytes=limit << 20),
        cost_estimate=pl.CostEstimate(flops=flops, bytes_accessed=moved, transcendentals=0),
        name=name,
        **more,
    )


def turn(values, cosine, sine):
    half = HDIM // 2
    turned = jnp.concatenate([-values[:, half:], values[:, :half]], axis=1)
    return values * cosine + turned * sine


def project(blocks, place, offsets, pieces, a_first, b_first, cosine_pair, sine_pair):
    rows, width = blocks[0].shape
    count = len(blocks)
    size = pieces[0].shape[1]
    heads = size // (3 * HDIM)
    thin = a_first.shape[0]
    n = len(pieces)

    def kernel(place_ref, offsets_ref, *refs):
        x_refs, refs = refs[:count], refs[count:]
        piece_refs, refs = refs[:n], refs[n:]
        a_ref, b_ref, cos_ref, sin_ref, q_ref, k_ref, v_ref, narrow_ref, whole, sems = refs
        copies = load_pieces(offsets_ref, piece_refs, whole, sems)
        starts = [pl.multiple_of((place_ref[0] ^ block) * rows, rows) for block in range(count)]
        for block in range(count):
            narrow_ref[:, pl.ds(starts[block], rows)] = dot_t(a_ref[...], x_refs[block][...]).astype(BF16)
        for copy in copies:
            copy.wait()
        both = 2 * heads * HDIM
        lane = lax.broadcasted_iota(jnp.int32, (rows, both), 1) % HDIM
        lower = lane < HDIM // 2
        for block in range(count):
            start = starts[block]
            narrow = narrow_ref[:, pl.ds(start, rows)]
            pre = dot(x_refs[block][...], whole[...]) + t_dot(narrow, b_ref[...])
            flat = pre[:, :both]
            cosine_here = jnp.tile(cos_ref[pl.ds(start, rows), :], (1, both // (2 * HDIM)))
            sine_here = jnp.tile(sin_ref[pl.ds(start, rows), :], (1, both // (2 * HDIM)))
            other = jnp.where(
                lower, pltpu.roll(flat, both - HDIM // 2, 1), pltpu.roll(flat, HDIM // 2, 1)
            )
            turned = (flat * cosine_here + other * sine_here).astype(BF16)
            straight = pre[:, both:].astype(BF16)
            for number, out in enumerate((q_ref, k_ref, v_ref)):
                for head in range(heads):
                    at = (number % 2 * heads + head) * HDIM
                    source = turned if number < 2 else straight
                    out[head, pl.ds(start, rows), :] = source[:, at : at + HDIM]

    by_heads = jax.ShapeDtypeStruct((heads, rows * count, HDIM), BF16)
    return call(
        kernel,
        [by_heads] * 3 + [jax.ShapeDtypeStruct((thin, rows * count), BF16)],
        [smem(), smem()] + [vmem()] * count + [anywhere()] * n + [vmem()] * 4,
        [vmem()] * 4,
        [pltpu.VMEM((width, size), BF16), pltpu.SemaphoreType.DMA((n,))],
        2 * rows * count * width * size,
        2 * (rows * count * width + width * size + 2 * rows * count * size),
        "project",
        limit=56,
    )(place[None], offsets, *blocks, *pieces, a_first, b_first, cosine_pair, sine_pair)


def label_of(positions, starts_ref):
    label = jnp.full(positions.shape, -1, jnp.int32)
    for number in range(starts_ref.shape[0]):
        inside = (positions >= starts_ref[number]) & (positions < starts_ref[number] + SPAN)
        label = jnp.where(inside, jnp.int32(number), label)
    return label


def hidden_bias(query_at, key_at, starts_ref):
    query_label = label_of(query_at, starts_ref)
    key_label = label_of(key_at, starts_ref)
    visible = (key_at <= query_at) | (query_label == key_label) & (query_label >= 0)
    return jnp.where(visible, 0.0, -1e30)


def crosses(starts_ref, edge):
    hit = None
    for number in range(starts_ref.shape[0]):
        start = starts_ref[number]
        here = (start < edge) & (start + SPAN > edge)
        hit = here if hit is None else hit | here
    return hit


def fill_bias(bias, starts_ref, rows):
    for block in range(bias.shape[0]):
        shape = (2 * rows, rows)
        query_at = block * rows + lax.broadcasted_iota(jnp.int32, shape, 1)
        key_at = block * rows + lax.broadcasted_iota(jnp.int32, shape, 0)
        bias[block] = hidden_bias(query_at, key_at, starts_ref)


def attend(starts, query, key, value, rows):
    heads, length, _ = query.shape
    count = length // rows
    factor = LOG2E / math.sqrt(HDIM)
    each = 3

    def kernel(starts_ref, q_ref, k_ref, v_ref, o_ref, log_ref, bias):
        @pl.when(pl.program_id(0) == 0)
        def _():
            for block in range(count):
                shape = (rows, 2 * rows)
                query_at = block * rows + lax.broadcasted_iota(jnp.int32, shape, 0)
                key_at = block * rows + lax.broadcasted_iota(jnp.int32, shape, 1)
                bias[block] = hidden_bias(query_at, key_at, starts_ref)

        def one(block, extra):
            low, high = block * rows, (block + 1 + extra) * rows
            here = slice(low, low + rows)
            states = []
            for head in range(each):
                q = q_ref[head, here, :]
                edge = dot_t(q, k_ref[head, low:high, :]) + bias[block, :, : high - low]
                before = dot_t(q, k_ref[head, :low, :]) if block else None
                states.append((edge, before))
            for head, (edge, before) in enumerate(states):
                top = jnp.max(edge, axis=1, keepdims=True)
                if block:
                    top = jnp.maximum(top, jnp.max(before, axis=1, keepdims=True))
                shift = top * factor
                weight = jnp.exp2(edge * factor - shift)
                total = jnp.sum(weight, axis=1, keepdims=True)
                out = dot(weight.astype(BF16), v_ref[head, low:high, :])
                if block:
                    weight = jnp.exp2(before * factor - shift)
                    total = total + jnp.sum(weight, axis=1, keepdims=True)
                    out = out + dot(weight.astype(BF16), v_ref[head, :low, :])
                o_ref[head, here, :] = (out * (1.0 / total)).astype(BF16)
                logs = jnp.broadcast_to(shift + jnp.log2(total), (rows, 128))
                log_ref[head, :, here] = logs.T[:1]

        for block in range(count):
            if block == count - 1:
                one(block, 0)
                continue
            wide = crosses(starts_ref, (block + 1) * rows)
            pl.when(wide)(functools.partial(one, block, 1))
            pl.when(jnp.logical_not(wide))(functools.partial(one, block, 0))

    spec = pl.BlockSpec((each, length, HDIM), lambda h: (h, 0, 0))
    return call(
        kernel,
        [jax.ShapeDtypeStruct(query.shape, BF16), jax.ShapeDtypeStruct((heads, 1, length), F32)],
        [smem(), spec, spec, spec],
        [spec, pl.BlockSpec((each, 1, length), lambda h: (h, 0, 0))],
        [pltpu.VMEM((count, rows, 2 * rows), F32)],
        4 * heads * length * length * HDIM * 4,
        16 * heads * length * HDIM,
        "attend",
        limit=56,
        grid=(heads // each,),
    )(starts, query, key, value)


def attend_back(
    starts, place, query, key, value, mixed, logs, near, far, cosine, sine, narrow, b_heads, rows, first, heads
):
    length = query.shape[1]
    thin = narrow.shape[0]
    rank = thin // 3
    count = length // rows
    scale = 1.0 / math.sqrt(HDIM)
    factor = LOG2E * scale

    def kernel(
        starts_ref, place_ref, q_ref, k_ref, v_ref, o_ref, log_ref, near_ref, far_ref, cos_ref, sin_ref,
        narrow_ref, b_ref, dq_ref, dk_ref, dv_ref, thin_ref, out_ref,
        bias, key_sum, value_sum, key_turned, query_sum,
    ):
        fill_bias(bias, starts_ref, rows)
        ones = jnp.ones((8, HDIM), BF16)
        for head in range(heads):
            key_turned[head] = k_ref[head].astype(F32).T.astype(BF16)

        def pair(head, query, keys, mask, new, many=1):
            q, g, logs, inner = query
            here = slice(keys * rows, (keys + many) * rows)
            raw = dot_t(k_ref[head, here, :], q)
            if mask is not None:
                raw = raw + mask
            probs = jnp.exp2(raw * factor - logs)
            grad_probs = dot_t(v_ref[head, here, :], g)
            grad_scores = (probs * (grad_probs - inner)).astype(BF16)
            value_term = dot(probs.astype(BF16), g)
            key_term = dot(grad_scores, q)
            if new:
                value_sum[head, here, :] = value_term
                key_sum[head, here, :] = key_term
            else:
                value_sum[head, here, :] += value_term
                key_sum[head, here, :] += key_term
            return dot(key_turned[head, :, here], grad_scores)

        for block in reversed(range(count)):
            here = slice(block * rows, (block + 1) * rows)
            relative = place_ref[0] ^ block
            at = pl.multiple_of((relative % 2) * rows, rows)
            queries = []
            for head in range(heads):
                g = jnp.where(
                    relative < 2, near_ref[head, pl.ds(at, rows), :], far_ref[head, pl.ds(at, rows), :]
                )
                product = g.astype(F32) * o_ref[head, here, :].astype(F32)
                high = product.astype(BF16)
                low = (product - high.astype(F32)).astype(BF16)
                inner = (dot_t(ones, high) + dot_t(ones, low))[:1]
                queries.append((q_ref[head, here, :], g, log_ref[head, :, here], inner))
            last = block == count - 1
            totals = [pair(head, queries[head], block, bias[block, :rows, :], last) for head in range(heads)]
            for keys in range(0, block, 4):
                for head in range(heads):
                    totals[head] = totals[head] + pair(
                        head, queries[head], keys, None, last, min(4, block - keys)
                    )
            if not last:
                for head in range(heads):
                    query_sum[head] = totals[head]

                @pl.when(crosses(starts_ref, (block + 1) * rows))
                def _():
                    for head in range(heads):
                        query_sum[head] += pair(head, queries[head], block + 1, bias[block, rows:, :], False)

                totals = [query_sum[head] for head in range(heads)]
            for head in range(heads):
                dq_ref[head, here, :] = turn(
                    totals[head].T * scale, cos_ref[here, :], -sin_ref[here, :]
                ).astype(BF16)
        thins = [None] * 3
        sums = [[], [], []]
        for head in range(heads):
            dk_ref[head] = turn(key_sum[head] * scale, cos_ref[...], -sin_ref[...]).astype(BF16)
            dv_ref[head] = value_sum[head].astype(BF16)
            for number, ref in enumerate((dq_ref, dk_ref, dv_ref)):
                here = slice(number * rank, (number + 1) * rank)
                term = dot_t(b_ref[head, here, :], ref[head])
                thins[number] = term if head == 0 else thins[number] + term
                sums[number].append(dot(narrow_ref[here, :], ref[head]))
        for number in range(3):
            here = slice(number * rank, (number + 1) * rank)
            thin_ref[here, :] = thins[number]
            out_ref[here, :] = jnp.concatenate(sums[number], axis=1)

    step = first // heads
    spec = pl.BlockSpec((heads, length, HDIM), lambda h: (step, 0, 0))
    half = pl.BlockSpec((heads, length // 2, HDIM), lambda h: (step, 0, 0))
    out = pl.BlockSpec((heads, length, HDIM), lambda h: (0, 0, 0))
    table = pl.BlockSpec((length, HDIM), lambda h: (0, 0))
    thin_spec = pl.BlockSpec((thin, length), lambda h: (0, 0))
    return call(
        kernel,
        [jax.ShapeDtypeStruct((heads, length, HDIM), BF16)] * 3
        + [
            jax.ShapeDtypeStruct((thin, length), F32),
            jax.ShapeDtypeStruct((thin, heads * HDIM), F32),
        ],
        [smem(), smem(), spec, spec, spec, spec]
        + [pl.BlockSpec((heads, 1, length), lambda h: (step, 0, 0)), half, half, table, table, thin_spec]
        + [pl.BlockSpec((heads, thin, HDIM), lambda h: (step, 0, 0))],
        [out] * 3 + [thin_spec, pl.BlockSpec((thin, heads * HDIM), lambda h: (0, 0))],
        [
            pltpu.VMEM((count, 2 * rows, rows), F32),
            pltpu.VMEM((heads, length, HDIM), F32),
            pltpu.VMEM((heads, length, HDIM), F32),
            pltpu.VMEM((heads, HDIM, length), BF16),
            pltpu.VMEM((heads, HDIM, rows), F32),
        ],
        10 * heads * length * length * HDIM * 4,
        32 * heads * length * HDIM,
        "attend_back",
        limit=32,
        grid=(1,),
    )(
        starts, place[None], query, key, value, mixed, logs, near, far, cosine, sine, narrow, b_heads
    )


def rows_by_heads(refs, start, rows):
    return jnp.concatenate(
        [ref[head, pl.ds(start, rows), :] for ref in refs for head in range(ref.shape[0])], axis=1
    )


def close_attention(mixed, place, weight, a_out, wanted, rows):
    size, width = weight.shape
    rank = a_out.shape[0]

    def kernel(place_ref, m_ref, w_ref, a_ref, *outs):
        for block, out in zip(wanted, outs):
            start = pl.multiple_of((place_ref[0] ^ block) * rows, rows)
            here = rows_by_heads([m_ref], start, rows)
            out[:, :width] = dot(here, w_ref[...]).astype(BF16)
            narrow = dot_t(here, a_ref[...]).astype(BF16)
            out[:, width:] = jnp.concatenate(
                [narrow, jnp.zeros((rows, EXTRA - rank), BF16)], axis=1
            )

    return call(
        kernel,
        [jax.ShapeDtypeStruct((rows, width + EXTRA), BF16)] * len(wanted),
        [smem()] + [vmem()] * 3,
        [vmem()] * len(wanted),
        [],
        2 * rows * len(wanted) * size * width,
        2 * size * width + 2 * rows * len(wanted) * (width + size),
        "close_attention",
        limit=28,
    )(place[None], mixed, weight, a_out)


def open_attention(blocks, seconds, wanted, place, mixed, weight, a_out, b_out):
    rows, width_ext = blocks[0].shape
    size, width = weight.shape
    rank = a_out.shape[0]
    count = len(blocks)
    heads = size // HDIM

    def kernel(place_ref, *refs):
        g_refs, refs = refs[:count], refs[count:]
        s_refs, refs = refs[:count], refs[count:]
        m_ref, w_ref, a_ref, b_ref, out, sum_ref, wide_ref = refs
        total, branch, second = None, None, None
        for block in range(count):
            start = pl.multiple_of((place_ref[0] ^ wanted[block]) * rows, rows)
            grad = g_refs[block][:, :width]
            thin = g_refs[block][:, width:]
            narrow = dot_t(grad, b_ref[...]).astype(BF16)
            back = dot_t(grad, w_ref[...]) + dot(narrow, a_ref[...])
            for head in range(heads):
                part = back[:, head * HDIM : (head + 1) * HDIM]
                out[head, block * rows : (block + 1) * rows, :] = part.astype(BF16)
            terms = (
                t_dot(narrow, rows_by_heads([m_ref], start, rows)),
                t_dot(thin, grad)[:rank],
                t_dot(thin, s_refs[block][...])[rank : 3 * rank],
            )
            if block == 0:
                total, branch, second = terms
            else:
                total, branch, second = total + terms[0], branch + terms[1], second + terms[2]
        sum_ref[...] = total
        wide_ref[:rank, :] = branch
        wide_ref[rank:, :] = second

    return call(
        kernel,
        [
            jax.ShapeDtypeStruct((heads, rows * count, HDIM), BF16),
            jax.ShapeDtypeStruct((rank, size), F32),
            jax.ShapeDtypeStruct((3 * rank, width), F32),
        ],
        [smem()] + [vmem()] * (2 * count + 4),
        [vmem()] * 3,
        [],
        2 * rows * count * size * width,
        2 * size * width + 2 * rows * count * (2 * width + 2 * size),
        "open_attention",
        limit=32,
    )(place[None], *blocks, *seconds, mixed, weight, a_out, b_out)


def feed_forward(blocks, grads, offsets, pieces, down, a_mlp, b_down, a_hidden, b_hidden):
    rows, width = blocks[0].shape
    count = len(blocks)
    size = down.shape[0]
    rank = b_down.shape[0]
    n = len(pieces)

    def kernel(offsets_ref, *refs):
        x_refs, refs = refs[:count], refs[count:]
        g_refs, refs = refs[:count], refs[count:]
        piece_refs, refs = refs[:n], refs[n:]
        down_hbm, am_ref, bd_ref, ah_ref, bh_ref = refs[:5]
        refs = refs[5:]
        feed_refs, refs = refs[:count], refs[count:]
        back_refs, refs = refs[:count], refs[count:]
        sum_ref, whole, down_ref, grad_ref, sems, down_sem = refs
        down_copy = pltpu.make_async_copy(down_hbm, down_ref, down_sem)
        down_copy.start()
        copies = load_pieces(offsets_ref, piece_refs, whole, sems)
        x = jnp.concatenate([ref[...] for ref in x_refs], axis=0)
        grad = jnp.concatenate([ref[...] for ref in g_refs], axis=0)
        narrow = dot_t(x, am_ref[...]).astype(BF16)
        thin = dot_t(grad, bd_ref[...]).astype(BF16)
        down_copy.wait()
        grad_ref[...] = (dot_t(grad, down_ref[...]) + dot(thin, ah_ref[...])).astype(BF16)
        for copy in copies:
            copy.wait()
        gate = dot(x, whole[0]) + dot(narrow[:, :rank], bh_ref[0])
        up = dot(x, whole[1]) + dot(narrow[:, rank:], bh_ref[1])
        sigmoid = 0.5 + 0.5 * jnp.tanh(0.5 * gate)
        silu = gate * sigmoid
        hidden = (silu * up).astype(BF16)
        grad_hidden = grad_ref[...].astype(F32)
        grad_up = (grad_hidden * silu).astype(BF16)
        grad_gate = (grad_hidden * up * (sigmoid + silu * (1.0 - sigmoid))).astype(BF16)
        feed = dot(hidden, down_ref[...]).astype(BF16)
        feed_thin = dot_t(hidden, ah_ref[...]).astype(BF16)
        back = (dot_t(grad_gate, whole[0]) + dot_t(grad_up, whole[1])).astype(BF16)
        back_thin = jnp.concatenate(
            [dot_t(grad_gate, bh_ref[0]).astype(BF16), dot_t(grad_up, bh_ref[1]).astype(BF16)], axis=1
        )
        for block in range(count):
            here = slice(block * rows, (block + 1) * rows)
            feed_refs[block][:, :width] = feed[here]
            feed_refs[block][:, width:] = jnp.concatenate(
                [feed_thin[here], jnp.zeros((rows, EXTRA - rank), BF16)], axis=1
            )
            back_refs[block][:, :width] = back[here]
            back_refs[block][:, width:] = jnp.concatenate(
                [back_thin[here], jnp.zeros((rows, EXTRA - 2 * rank), BF16)], axis=1
            )
        sum_ref[:rank, :] = t_dot(thin, hidden)
        sum_ref[rank : 2 * rank, :] = t_dot(narrow[:, :rank], grad_gate)
        sum_ref[2 * rank :, :] = t_dot(narrow[:, rank:], grad_up)

    out = jax.ShapeDtypeStruct((rows, width + EXTRA), BF16)
    return call(
        kernel,
        [out] * (2 * count)
        + [jax.ShapeDtypeStruct((3 * rank, size), F32)],
        [smem()] + [vmem()] * (2 * count) + [anywhere()] * (n + 1) + [vmem()] * 4,
        [vmem()] * (2 * count + 1),
        [
            pltpu.VMEM((2, width, size), BF16),
            pltpu.VMEM((size, width), BF16),
            pltpu.VMEM((count * rows, size), BF16),
            pltpu.SemaphoreType.DMA((n,)),
            pltpu.SemaphoreType.DMA,
        ],
        12 * rows * count * width * size,
        6 * width * size + 8 * rows * count * width,
        "feed_forward",
    )(offsets, *blocks, *grads, *pieces, down, a_mlp, b_down, a_hidden, b_hidden)


def project_back(grads, place, offsets, pieces, wanted, rows):
    size = pieces[0].shape[1]
    width = 4 * pieces[0].shape[0]
    n = len(pieces)
    count = len(wanted)

    def kernel(place_ref, offsets_ref, *refs):
        g_refs, refs = refs[: len(grads)], refs[len(grads) :]
        piece_refs, refs = refs[:n], refs[n:]
        back_refs, (whole, sems) = refs[:count], refs[count:]
        copies = load_pieces(offsets_ref, piece_refs, whole, sems)
        starts = [pl.multiple_of((place_ref[0] ^ block) * rows, rows) for block in wanted]
        parts = [rows_by_heads(g_refs, start, rows) for start in starts]
        for copy in copies:
            copy.wait()
        for part, back in zip(parts, back_refs):
            back[...] = dot_t(part, whole[...]).astype(BF16)

    return call(
        kernel,
        [jax.ShapeDtypeStruct((rows, width), BF16)] * count,
        [smem(), smem()] + [vmem()] * len(grads) + [anywhere()] * n,
        [vmem()] * count,
        [pltpu.VMEM((width, size), BF16), pltpu.SemaphoreType.DMA((n,))],
        2 * rows * count * width * size,
        2 * (rows * count * (width + size) + width * size),
        "project_back",
        limit=56,
    )(place[None], offsets, *grads, *pieces)


def thin_product(thin, place, blocks):
    rows, width = blocks[0].shape
    count = len(blocks)

    def kernel(place_ref, thin_ref, *refs):
        total = None
        for block in range(count):
            start = pl.multiple_of((place_ref[0] ^ block) * rows, rows)
            term = dot(thin_ref[:, pl.ds(start, rows)], refs[block][...])
            total = term if total is None else total + term
        refs[count][...] = total

    return call(
        kernel,
        jax.ShapeDtypeStruct((thin.shape[0], width), F32),
        [smem()] + [vmem()] * (count + 1),
        vmem(),
        [],
        2 * 128 * rows * count * width,
        2 * rows * count * width,
        "thin_product",
        limit=24,
    )(place[None], thin, *blocks)


def shards(
    tokens,
    cotangent,
    sequence_adapter_index,
    image_span_start,
    attention_norm_gain,
    feedforward_norm_gain,
    query_key_value_weight,
    attention_output_weight,
    gate_up_projection_weight,
    down_projection_weight,
    adapter_model_input_maps,
    adapter_model_output_maps,
    adapter_hidden_input_map,
    adapter_hidden_output_maps,
):
    rows = tokens.shape[1]
    width = tokens.shape[2]
    rank = adapter_model_input_maps.shape[2]
    group = lax.axis_size("shard")
    place = lax.axis_index("shard").astype(jnp.int32)
    rep_place = lax.axis_index("rep").astype(jnp.int32)
    pick = sequence_adapter_index[0]
    starts = image_span_start[0]
    head_cols = width // group
    ff_cols = down_projection_weight.shape[0]
    k_rows = query_key_value_weight.shape[1]

    gain_one = attention_norm_gain.astype(F32)
    gain_two = feedforward_norm_gain.astype(F32)
    residual_in = tokens[0].astype(F32)
    grad_out = cotangent[0].astype(F32)

    def own_columns(values, size):
        return lax.dynamic_slice_in_dim(values, place * size, size, values.ndim - 1)

    quarter = k_rows // 4
    quarter_one, quarter_two = sides(
        query_key_value_weight, rep_place % 4 * quarter, quarter, place, head_cols, (2, 3), "sides_far"
    )
    first_a = hop(quarter_one, "shard", 2)
    normed = norm_rows(residual_in, gain_one).astype(BF16)
    front_chip, front_part = chip_picked(
        jnp.concatenate([adapter_model_input_maps[0:3], adapter_model_output_maps[0:3]]), pick, place
    )
    first_a, front_part, quarter_two, normed, qkv = fence(
        first_a, front_part, quarter_two, normed, query_key_value_weight
    )
    first_b = hop(quarter_two, "shard", 3)
    first_a_two, first_a_three = hop(first_a, "rep", 2), hop(first_a, "rep", 1)
    first_own, near_out = sides(qkv, 0, k_rows, place, head_cols, (0, 1), "sides_near")
    normed_near = core(normed)
    first_b, front_part, near_out, rest_bank, wide_bank = fence(
        first_b, front_part, near_out,
        (adapter_model_input_maps[3:6], adapter_model_output_maps[3:5]),
        (adapter_hidden_input_map[None], adapter_hidden_output_maps),
    )
    front_far = across(front_part)
    first_b_two, first_b_three = hop(first_b, "rep", 1), hop(first_b, "rep", 2)
    front_far, normed, first_a_two, first_a_three = fence(front_far, normed, first_a_two, first_a_three)
    normed_far = across(normed)
    first_a_four = hop(first_a_two, "rep", 1)
    first_near = core(near_out)
    rest_chip, rest_part = chip_picked(jnp.concatenate(rest_bank), pick, place)
    wide_chip, wide_part = chip_picked(jnp.concatenate(wide_bank), pick, place)
    first_b_two, first_b_three, gate_up, grad_out, front_chip = fence(
        first_b_two, first_b_three, gate_up_projection_weight, grad_out, front_chip
    )
    first_b_four = hop(first_b_two, "rep", 2)
    mlp_leaving = [side(gate_up, rep_place % 4 * quarter, quarter, place ^ j, ff_cols) for j in (2, 3)]
    grad_feed = (BRANCH * grad_out).astype(BF16)
    half = HDIM // 2
    frequency = jnp.exp(jnp.arange(half, dtype=F32) * (-2.0 / HDIM) * math.log(THETA))
    angle = jnp.arange(rows * group, dtype=jnp.int32).astype(F32)[:, None] * frequency[None, :]
    cosine = jnp.concatenate([jnp.cos(angle), jnp.cos(angle)], axis=1)
    sine = jnp.concatenate([jnp.sin(angle), jnp.sin(angle)], axis=1)
    cosine_pair = jnp.concatenate([jnp.cos(angle)] * 4, axis=1)
    sine_pair = jnp.concatenate([-jnp.sin(angle), jnp.sin(angle)] * 2, axis=1)
    tables = (cosine, sine, cosine_pair, sine_pair)
    front = whole_picked(front_chip, front_far, place)
    a_first = front[:3].reshape(3 * rank, width)
    b_first = own_columns(front[3:], head_cols)
    b_wide = jnp.concatenate(
        [jnp.pad(b_first[i], ((0, 0), (i * head_cols, (2 - i) * head_cols))) for i in range(3)]
    )
    (
        normed_far, first_a_four, first_b_four, mlp_leaving, grad_feed, b_wide, a_first, rest_part, wide_part,
        tables,
    ) = fence(
        normed_far, first_a_four, first_b_four, mlp_leaving, grad_feed, b_wide, a_first, rest_part, wide_part,
        tables,
    )
    cosine, sine, cosine_pair, sine_pair = tables
    first_blocks = (normed, normed_near, normed_far, core(normed_far))
    first_offsets, first_pieces = arrange(
        k_rows, first_own, first_near,
        (
            (first_a, first_a_two, first_a_three, first_a_four),
            (first_b, first_b_two, first_b_three, first_b_four),
        ),
        place, rep_place,
    )

    mlp_a, mlp_b = hop(mlp_leaving[0], "shard", 2), hop(mlp_leaving[1], "shard", 3)
    query, key, value, narrow_first = project(
        first_blocks, place, first_offsets, first_pieces, a_first, b_wide, cosine_pair, sine_pair
    )
    query, mlp_a, rest_part, wide_part = fence(query, mlp_a, rest_part, wide_part)
    mlp_a_two, mlp_a_three = hop(mlp_a, "rep", 2), hop(mlp_a, "rep", 1)
    rest_far, wide_far = across(rest_part), across(wide_part)
    mixed, logs = attend(starts, query, key, value, rows)
    mixed, mlp_b, mlp_a_two, mlp_a_three, rest_far = fence(
        mixed, mlp_b, mlp_a_two, mlp_a_three, rest_far
    )
    mlp_b_two, mlp_b_three = hop(mlp_b, "rep", 1), hop(mlp_b, "rep", 2)
    rest = whole_picked(rest_chip, rest_far, place)
    a_out = own_columns(rest[0], head_cols)
    a_mlp = rest[1:3].reshape(2 * rank, width)
    b_out, b_down = rest[3], rest[4]
    far_out = close_attention(mixed, place, attention_output_weight, a_out, (2, 3), rows)
    far_sum = (far_out[0].astype(F32) + core(far_out[1]).astype(F32)).astype(BF16)
    far_sum, mixed_here, grad_feed, wide_far = fence(far_sum, mixed, grad_feed, wide_far)
    branch_low, far_rest = across(far_sum[: rows // 2]), far_sum[rows // 2 :]
    feed_near_in = core(grad_feed)
    near_out = close_attention(mixed_here, place, attention_output_weight, a_out, (0, 1), rows)
    near_out, gate_up = fence(near_out, gate_up)
    mlp_near_out = side(gate_up, 0, k_rows, place ^ 1, ff_cols)
    mlp_own = side(gate_up, 0, k_rows, place, ff_cols)
    near_out, mlp_b_two, mlp_b_three, branch_low, far_rest, mlp_near_out, mlp_own = fence(
        near_out, mlp_b_two, mlp_b_three, branch_low, far_rest, mlp_near_out, mlp_own
    )
    mlp_a_four, mlp_b_four = hop(mlp_a_two, "rep", 1), hop(mlp_b_two, "rep", 2)
    branch_high = across(far_rest)
    near_here = core(near_out[1])
    mlp_near = core(mlp_near_out)
    hidden_cols = own_columns(whole_picked(wide_chip, wide_far, place), ff_cols)
    near_here, branch_high, hidden_cols, mlp_own = fence(near_here, branch_high, hidden_cols, mlp_own)
    branch_far = jnp.concatenate([branch_low, branch_high])
    feed_low = across(after(grad_feed[: rows // 2], branch_high))
    feed_rest = after(grad_feed[rows // 2 :], branch_high)
    a_hidden, b_hidden = hidden_cols[0], hidden_cols[1:]
    branch_own = near_out[0].astype(F32) + near_here.astype(F32) + branch_far.astype(F32)
    narrow_out = branch_own[:, width : width + rank].astype(BF16)
    branch = branch_own[:, :width] + dot(narrow_out, b_out)
    middle = residual_in + BRANCH * branch
    normed_second = norm_rows(middle, gain_two).astype(BF16)
    second_far = across(normed_second)
    second_near = core(normed_second)
    second_near, feed_near_in, mlp_near, mlp_a_four, mlp_b_four, feed_low = fence(
        second_near, feed_near_in, mlp_near, mlp_a_four, mlp_b_four, feed_low
    )
    feed_high = across(feed_rest)
    mlp_offsets, mlp_pieces = arrange(
        k_rows, mlp_own, mlp_near,
        (
            (mlp_a, mlp_a_two, mlp_a_three, mlp_a_four),
            (mlp_b, mlp_b_two, mlp_b_three, mlp_b_four),
        ),
        place, rep_place,
    )
    *parts, sum_near = feed_forward(
        (normed_second, second_near), (grad_feed, feed_near_in), mlp_offsets, mlp_pieces,
        down_projection_weight, a_mlp, b_down, a_hidden, b_hidden,
    )
    feed_near, back_near = parts[:2], parts[2:]
    second_far, feed_high, back_near, feed_near = fence(second_far, feed_high, back_near, feed_near)
    feed_far_in = jnp.concatenate([feed_low, feed_high])
    second_blocks = (normed_second, second_near, second_far, core(second_far))
    feed_blocks = (grad_feed, feed_near_in, feed_far_in, core(feed_far_in))
    *parts, sum_far = feed_forward(
        second_blocks[2:], feed_blocks[2:], mlp_offsets, mlp_pieces, down_projection_weight,
        a_mlp, b_down, a_hidden, b_hidden,
    )
    feed_far, back_far = parts[:2], parts[2:]
    back_sum = (back_far[0].astype(F32) + core(back_far[1]).astype(F32)).astype(BF16)
    back_sum, back_near, feed_near, feed_far, sum_near = fence(
        back_sum, back_near, feed_near, feed_far, sum_near
    )
    back_low, back_rest = across(back_sum[: rows // 2]), back_sum[rows // 2 :]

    bits = reps_bits()
    back_here = core(back_near[1])
    feed_here = core(feed_near[1])
    feed_mate = core(feed_far[1])
    mark = jnp.full((rank, ff_cols), pick.astype(F32))
    wide_all = jnp.concatenate([sum_near + sum_far, mark]).astype(BF16)[None]
    wide_hop = hop(wide_all, "rep", bits[0])
    back_low, feed_here, feed_mate, back_here, back_rest, sum_near = fence(
        back_low, feed_here, feed_mate, back_here, back_rest, sum_near
    )
    back_high = across(back_rest)
    feed_here = feed_near[0].astype(F32) + feed_here.astype(F32)
    feed_sum = (feed_far[0].astype(F32) + feed_mate.astype(F32)).astype(BF16)
    back_high, feed_here, feed_sum, back_here, wide_hop = fence(
        back_high, feed_here, feed_sum, back_here, wide_hop
    )
    back_from_far = jnp.concatenate([back_low, back_high])
    second_own = back_near[0].astype(F32) + back_here.astype(F32) + back_from_far.astype(F32)
    grad_narrow_mlp = second_own[:, width : width + 2 * rank].astype(BF16)
    grad_normed_second = second_own[:, :width] + dot(grad_narrow_mlp, a_mlp)
    grad_middle = grad_out + norm_back(middle, gain_two, grad_normed_second)
    grad_branch = (BRANCH * grad_middle).astype(BF16)
    branch_rows = pad_columns([grad_branch, narrow_out, grad_narrow_mlp], width + EXTRA)
    branch_rows, wide_hop = fence(branch_rows, wide_hop)
    branch_far_in = across(branch_rows)
    branch_near_in = core(branch_rows)
    wide_all = both(wide_all, wide_hop, rep_place, bits[0])
    for bit in bits[1:-2]:
        wide_all = both(wide_all, hop(wide_all, "rep", bit), rep_place, bit)
    wide_hop = hop(wide_all, "rep", bits[-2])
    branch_near_in, wide_all = fence(branch_near_in, wide_all)
    mixed_near, grad_a_near, thin_near = open_attention(
        (branch_rows, branch_near_in), second_blocks[:2], (0, 1), place, mixed,
        attention_output_weight, a_out, b_out,
    )
    mixed_near, wide_hop = fence(mixed_near, wide_hop)
    wide_all = both(wide_all, wide_hop, rep_place, bits[-2])
    wide_hop = hop(wide_all, "rep", bits[-1])
    branch_far_in, mixed_near, wide_all = fence(branch_far_in, mixed_near, wide_all)
    feed_from_far = across(after(feed_sum, branch_far_in))
    mixed_far, grad_a_far, thin_far = open_attention(
        (branch_far_in, core(branch_far_in)), second_blocks[2:], (2, 3), place, mixed,
        attention_output_weight, a_out, b_out,
    )

    b_heads = b_first.reshape(3 * rank, head_cols // HDIM, HDIM).transpose(1, 0, 2)

    def attend_part(first, heads, starts):
        return attend_back(
            starts, place, query, key, value, mixed, logs, mixed_near, mixed_far, cosine, sine,
            narrow_first, b_heads, rows, first, heads,
        )

    mixed_far, starts_one, wide_all = fence(mixed_far, starts, wide_all)
    heads = query.shape[0]
    third = heads // 3
    part_one = attend_part(0, third, starts_one)
    part_one, feed_from_far, wide_hop, starts_two = fence(part_one, feed_from_far, wide_hop, starts_one)
    wide_all = both(wide_all, wide_hop, rep_place, bits[-1])
    picks = wide_all[:, -1, :1].astype(F32)
    adapters = adapter_model_input_maps.shape[1] * group
    chosen = (picks == jnp.arange(adapters, dtype=jnp.int32).astype(F32)[None, :]).astype(F32)
    wide_sent = send_sums(wide_all[:, :-rank], chosen, place, rank)
    feed_own = feed_here + feed_from_far.astype(F32)
    narrow_down = feed_own[:, width : width + rank].astype(BF16)
    down_far = across(narrow_down)
    down_near = core(narrow_down)
    starts_two, narrow_down = fence(starts_two, narrow_down)
    part_two = attend_part(third, third, starts_two)
    part_two, down_far, down_near, starts_three, wide_sent = fence(
        part_two, down_far, down_near, starts_two, wide_sent
    )
    down_thin = (narrow_down, down_near, down_far, core(down_far))
    grad_b_down = sum(t_dot(left, right) for left, right in zip(down_thin, feed_blocks))
    early_all = jnp.concatenate(
        [
            grad_a_near + grad_a_far,
            own_columns(jnp.concatenate([thin_near + thin_far, grad_b_down]), head_cols),
        ]
    ).astype(BF16)[None]
    early_hop = hop(early_all, "rep", bits[0])
    early_all, starts_three = fence(early_all, starts_three)
    part_three = attend_part(2 * third, heads - 2 * third, starts_three)
    part_three, early_hop = fence(part_three, early_hop)
    parts = (part_one, part_two, part_three)
    first_grads = [part[number] for number in range(3) for part in parts]
    thin = (part_one[3] + part_two[3] + part_three[3]).astype(BF16)
    thin_hop = core(thin)
    early_all = both(early_all, early_hop, rep_place, bits[0])
    for bit in bits[1:-2]:
        early_all = both(early_all, hop(early_all, "rep", bit), rep_place, bit)
    grad_b_first = jnp.concatenate([part[4] for part in parts], axis=1)
    thin = (thin.astype(F32) + thin_hop.astype(F32)).astype(BF16)
    thin, early_all, grad_b_first = fence(thin, early_all, grad_b_first)
    thin_hop = across(thin)
    early_hop = hop(early_all, "rep", bits[-2])
    grad_narrow = (thin.astype(F32) + thin_hop.astype(F32)).astype(BF16)
    late_all = jnp.concatenate(
        [own_columns(thin_product(grad_narrow, place, first_blocks), head_cols), grad_b_first]
    ).astype(BF16)[None]
    late_all, first_grads = fence(late_all, first_grads)
    late_hop = hop(late_all, "rep", bits[0])
    back_rows_far = project_back(first_grads, place, first_offsets, first_pieces, (2, 3), rows)
    back_rows_far, late_hop, early_hop = fence(back_rows_far, late_hop, early_hop)
    back_mate = core(back_rows_far[1])
    late_all = both(late_all, late_hop, rep_place, bits[0])
    for bit in bits[1:-2]:
        late_all = both(late_all, hop(late_all, "rep", bit), rep_place, bit)
    late_hop = hop(late_all, "rep", bits[-2])
    early_all = both(early_all, early_hop, rep_place, bits[-2])
    early_hop = hop(early_all, "rep", bits[-1])
    back_sum = (back_rows_far[0].astype(F32) + back_mate.astype(F32)).astype(BF16)
    back_sum, first_grads, early_all, late_all = fence(back_sum, first_grads, early_all, late_all)
    back_low, back_high = across(back_sum[: rows // 2]), across(back_sum[rows // 2 :])
    back_rows_near = project_back(first_grads, place, first_offsets, first_pieces, (0, 1), rows)
    back_rows_near, late_hop, early_hop, back_low = fence(back_rows_near, late_hop, early_hop, back_low)
    back_rows_here = core(back_rows_near[1])
    late_all = both(late_all, late_hop, rep_place, bits[-2])
    late_all, early_hop, early_all = fence(late_all, early_hop, early_all)
    late_hop = hop(late_all, "rep", bits[-1])
    early_sent = send_sums(both(early_all, early_hop, rep_place, bits[-1]), chosen, place, rank)

    def whole_maps(stacked, low, high):
        part = stacked[:, low // rank : high // rank]
        pieces = [lax.dynamic_index_in_dim(part, place ^ i, 0, keepdims=False) for i in range(group)]
        return jnp.concatenate(pieces, axis=-1).astype(F32)

    feed = feed_here[:, :width] + feed_from_far[:, :width].astype(F32) + dot(narrow_down, b_down)
    output = (middle + BRANCH * feed).astype(BF16)
    hidden_maps = whole_maps(jnp.stack(wide_sent), 0, 3 * rank)
    late_hop, hidden_maps, output, back_high, back_rows_here = fence(
        late_hop, hidden_maps, output, back_high, back_rows_here
    )
    back_far_in = jnp.concatenate([back_low, back_high])
    late_sent = send_sums(both(late_all, late_hop, rep_place, bits[-1]), chosen, place, rank)
    narrow_own = lax.dynamic_slice_in_dim(grad_narrow, place * rows, rows, 1)
    grad_normed = (
        back_rows_near[0].astype(F32) + back_rows_here.astype(F32) + back_far_in.astype(F32)
        + t_dot(narrow_own, a_first)
    )
    input_grad = grad_middle + norm_back(residual_in, gain_one, grad_normed)
    late_sent, input_grad, early_sent = fence(late_sent, input_grad, early_sent)
    early_got = jnp.stack(early_sent)
    late_got = jnp.stack(late_sent)
    grad_a_model = jnp.concatenate(
        [
            whole_maps(late_got, 0, 3 * rank),
            whole_maps(early_got, 0, rank),
            whole_maps(early_got, 2 * rank, 4 * rank),
        ]
    )
    grad_b_model = jnp.concatenate(
        [
            whole_maps(late_got, 3 * rank, 6 * rank),
            whole_maps(early_got, rank, 2 * rank),
            whole_maps(early_got, 4 * rank, 5 * rank),
        ]
    )
    return (
        output[None], input_grad[None], grad_a_model, grad_b_model, hidden_maps[0], hidden_maps[1:3],
    )


def solution(mesh):
    in_specs = (
        P("rep", "shard", None),
        P("rep", "shard", None),
        P("rep"),
        P("rep", None),
        P(),
        P(),
        P(None, "shard", None),
        P("shard", None),
        P(None, "shard", None),
        P("shard", None),
        P(None, "shard", None, None),
        P(None, "shard", None, None),
        P("shard", None, None),
        P(None, "shard", None, None),
    )
    out_specs = (
        P("rep", "shard", None),
        P("rep", "shard", None),
        P(None, "shard", None, None),
        P(None, "shard", None, None),
        P("shard", None, None),
        P(None, "shard", None, None),
    )
    return jax.shard_map(shards, mesh=mesh, in_specs=in_specs, out_specs=out_specs, check_vma=False)
```

```python
import functools
import math

import jax
import jax.numpy as jnp
from jax import lax
from jax.experimental import pallas as pl
from jax.experimental.pallas import tpu as pltpu
from jax.sharding import PartitionSpec as P

HDIM = 64
SPAN = 256
EPS = 1e-05
THETA = 10000.0
BRANCH = 1.4 / math.sqrt(40.0)
EXTRA = 128
F32 = jnp.float32
BF16 = jnp.bfloat16
LOG2E = math.log2(math.e)


def hop(values, axis, bit):
    size = lax.axis_size(axis)
    return lax.ppermute(values, axis, [(i, i ^ bit) for i in range(size)])


def core(values):
    return hop(values, "shard", 1)


def across(values):
    return hop(values, "shard", 2)


def rows_of(values, count):
    size = values.shape[0] // count
    return tuple(values[i * size : (i + 1) * size] for i in range(count))


def norm_rows(values, gain):
    return values * lax.rsqrt(jnp.mean(values * values, axis=-1, keepdims=True) + EPS) * gain


def norm_back(values, gain, grad):
    width = values.shape[-1]
    scale = lax.rsqrt(jnp.mean(values * values, axis=-1, keepdims=True) + EPS)
    moved = grad * gain
    inner = jnp.sum(values * moved, axis=-1, keepdims=True) / width
    return scale * moved - values * (scale * scale * scale) * inner


def dot(left, right):
    return jnp.dot(left, right, preferred_element_type=F32)


def dot_t(left, right):
    return lax.dot_general(left, right, (((1,), (1,)), ((), ())), preferred_element_type=F32)


def t_dot(left, right):
    return lax.dot_general(left, right, (((0,), (0,)), ((), ())), preferred_element_type=F32)


def pad_columns(pieces, width):
    used = sum(piece.shape[1] for piece in pieces)
    rest = jnp.zeros((pieces[0].shape[0], width - used), pieces[0].dtype)
    return jnp.concatenate(list(pieces) + [rest], axis=1)


def reps_bits():
    bits = []
    bit = 2
    while bit < lax.axis_size("rep"):
        bits.append(bit)
        bit *= 2
    return bits + [1]


def both(held, arrived, rep_place, bit):
    low = jnp.concatenate([held, arrived])
    high = jnp.concatenate([arrived, held])
    return jnp.where((rep_place // bit) % 2 == 0, low, high)


def send_sums(everyone, chosen, place, rank):
    group = lax.axis_size("shard")
    everyone = everyone.reshape(everyone.shape[0], -1, rank, everyone.shape[2])
    per = chosen.shape[1] // group
    sent = []
    for j in range(group):
        marks = lax.dynamic_slice_in_dim(chosen, (place ^ j) * per, per, 1)
        sums = jnp.sum(
            marks[:, None, :, None, None] * everyone[:, :, None].astype(F32), axis=0
        ).astype(BF16)
        sent.append(hop(sums, "shard", j) if j else sums)
    return sent


def chip_picked(bank, pick, place):
    per = bank.shape[1]
    rank = bank.shape[2]
    owner = pick // per
    mine = lax.dynamic_index_in_dim(bank, pick % per, 1, keepdims=False)
    mine = jnp.where(owner == place, mine, jnp.zeros_like(mine))
    chip = mine + core(mine)
    return chip, lax.dynamic_slice_in_dim(chip, (place % 2) * (rank // 2), rank // 2, 1)


def whole_picked(chip, far, place):
    other = core(far)
    low = jnp.where(place % 2 == 0, far, other)
    high = jnp.where(place % 2 == 0, other, far)
    return chip + jnp.concatenate([low, high], axis=1)


def after(value, *others):
    return lax.optimization_barrier((value, others))[0]


def side(weight, row, count, owner, size):
    return lax.dynamic_slice(weight, (0, row, owner * size), (weight.shape[0], count, size))


def sides(weight, row, count, place, size, wanted, name):
    maps, _, columns = weight.shape

    def kernel(where_ref, w_ref, *refs):
        outs, (held, sem) = refs[:-2], refs[-2:]
        start = pl.multiple_of(where_ref[1], 16)
        copy = pltpu.make_async_copy(w_ref.at[:, pl.ds(start, count), :], held, sem)
        copy.start()
        copy.wait()

        def write(out, owner):
            out[...] = jnp.concatenate(
                [held[i, :, owner * size : (owner + 1) * size] for i in range(maps)], axis=1
            )

        for j, out in zip(wanted, outs):
            for owner in range(columns // size):
                pl.when((where_ref[0] ^ j) == owner)(functools.partial(write, out, owner))

    return call(
        kernel,
        [jax.ShapeDtypeStruct((count, maps * size), BF16)] * len(wanted),
        [smem(), anywhere()],
        [vmem()] * len(wanted),
        [pltpu.VMEM((maps, count, columns), BF16), pltpu.SemaphoreType.DMA],
        0,
        2 * maps * count * (columns + size * len(wanted)),
        name,
        limit=58,
    )(jnp.stack([place, jnp.asarray(row, jnp.int32)]), weight)


def arrange(rows, own, near, ways, place, rep_place):
    quarter = rows // 4
    part = rep_place % 4
    pieces = [(place * rows, own), ((place ^ 1) * rows, near)]
    for j, one, two, parts in zip((2, 3), (2, 1), (1, 2), ways):
        for bits, piece in zip((0, one, two, one ^ two), parts):
            pieces.append(((place ^ j) * rows + (part ^ bits) * quarter, piece))
    offsets = jnp.stack([row.astype(jnp.int32) for row, _ in pieces])
    return offsets, [piece for _, piece in pieces]


def fence(*values):
    return lax.optimization_barrier(values)


def load_pieces(offsets, pieces, whole, sems):
    copies = []
    for number, piece in enumerate(pieces):
        start = pl.multiple_of(offsets[number], 16)
        here = pl.ds(start, piece.shape[-2])
        target = whole.at[here, :] if len(piece.shape) == 2 else whole.at[:, here, :]
        copy = pltpu.make_async_copy(piece, target, sems.at[number])
        copy.start()
        copies.append(copy)
    return copies


def vmem():
    return pl.BlockSpec(memory_space=pltpu.VMEM)


def smem():
    return pl.BlockSpec(memory_space=pltpu.SMEM)


def anywhere():
    return pl.BlockSpec(memory_space=pl.ANY)


def call(kernel, outs, in_specs, out_specs, scratch, flops, moved, name, limit=56, **more):
    return pl.pallas_call(
        kernel,
        out_shape=outs,
        in_specs=in_specs,
        out_specs=out_specs,
        scratch_shapes=scratch,
        compiler_params=pltpu.CompilerParams(vmem_limit_bytes=limit << 20),
        cost_estimate=pl.CostEstimate(flops=flops, bytes_accessed=moved, transcendentals=0),
        name=name,
        **more,
    )


def turn(values, cosine, sine):
    half = HDIM // 2
    turned = jnp.concatenate([-values[:, half:], values[:, :half]], axis=1)
    return values * cosine + turned * sine


def project(blocks, place, offsets, pieces, a_first, b_first, cosine_pair, sine_pair):
    rows, width = blocks[0].shape
    count = len(blocks)
    size = pieces[0].shape[1]
    heads = size // (3 * HDIM)
    thin = a_first.shape[0]
    n = len(pieces)

    def kernel(place_ref, offsets_ref, *refs):
        x_refs, refs = refs[:count], refs[count:]
        piece_refs, refs = refs[:n], refs[n:]
        a_ref, b_ref, cos_ref, sin_ref, q_ref, k_ref, v_ref, narrow_ref, whole, sems = refs
        copies = load_pieces(offsets_ref, piece_refs, whole, sems)
        starts = [pl.multiple_of((place_ref[0] ^ block) * rows, rows) for block in range(count)]
        for block in range(count):
            narrow_ref[:, pl.ds(starts[block], rows)] = dot_t(a_ref[...], x_refs[block][...]).astype(BF16)
        for copy in copies:
            copy.wait()
        both = 2 * heads * HDIM
        lane = lax.broadcasted_iota(jnp.int32, (rows, both), 1) % HDIM
        lower = lane < HDIM // 2
        for block in range(count):
            start = starts[block]
            narrow = narrow_ref[:, pl.ds(start, rows)]
            pre = dot(x_refs[block][...], whole[...]) + t_dot(narrow, b_ref[...])
            flat = pre[:, :both]
            cosine_here = jnp.tile(cos_ref[pl.ds(start, rows), :], (1, both // (2 * HDIM)))
            sine_here = jnp.tile(sin_ref[pl.ds(start, rows), :], (1, both // (2 * HDIM)))
            other = jnp.where(
                lower, pltpu.roll(flat, both - HDIM // 2, 1), pltpu.roll(flat, HDIM // 2, 1)
            )
            turned = (flat * cosine_here + other * sine_here).astype(BF16)
            straight = pre[:, both:].astype(BF16)
            for number, out in enumerate((q_ref, k_ref, v_ref)):
                for head in range(heads):
                    at = (number % 2 * heads + head) * HDIM
                    source = turned if number < 2 else straight
                    out[head, pl.ds(start, rows), :] = source[:, at : at + HDIM]

    by_heads = jax.ShapeDtypeStruct((heads, rows * count, HDIM), BF16)
    return call(
        kernel,
        [by_heads] * 3 + [jax.ShapeDtypeStruct((thin, rows * count), BF16)],
        [smem(), smem()] + [vmem()] * count + [anywhere()] * n + [vmem()] * 4,
        [vmem()] * 4,
        [pltpu.VMEM((width, size), BF16), pltpu.SemaphoreType.DMA((n,))],
        2 * rows * count * width * size,
        2 * (rows * count * width + width * size + 2 * rows * count * size),
        "project",
        limit=56,
    )(place[None], offsets, *blocks, *pieces, a_first, b_first, cosine_pair, sine_pair)


def label_of(positions, starts_ref):
    label = jnp.full(positions.shape, -1, jnp.int32)
    for number in range(starts_ref.shape[0]):
        inside = (positions >= starts_ref[number]) & (positions < starts_ref[number] + SPAN)
        label = jnp.where(inside, jnp.int32(number), label)
    return label


def hidden_bias(query_at, key_at, starts_ref):
    query_label = label_of(query_at, starts_ref)
    key_label = label_of(key_at, starts_ref)
    visible = (key_at <= query_at) | (query_label == key_label) & (query_label >= 0)
    return jnp.where(visible, 0.0, -1e30)


def crosses(starts_ref, edge):
    hit = None
    for number in range(starts_ref.shape[0]):
        start = starts_ref[number]
        here = (start < edge) & (start + SPAN > edge)
        hit = here if hit is None else hit | here
    return hit


def fill_bias(bias, starts_ref, rows):
    for block in range(bias.shape[0]):
        shape = (2 * rows, rows)
        query_at = block * rows + lax.broadcasted_iota(jnp.int32, shape, 1)
        key_at = block * rows + lax.broadcasted_iota(jnp.int32, shape, 0)
        bias[block] = hidden_bias(query_at, key_at, starts_ref)


def attend(starts, query, key, value, rows):
    heads, length, _ = query.shape
    count = length // rows
    factor = LOG2E / math.sqrt(HDIM)
    each = 3

    def kernel(starts_ref, q_ref, k_ref, v_ref, o_ref, log_ref, bias):
        @pl.when(pl.program_id(0) == 0)
        def _():
            for block in range(count):
                shape = (rows, 2 * rows)
                query_at = block * rows + lax.broadcasted_iota(jnp.int32, shape, 0)
                key_at = block * rows + lax.broadcasted_iota(jnp.int32, shape, 1)
                bias[block] = hidden_bias(query_at, key_at, starts_ref)

        def one(block, extra):
            low, high = block * rows, (block + 1 + extra) * rows
            here = slice(low, low + rows)
            states = []
            for head in range(each):
                q = q_ref[head, here, :]
                edge = dot_t(q, k_ref[head, low:high, :]) + bias[block, :, : high - low]
                before = dot_t(q, k_ref[head, :low, :]) if block else None
                states.append((edge, before))
            for head, (edge, before) in enumerate(states):
                top = jnp.max(edge, axis=1, keepdims=True)
                if block:
                    top = jnp.maximum(top, jnp.max(before, axis=1, keepdims=True))
                shift = top * factor
                weight = jnp.exp2(edge * factor - shift)
                total = jnp.sum(weight, axis=1, keepdims=True)
                out = dot(weight.astype(BF16), v_ref[head, low:high, :])
                if block:
                    weight = jnp.exp2(before * factor - shift)
                    total = total + jnp.sum(weight, axis=1, keepdims=True)
                    out = out + dot(weight.astype(BF16), v_ref[head, :low, :])
                o_ref[head, here, :] = (out * (1.0 / total)).astype(BF16)
                logs = jnp.broadcast_to(shift + jnp.log2(total), (rows, 128))
                log_ref[head, :, here] = logs.T[:1]

        for block in range(count):
            if block == count - 1:
                one(block, 0)
                continue
            wide = crosses(starts_ref, (block + 1) * rows)
            pl.when(wide)(functools.partial(one, block, 1))
            pl.when(jnp.logical_not(wide))(functools.partial(one, block, 0))

    spec = pl.BlockSpec((each, length, HDIM), lambda h: (h, 0, 0))
    return call(
        kernel,
        [jax.ShapeDtypeStruct(query.shape, BF16), jax.ShapeDtypeStruct((heads, 1, length), F32)],
        [smem(), spec, spec, spec],
        [spec, pl.BlockSpec((each, 1, length), lambda h: (h, 0, 0))],
        [pltpu.VMEM((count, rows, 2 * rows), F32)],
        4 * heads * length * length * HDIM * 4,
        16 * heads * length * HDIM,
        "attend",
        limit=56,
        grid=(heads // each,),
    )(starts, query, key, value)


def attend_back(
    starts, place, query, key, value, mixed, logs, near, far, cosine, sine, narrow, b_heads, rows, first, heads
):
    length = query.shape[1]
    thin = narrow.shape[0]
    rank = thin // 3
    count = length // rows
    scale = 1.0 / math.sqrt(HDIM)
    factor = LOG2E * scale

    def kernel(
        starts_ref, place_ref, q_ref, k_ref, v_ref, o_ref, log_ref, near_ref, far_ref, cos_ref, sin_ref,
        narrow_ref, b_ref, dq_ref, dk_ref, dv_ref, thin_ref, out_ref,
        bias, key_sum, value_sum, key_turned, query_sum,
    ):
        fill_bias(bias, starts_ref, rows)
        ones = jnp.ones((8, HDIM), BF16)
        for head in range(heads):
            key_turned[head] = k_ref[head].astype(F32).T.astype(BF16)

        def pair(head, query, keys, mask, new, many=1):
            q, g, logs, inner = query
            here = slice(keys * rows, (keys + many) * rows)
            raw = dot_t(k_ref[head, here, :], q)
            if many > 1:
                edge = (many - 1) * rows
                raw = jnp.concatenate([raw[:edge], raw[edge:] + mask], axis=0)
            else:
                raw = raw + mask
            probs = jnp.exp2(raw * factor - logs)
            grad_probs = dot_t(v_ref[head, here, :], g)
            grad_scores = (probs * (grad_probs - inner)).astype(BF16)
            value_term = dot(probs.astype(BF16), g)
            key_term = dot(grad_scores, q)
            if new:
                value_sum[head, here, :] = value_term
                key_sum[head, here, :] = key_term
            else:
                value_sum[head, here, :] += value_term
                key_sum[head, here, :] += key_term
            return dot(key_turned[head, :, here], grad_scores)

        for block in reversed(range(count)):
            here = slice(block * rows, (block + 1) * rows)
            relative = place_ref[0] ^ block
            at = pl.multiple_of((relative % 2) * rows, rows)
            queries = []
            for head in range(heads):
                g = jnp.where(
                    relative < 2, near_ref[head, pl.ds(at, rows), :], far_ref[head, pl.ds(at, rows), :]
                )
                product = g.astype(F32) * o_ref[head, here, :].astype(F32)
                high = product.astype(BF16)
                low = (product - high.astype(F32)).astype(BF16)
                inner = (dot_t(ones, high) + dot_t(ones, low))[:1]
                queries.append((q_ref[head, here, :], g, log_ref[head, :, here], inner))
            last = block == count - 1
            totals = [
                pair(head, queries[head], 0, bias[block, :rows, :], last, block + 1) for head in range(heads)
            ]
            if not last:
                for head in range(heads):
                    query_sum[head] = totals[head]

                @pl.when(crosses(starts_ref, (block + 1) * rows))
                def _():
                    for head in range(heads):
                        query_sum[head] += pair(head, queries[head], block + 1, bias[block, rows:, :], False)

                totals = [query_sum[head] for head in range(heads)]
            for head in range(heads):
                dq_ref[head, here, :] = turn(
                    totals[head].T * scale, cos_ref[here, :], -sin_ref[here, :]
                ).astype(BF16)
        thins = [None] * 3
        sums = [[], [], []]
        for head in range(heads):
            dk_ref[head] = turn(key_sum[head] * scale, cos_ref[...], -sin_ref[...]).astype(BF16)
            dv_ref[head] = value_sum[head].astype(BF16)
            for number, ref in enumerate((dq_ref, dk_ref, dv_ref)):
                here = slice(number * rank, (number + 1) * rank)
                term = dot_t(b_ref[head, here, :], ref[head])
                thins[number] = term if head == 0 else thins[number] + term
                sums[number].append(dot(narrow_ref[here, :], ref[head]))
        for number in range(3):
            here = slice(number * rank, (number + 1) * rank)
            thin_ref[here, :] = thins[number]
            out_ref[here, :] = jnp.concatenate(sums[number], axis=1)

    step = first // heads
    spec = pl.BlockSpec((heads, length, HDIM), lambda h: (step, 0, 0))
    half = pl.BlockSpec((heads, length // 2, HDIM), lambda h: (step, 0, 0))
    out = pl.BlockSpec((heads, length, HDIM), lambda h: (0, 0, 0))
    table = pl.BlockSpec((length, HDIM), lambda h: (0, 0))
    thin_spec = pl.BlockSpec((thin, length), lambda h: (0, 0))
    return call(
        kernel,
        [jax.ShapeDtypeStruct((heads, length, HDIM), BF16)] * 3
        + [
            jax.ShapeDtypeStruct((thin, length), F32),
            jax.ShapeDtypeStruct((thin, heads * HDIM), F32),
        ],
        [smem(), smem(), spec, spec, spec, spec]
        + [pl.BlockSpec((heads, 1, length), lambda h: (step, 0, 0)), half, half, table, table, thin_spec]
        + [pl.BlockSpec((heads, thin, HDIM), lambda h: (step, 0, 0))],
        [out] * 3 + [thin_spec, pl.BlockSpec((thin, heads * HDIM), lambda h: (0, 0))],
        [
            pltpu.VMEM((count, 2 * rows, rows), F32),
            pltpu.VMEM((heads, length, HDIM), F32),
            pltpu.VMEM((heads, length, HDIM), F32),
            pltpu.VMEM((heads, HDIM, length), BF16),
            pltpu.VMEM((heads, HDIM, rows), F32),
        ],
        10 * heads * length * length * HDIM * 4,
        32 * heads * length * HDIM,
        "attend_back",
        limit=32,
        grid=(1,),
    )(
        starts, place[None], query, key, value, mixed, logs, near, far, cosine, sine, narrow, b_heads
    )


def rows_by_heads(refs, start, rows):
    return jnp.concatenate(
        [ref[head, pl.ds(start, rows), :] for ref in refs for head in range(ref.shape[0])], axis=1
    )


def close_attention(mixed, place, weight, a_out, wanted, rows):
    size, width = weight.shape
    rank = a_out.shape[0]

    def kernel(place_ref, m_ref, w_ref, a_ref, *outs):
        for block, out in zip(wanted, outs):
            start = pl.multiple_of((place_ref[0] ^ block) * rows, rows)
            here = rows_by_heads([m_ref], start, rows)
            out[:, :width] = dot(here, w_ref[...]).astype(BF16)
            narrow = dot_t(here, a_ref[...]).astype(BF16)
            out[:, width:] = jnp.concatenate(
                [narrow, jnp.zeros((rows, EXTRA - rank), BF16)], axis=1
            )

    return call(
        kernel,
        [jax.ShapeDtypeStruct((rows, width + EXTRA), BF16)] * len(wanted),
        [smem()] + [vmem()] * 3,
        [vmem()] * len(wanted),
        [],
        2 * rows * len(wanted) * size * width,
        2 * size * width + 2 * rows * len(wanted) * (width + size),
        "close_attention",
        limit=28,
    )(place[None], mixed, weight, a_out)


def open_attention(blocks, seconds, wanted, place, mixed, weight, a_out, b_out):
    rows, width_ext = blocks[0].shape
    size, width = weight.shape
    rank = a_out.shape[0]
    count = len(blocks)
    heads = size // HDIM

    def kernel(place_ref, *refs):
        g_refs, refs = refs[:count], refs[count:]
        s_refs, refs = refs[:count], refs[count:]
        m_ref, w_ref, a_ref, b_ref, out, sum_ref, wide_ref = refs
        total, branch, second = None, None, None
        for block in range(count):
            start = pl.multiple_of((place_ref[0] ^ wanted[block]) * rows, rows)
            grad = g_refs[block][:, :width]
            thin = g_refs[block][:, width:]
            narrow = dot_t(grad, b_ref[...]).astype(BF16)
            back = dot_t(grad, w_ref[...]) + dot(narrow, a_ref[...])
            for head in range(heads):
                part = back[:, head * HDIM : (head + 1) * HDIM]
                out[head, block * rows : (block + 1) * rows, :] = part.astype(BF16)
            terms = (
                t_dot(narrow, rows_by_heads([m_ref], start, rows)),
                t_dot(thin, grad)[:rank],
                t_dot(thin, s_refs[block][...])[rank : 3 * rank],
            )
            if block == 0:
                total, branch, second = terms
            else:
                total, branch, second = total + terms[0], branch + terms[1], second + terms[2]
        sum_ref[...] = total
        wide_ref[:rank, :] = branch
        wide_ref[rank:, :] = second

    return call(
        kernel,
        [
            jax.ShapeDtypeStruct((heads, rows * count, HDIM), BF16),
            jax.ShapeDtypeStruct((rank, size), F32),
            jax.ShapeDtypeStruct((3 * rank, width), F32),
        ],
        [smem()] + [vmem()] * (2 * count + 4),
        [vmem()] * 3,
        [],
        2 * rows * count * size * width,
        2 * size * width + 2 * rows * count * (2 * width + 2 * size),
        "open_attention",
        limit=32,
    )(place[None], *blocks, *seconds, mixed, weight, a_out, b_out)


def feed_forward(blocks, grads, offsets, pieces, down, a_mlp, b_down, a_hidden, b_hidden):
    rows, width = blocks[0].shape
    count = len(blocks)
    size = down.shape[0]
    rank = b_down.shape[0]
    n = len(pieces)

    def kernel(offsets_ref, *refs):
        x_refs, refs = refs[:count], refs[count:]
        g_refs, refs = refs[:count], refs[count:]
        piece_refs, refs = refs[:n], refs[n:]
        down_hbm, am_ref, bd_ref, ah_ref, bh_ref = refs[:5]
        refs = refs[5:]
        feed_refs, refs = refs[:count], refs[count:]
        back_refs, refs = refs[:count], refs[count:]
        sum_ref, whole, down_ref, grad_ref, sems, down_sem = refs
        down_copy = pltpu.make_async_copy(down_hbm, down_ref, down_sem)
        down_copy.start()
        copies = load_pieces(offsets_ref, piece_refs, whole, sems)
        x = jnp.concatenate([ref[...] for ref in x_refs], axis=0)
        grad = jnp.concatenate([ref[...] for ref in g_refs], axis=0)
        narrow = dot_t(x, am_ref[...]).astype(BF16)
        thin = dot_t(grad, bd_ref[...]).astype(BF16)
        down_copy.wait()
        grad_ref[...] = (dot_t(grad, down_ref[...]) + dot(thin, ah_ref[...])).astype(BF16)
        for copy in copies:
            copy.wait()
        gate = dot(x, whole[0]) + dot(narrow[:, :rank], bh_ref[0])
        up = dot(x, whole[1]) + dot(narrow[:, rank:], bh_ref[1])
        sigmoid = 0.5 + 0.5 * jnp.tanh(0.5 * gate)
        silu = gate * sigmoid
        hidden = (silu * up).astype(BF16)
        grad_hidden = grad_ref[...].astype(F32)
        grad_up = (grad_hidden * silu).astype(BF16)
        grad_gate = (grad_hidden * up * (sigmoid + silu * (1.0 - sigmoid))).astype(BF16)
        feed = dot(hidden, down_ref[...]).astype(BF16)
        feed_thin = dot_t(hidden, ah_ref[...]).astype(BF16)
        back = (dot_t(grad_gate, whole[0]) + dot_t(grad_up, whole[1])).astype(BF16)
        back_thin = jnp.concatenate(
            [dot_t(grad_gate, bh_ref[0]).astype(BF16), dot_t(grad_up, bh_ref[1]).astype(BF16)], axis=1
        )
        for block in range(count):
            here = slice(block * rows, (block + 1) * rows)
            feed_refs[block][:, :width] = feed[here]
            feed_refs[block][:, width:] = jnp.concatenate(
                [feed_thin[here], jnp.zeros((rows, EXTRA - rank), BF16)], axis=1
            )
            back_refs[block][:, :width] = back[here]
            back_refs[block][:, width:] = jnp.concatenate(
                [back_thin[here], jnp.zeros((rows, EXTRA - 2 * rank), BF16)], axis=1
            )
        sum_ref[:rank, :] = t_dot(thin, hidden)
        sum_ref[rank : 2 * rank, :] = t_dot(narrow[:, :rank], grad_gate)
        sum_ref[2 * rank :, :] = t_dot(narrow[:, rank:], grad_up)

    out = jax.ShapeDtypeStruct((rows, width + EXTRA), BF16)
    return call(
        kernel,
        [out] * (2 * count)
        + [jax.ShapeDtypeStruct((3 * rank, size), F32)],
        [smem()] + [vmem()] * (2 * count) + [anywhere()] * (n + 1) + [vmem()] * 4,
        [vmem()] * (2 * count + 1),
        [
            pltpu.VMEM((2, width, size), BF16),
            pltpu.VMEM((size, width), BF16),
            pltpu.VMEM((count * rows, size), BF16),
            pltpu.SemaphoreType.DMA((n,)),
            pltpu.SemaphoreType.DMA,
        ],
        12 * rows * count * width * size,
        6 * width * size + 8 * rows * count * width,
        "feed_forward",
    )(offsets, *blocks, *grads, *pieces, down, a_mlp, b_down, a_hidden, b_hidden)


def project_back(grads, place, offsets, pieces, wanted, rows):
    size = pieces[0].shape[1]
    width = 4 * pieces[0].shape[0]
    n = len(pieces)
    count = len(wanted)

    def kernel(place_ref, offsets_ref, *refs):
        g_refs, refs = refs[: len(grads)], refs[len(grads) :]
        piece_refs, refs = refs[:n], refs[n:]
        back_refs, (whole, sems) = refs[:count], refs[count:]
        copies = load_pieces(offsets_ref, piece_refs, whole, sems)
        starts = [pl.multiple_of((place_ref[0] ^ block) * rows, rows) for block in wanted]
        parts = [rows_by_heads(g_refs, start, rows) for start in starts]
        for copy in copies:
            copy.wait()
        for part, back in zip(parts, back_refs):
            back[...] = dot_t(part, whole[...]).astype(BF16)

    return call(
        kernel,
        [jax.ShapeDtypeStruct((rows, width), BF16)] * count,
        [smem(), smem()] + [vmem()] * len(grads) + [anywhere()] * n,
        [vmem()] * count,
        [pltpu.VMEM((width, size), BF16), pltpu.SemaphoreType.DMA((n,))],
        2 * rows * count * width * size,
        2 * (rows * count * (width + size) + width * size),
        "project_back",
        limit=56,
    )(place[None], offsets, *grads, *pieces)


def thin_product(thin, place, blocks):
    rows, width = blocks[0].shape
    count = len(blocks)

    def kernel(place_ref, thin_ref, *refs):
        total = None
        for block in range(count):
            start = pl.multiple_of((place_ref[0] ^ block) * rows, rows)
            term = dot(thin_ref[:, pl.ds(start, rows)], refs[block][...])
            total = term if total is None else total + term
        refs[count][...] = total

    return call(
        kernel,
        jax.ShapeDtypeStruct((thin.shape[0], width), F32),
        [smem()] + [vmem()] * (count + 1),
        vmem(),
        [],
        2 * 128 * rows * count * width,
        2 * rows * count * width,
        "thin_product",
        limit=24,
    )(place[None], thin, *blocks)


def shards(
    tokens,
    cotangent,
    sequence_adapter_index,
    image_span_start,
    attention_norm_gain,
    feedforward_norm_gain,
    query_key_value_weight,
    attention_output_weight,
    gate_up_projection_weight,
    down_projection_weight,
    adapter_model_input_maps,
    adapter_model_output_maps,
    adapter_hidden_input_map,
    adapter_hidden_output_maps,
):
    rows = tokens.shape[1]
    width = tokens.shape[2]
    rank = adapter_model_input_maps.shape[2]
    group = lax.axis_size("shard")
    place = lax.axis_index("shard").astype(jnp.int32)
    rep_place = lax.axis_index("rep").astype(jnp.int32)
    pick = sequence_adapter_index[0]
    starts = image_span_start[0]
    head_cols = width // group
    ff_cols = down_projection_weight.shape[0]
    k_rows = query_key_value_weight.shape[1]

    gain_one = attention_norm_gain.astype(F32)
    gain_two = feedforward_norm_gain.astype(F32)
    residual_in = tokens[0].astype(F32)
    grad_out = cotangent[0].astype(F32)

    def own_columns(values, size):
        return lax.dynamic_slice_in_dim(values, place * size, size, values.ndim - 1)

    quarter = k_rows // 4
    quarter_one, quarter_two = sides(
        query_key_value_weight, rep_place % 4 * quarter, quarter, place, head_cols, (2, 3), "sides_far"
    )
    first_a = hop(quarter_one, "shard", 2)
    normed = norm_rows(residual_in, gain_one).astype(BF16)
    front_chip, front_part = chip_picked(
        jnp.concatenate([adapter_model_input_maps[0:3], adapter_model_output_maps[0:3]]), pick, place
    )
    first_a, front_part, quarter_two, normed, qkv = fence(
        first_a, front_part, quarter_two, normed, query_key_value_weight
    )
    first_b = hop(quarter_two, "shard", 3)
    first_a_two, first_a_three = hop(first_a, "rep", 2), hop(first_a, "rep", 1)
    first_own, near_out = sides(qkv, 0, k_rows, place, head_cols, (0, 1), "sides_near")
    normed_near = core(normed)
    first_b, front_part, near_out, rest_bank, wide_bank = fence(
        first_b, front_part, near_out,
        (adapter_model_input_maps[3:6], adapter_model_output_maps[3:5]),
        (adapter_hidden_input_map[None], adapter_hidden_output_maps),
    )
    front_far = across(front_part)
    first_b_two, first_b_three = hop(first_b, "rep", 1), hop(first_b, "rep", 2)
    front_far, normed, first_a_two, first_a_three = fence(front_far, normed, first_a_two, first_a_three)
    normed_far = across(normed)
    first_a_four = hop(first_a_two, "rep", 1)
    first_near = core(near_out)
    rest_chip, rest_part = chip_picked(jnp.concatenate(rest_bank), pick, place)
    wide_chip, wide_part = chip_picked(jnp.concatenate(wide_bank), pick, place)
    first_b_two, first_b_three, gate_up, grad_out, front_chip = fence(
        first_b_two, first_b_three, gate_up_projection_weight, grad_out, front_chip
    )
    first_b_four = hop(first_b_two, "rep", 2)
    mlp_leaving = [side(gate_up, rep_place % 4 * quarter, quarter, place ^ j, ff_cols) for j in (2, 3)]
    grad_feed = (BRANCH * grad_out).astype(BF16)
    half = HDIM // 2
    frequency = jnp.exp(jnp.arange(half, dtype=F32) * (-2.0 / HDIM) * math.log(THETA))
    angle = jnp.arange(rows * group, dtype=jnp.int32).astype(F32)[:, None] * frequency[None, :]
    cosine = jnp.concatenate([jnp.cos(angle), jnp.cos(angle)], axis=1)
    sine = jnp.concatenate([jnp.sin(angle), jnp.sin(angle)], axis=1)
    cosine_pair = jnp.concatenate([jnp.cos(angle)] * 4, axis=1)
    sine_pair = jnp.concatenate([-jnp.sin(angle), jnp.sin(angle)] * 2, axis=1)
    tables = (cosine, sine, cosine_pair, sine_pair)
    front = whole_picked(front_chip, front_far, place)
    a_first = front[:3].reshape(3 * rank, width)
    b_first = own_columns(front[3:], head_cols)
    b_wide = jnp.concatenate(
        [jnp.pad(b_first[i], ((0, 0), (i * head_cols, (2 - i) * head_cols))) for i in range(3)]
    )
    (
        normed_far, first_a_four, first_b_four, mlp_leaving, grad_feed, b_wide, a_first, rest_part, wide_part,
        tables,
    ) = fence(
        normed_far, first_a_four, first_b_four, mlp_leaving, grad_feed, b_wide, a_first, rest_part, wide_part,
        tables,
    )
    cosine, sine, cosine_pair, sine_pair = tables
    first_blocks = (normed, normed_near, normed_far, core(normed_far))
    first_offsets, first_pieces = arrange(
        k_rows, first_own, first_near,
        (
            (first_a, first_a_two, first_a_three, first_a_four),
            (first_b, first_b_two, first_b_three, first_b_four),
        ),
        place, rep_place,
    )

    mlp_a, mlp_b = hop(mlp_leaving[0], "shard", 2), hop(mlp_leaving[1], "shard", 3)
    query, key, value, narrow_first = project(
        first_blocks, place, first_offsets, first_pieces, a_first, b_wide, cosine_pair, sine_pair
    )
    query, mlp_a, rest_part, wide_part = fence(query, mlp_a, rest_part, wide_part)
    mlp_a_two, mlp_a_three = hop(mlp_a, "rep", 2), hop(mlp_a, "rep", 1)
    rest_far, wide_far = across(rest_part), across(wide_part)
    mixed, logs = attend(starts, query, key, value, rows)
    mixed, mlp_b, mlp_a_two, mlp_a_three, rest_far = fence(
        mixed, mlp_b, mlp_a_two, mlp_a_three, rest_far
    )
    mlp_b_two, mlp_b_three = hop(mlp_b, "rep", 1), hop(mlp_b, "rep", 2)
    rest = whole_picked(rest_chip, rest_far, place)
    a_out = own_columns(rest[0], head_cols)
    a_mlp = rest[1:3].reshape(2 * rank, width)
    b_out, b_down = rest[3], rest[4]
    far_out = close_attention(mixed, place, attention_output_weight, a_out, (2, 3), rows)
    far_sum = (far_out[0].astype(F32) + core(far_out[1]).astype(F32)).astype(BF16)
    far_sum, mixed_here, grad_feed, wide_far = fence(far_sum, mixed, grad_feed, wide_far)
    branch_low, far_rest = across(far_sum[: rows // 2]), far_sum[rows // 2 :]
    feed_near_in = core(grad_feed)
    near_out = close_attention(mixed_here, place, attention_output_weight, a_out, (0, 1), rows)
    near_out, gate_up = fence(near_out, gate_up)
    mlp_near_out = side(gate_up, 0, k_rows, place ^ 1, ff_cols)
    mlp_own = side(gate_up, 0, k_rows, place, ff_cols)
    near_out, mlp_b_two, mlp_b_three, branch_low, far_rest, mlp_near_out, mlp_own = fence(
        near_out, mlp_b_two, mlp_b_three, branch_low, far_rest, mlp_near_out, mlp_own
    )
    mlp_a_four, mlp_b_four = hop(mlp_a_two, "rep", 1), hop(mlp_b_two, "rep", 2)
    branch_high = across(far_rest)
    near_here = core(near_out[1])
    mlp_near = core(mlp_near_out)
    hidden_cols = own_columns(whole_picked(wide_chip, wide_far, place), ff_cols)
    near_here, branch_high, hidden_cols, mlp_own = fence(near_here, branch_high, hidden_cols, mlp_own)
    branch_far = jnp.concatenate([branch_low, branch_high])
    feed_low = across(after(grad_feed[: rows // 2], branch_high))
    feed_rest = after(grad_feed[rows // 2 :], branch_high)
    a_hidden, b_hidden = hidden_cols[0], hidden_cols[1:]
    branch_own = near_out[0].astype(F32) + near_here.astype(F32) + branch_far.astype(F32)
    narrow_out = branch_own[:, width : width + rank].astype(BF16)
    branch = branch_own[:, :width] + dot(narrow_out, b_out)
    middle = residual_in + BRANCH * branch
    normed_second = norm_rows(middle, gain_two).astype(BF16)
    second_far = across(normed_second)
    second_near = core(normed_second)
    second_near, feed_near_in, mlp_near, mlp_a_four, mlp_b_four, feed_low = fence(
        second_near, feed_near_in, mlp_near, mlp_a_four, mlp_b_four, feed_low
    )
    feed_high = across(feed_rest)
    mlp_offsets, mlp_pieces = arrange(
        k_rows, mlp_own, mlp_near,
        (
            (mlp_a, mlp_a_two, mlp_a_three, mlp_a_four),
            (mlp_b, mlp_b_two, mlp_b_three, mlp_b_four),
        ),
        place, rep_place,
    )
    *parts, sum_near = feed_forward(
        (normed_second, second_near), (grad_feed, feed_near_in), mlp_offsets, mlp_pieces,
        down_projection_weight, a_mlp, b_down, a_hidden, b_hidden,
    )
    feed_near, back_near = parts[:2], parts[2:]
    second_far, feed_high, back_near, feed_near = fence(second_far, feed_high, back_near, feed_near)
    feed_far_in = jnp.concatenate([feed_low, feed_high])
    second_blocks = (normed_second, second_near, second_far, core(second_far))
    feed_blocks = (grad_feed, feed_near_in, feed_far_in, core(feed_far_in))
    *parts, sum_far = feed_forward(
        second_blocks[2:], feed_blocks[2:], mlp_offsets, mlp_pieces, down_projection_weight,
        a_mlp, b_down, a_hidden, b_hidden,
    )
    feed_far, back_far = parts[:2], parts[2:]
    back_sum = (back_far[0].astype(F32) + core(back_far[1]).astype(F32)).astype(BF16)
    back_sum, back_near, feed_near, feed_far, sum_near = fence(
        back_sum, back_near, feed_near, feed_far, sum_near
    )
    back_low, back_rest = across(back_sum[: rows // 2]), back_sum[rows // 2 :]

    bits = reps_bits()
    back_here = core(back_near[1])
    feed_here = core(feed_near[1])
    feed_mate = core(feed_far[1])
    mark = jnp.full((rank, ff_cols), pick.astype(F32))
    wide_all = jnp.concatenate([sum_near + sum_far, mark]).astype(BF16)[None]
    wide_hop = hop(wide_all, "rep", bits[0])
    back_low, feed_here, feed_mate, back_here, back_rest, sum_near = fence(
        back_low, feed_here, feed_mate, back_here, back_rest, sum_near
    )
    back_high = across(back_rest)
    feed_here = feed_near[0].astype(F32) + feed_here.astype(F32)
    feed_sum = (feed_far[0].astype(F32) + feed_mate.astype(F32)).astype(BF16)
    back_high, feed_here, feed_sum, back_here, wide_hop = fence(
        back_high, feed_here, feed_sum, back_here, wide_hop
    )
    back_from_far = jnp.concatenate([back_low, back_high])
    second_own = back_near[0].astype(F32) + back_here.astype(F32) + back_from_far.astype(F32)
    grad_narrow_mlp = second_own[:, width : width + 2 * rank].astype(BF16)
    grad_normed_second = second_own[:, :width] + dot(grad_narrow_mlp, a_mlp)
    grad_middle = grad_out + norm_back(middle, gain_two, grad_normed_second)
    grad_branch = (BRANCH * grad_middle).astype(BF16)
    branch_rows = pad_columns([grad_branch, narrow_out, grad_narrow_mlp], width + EXTRA)
    branch_rows, wide_hop = fence(branch_rows, wide_hop)
    branch_far_in = across(branch_rows)
    branch_near_in = core(branch_rows)
    wide_all = both(wide_all, wide_hop, rep_place, bits[0])
    for bit in bits[1:-2]:
        wide_all = both(wide_all, hop(wide_all, "rep", bit), rep_place, bit)
    wide_hop = hop(wide_all, "rep", bits[-2])
    branch_near_in, wide_all = fence(branch_near_in, wide_all)
    mixed_near, grad_a_near, thin_near = open_attention(
        (branch_rows, branch_near_in), second_blocks[:2], (0, 1), place, mixed,
        attention_output_weight, a_out, b_out,
    )
    mixed_near, wide_hop = fence(mixed_near, wide_hop)
    wide_all = both(wide_all, wide_hop, rep_place, bits[-2])
    wide_hop = hop(wide_all, "rep", bits[-1])
    branch_far_in, mixed_near, wide_all = fence(branch_far_in, mixed_near, wide_all)
    feed_from_far = across(after(feed_sum, branch_far_in))
    mixed_far, grad_a_far, thin_far = open_attention(
        (branch_far_in, core(branch_far_in)), second_blocks[2:], (2, 3), place, mixed,
        attention_output_weight, a_out, b_out,
    )

    b_heads = b_first.reshape(3 * rank, head_cols // HDIM, HDIM).transpose(1, 0, 2)

    def attend_part(first, heads, starts):
        return attend_back(
            starts, place, query, key, value, mixed, logs, mixed_near, mixed_far, cosine, sine,
            narrow_first, b_heads, rows, first, heads,
        )

    mixed_far, starts_one, wide_all = fence(mixed_far, starts, wide_all)
    heads = query.shape[0]
    third = heads // 3
    part_one = attend_part(0, third, starts_one)
    part_one, feed_from_far, wide_hop, starts_two = fence(part_one, feed_from_far, wide_hop, starts_one)
    wide_all = both(wide_all, wide_hop, rep_place, bits[-1])
    picks = wide_all[:, -1, :1].astype(F32)
    adapters = adapter_model_input_maps.shape[1] * group
    chosen = (picks == jnp.arange(adapters, dtype=jnp.int32).astype(F32)[None, :]).astype(F32)
    wide_sent = send_sums(wide_all[:, :-rank], chosen, place, rank)
    feed_own = feed_here + feed_from_far.astype(F32)
    narrow_down = feed_own[:, width : width + rank].astype(BF16)
    down_far = across(narrow_down)
    down_near = core(narrow_down)
    starts_two, narrow_down = fence(starts_two, narrow_down)
    part_two = attend_part(third, third, starts_two)
    part_two, down_far, down_near, starts_three, wide_sent = fence(
        part_two, down_far, down_near, starts_two, wide_sent
    )
    down_thin = (narrow_down, down_near, down_far, core(down_far))
    grad_b_down = sum(t_dot(left, right) for left, right in zip(down_thin, feed_blocks))
    early_all = jnp.concatenate(
        [
            grad_a_near + grad_a_far,
            own_columns(jnp.concatenate([thin_near + thin_far, grad_b_down]), head_cols),
        ]
    ).astype(BF16)[None]
    early_hop = hop(early_all, "rep", bits[0])
    early_all, starts_three = fence(early_all, starts_three)
    part_three = attend_part(2 * third, heads - 2 * third, starts_three)
    part_three, early_hop = fence(part_three, early_hop)
    parts = (part_one, part_two, part_three)
    first_grads = [part[number] for number in range(3) for part in parts]
    thin = (part_one[3] + part_two[3] + part_three[3]).astype(BF16)
    thin_hop = core(thin)
    early_all = both(early_all, early_hop, rep_place, bits[0])
    for bit in bits[1:-2]:
        early_all = both(early_all, hop(early_all, "rep", bit), rep_place, bit)
    grad_b_first = jnp.concatenate([part[4] for part in parts], axis=1)
    thin = (thin.astype(F32) + thin_hop.astype(F32)).astype(BF16)
    thin, early_all, grad_b_first = fence(thin, early_all, grad_b_first)
    thin_hop = across(thin)
    early_hop = hop(early_all, "rep", bits[-2])
    grad_narrow = (thin.astype(F32) + thin_hop.astype(F32)).astype(BF16)
    late_all = jnp.concatenate(
        [own_columns(thin_product(grad_narrow, place, first_blocks), head_cols), grad_b_first]
    ).astype(BF16)[None]
    late_all, first_grads = fence(late_all, first_grads)
    late_hop = hop(late_all, "rep", bits[0])
    back_rows_far = project_back(first_grads, place, first_offsets, first_pieces, (2, 3), rows)
    back_rows_far, late_hop, early_hop = fence(back_rows_far, late_hop, early_hop)
    back_mate = core(back_rows_far[1])
    late_all = both(late_all, late_hop, rep_place, bits[0])
    for bit in bits[1:-2]:
        late_all = both(late_all, hop(late_all, "rep", bit), rep_place, bit)
    late_hop = hop(late_all, "rep", bits[-2])
    early_all = both(early_all, early_hop, rep_place, bits[-2])
    early_hop = hop(early_all, "rep", bits[-1])
    back_sum = (back_rows_far[0].astype(F32) + back_mate.astype(F32)).astype(BF16)
    back_sum, first_grads, early_all, late_all = fence(back_sum, first_grads, early_all, late_all)
    back_low, back_high = across(back_sum[: rows // 2]), across(back_sum[rows // 2 :])
    back_rows_near = project_back(first_grads, place, first_offsets, first_pieces, (0, 1), rows)
    back_rows_near, late_hop, early_hop, back_low = fence(back_rows_near, late_hop, early_hop, back_low)
    back_rows_here = core(back_rows_near[1])
    late_all = both(late_all, late_hop, rep_place, bits[-2])
    late_all, early_hop, early_all = fence(late_all, early_hop, early_all)
    late_hop = hop(late_all, "rep", bits[-1])
    early_sent = send_sums(both(early_all, early_hop, rep_place, bits[-1]), chosen, place, rank)

    def whole_maps(stacked, low, high):
        part = stacked[:, low // rank : high // rank]
        pieces = [lax.dynamic_index_in_dim(part, place ^ i, 0, keepdims=False) for i in range(group)]
        return jnp.concatenate(pieces, axis=-1).astype(F32)

    feed = feed_here[:, :width] + feed_from_far[:, :width].astype(F32) + dot(narrow_down, b_down)
    output = (middle + BRANCH * feed).astype(BF16)
    hidden_maps = whole_maps(jnp.stack(wide_sent), 0, 3 * rank)
    late_hop, hidden_maps, output, back_high, back_rows_here = fence(
        late_hop, hidden_maps, output, back_high, back_rows_here
    )
    back_far_in = jnp.concatenate([back_low, back_high])
    late_sent = send_sums(both(late_all, late_hop, rep_place, bits[-1]), chosen, place, rank)
    narrow_own = lax.dynamic_slice_in_dim(grad_narrow, place * rows, rows, 1)
    grad_normed = (
        back_rows_near[0].astype(F32) + back_rows_here.astype(F32) + back_far_in.astype(F32)
        + t_dot(narrow_own, a_first)
    )
    input_grad = grad_middle + norm_back(residual_in, gain_one, grad_normed)
    late_sent, input_grad, early_sent = fence(late_sent, input_grad, early_sent)
    early_got = jnp.stack(early_sent)
    late_got = jnp.stack(late_sent)
    grad_a_model = jnp.concatenate(
        [
            whole_maps(late_got, 0, 3 * rank),
            whole_maps(early_got, 0, rank),
            whole_maps(early_got, 2 * rank, 4 * rank),
        ]
    )
    grad_b_model = jnp.concatenate(
        [
            whole_maps(late_got, 3 * rank, 6 * rank),
            whole_maps(early_got, rank, 2 * rank),
            whole_maps(early_got, 4 * rank, 5 * rank),
        ]
    )
    return (
        output[None], input_grad[None], grad_a_model, grad_b_model, hidden_maps[0], hidden_maps[1:3],
    )


def solution(mesh):
    in_specs = (
        P("rep", "shard", None),
        P("rep", "shard", None),
        P("rep"),
        P("rep", None),
        P(),
        P(),
        P(None, "shard", None),
        P("shard", None),
        P(None, "shard", None),
        P("shard", None),
        P(None, "shard", None, None),
        P(None, "shard", None, None),
        P("shard", None, None),
        P(None, "shard", None, None),
    )
    out_specs = (
        P("rep", "shard", None),
        P("rep", "shard", None),
        P(None, "shard", None, None),
        P(None, "shard", None, None),
        P("shard", None, None),
        P(None, "shard", None, None),
    )
    return jax.shard_map(shards, mesh=mesh, in_specs=in_specs, out_specs=out_specs, check_vma=False)
```
